32 devices in a mesh: samp: 4 (over z), pix: 8 (over y, x, core).
Axes of the slice: x: 2, y: 2, z: 4, core: 2. Of those that a mesh axis runs over, the one named last changes fastest.
Arguments:
- stamps: bfloat16 [2048, 16384], P(('samp', 'pix')), may hold values from -6 to 6
- start_panel: float32 [16384, 32], P('pix'), may hold values from -0.046875 to 0.046875
Outputs:
- eigen_psfs: float32 [16384, 32], P('pix')
The draws below stay inside these ranges and needn't reach their ends.
All inputs are finite; a program needn't handle non-finite values.
Results may differ from the reference program's by a relative error of at most 0.025.
Values may be sent and summed in bfloat16 or wider, within the bound.
No kernel may reach another device: no remote copies, remote signals or barrier semaphores. Data moves between devices by JAX's collectives and lax.ppermute only.
A program may use at most 64 MiB of HBM per device.

```python
import math
import jax
import jax.numpy as jnp
from jax import lax

PIX = 16384
K = 32
ITERS = 10
SAMPLES = 2048


def draw_stamps(key, part):
    first = jax.random.fold_in(jax.random.fold_in(key, 7), 0)
    values = jax.random.normal(first, (SAMPLES, PIX), jnp.float32)
    return jnp.clip(values, -6.0, 6.0).astype(jnp.bfloat16)


def block_levels(rng, shape, cuts, least, top_value):
    def one(axis_at, parts):
        draws = jax.random.uniform(jax.random.fold_in(jax.random.fold_in(rng, 6), axis_at), (parts,), jnp.float32, least / len(cuts), top_value / len(cuts))
        return jnp.repeat(jnp.exp(draws), shape[axis_at] // parts).reshape((-1,) + (1,) * (len(shape) - axis_at - 1))

    loudness = one(*cuts[0])
    for cut in cuts[1:]:
        loudness = loudness * one(*cut)
    return loudness


def bell_draw(key, shape, deviation, most, shards=(), dtype=jnp.bfloat16):
    drawn = deviation * jax.random.normal(key, shape, jnp.float32)
    if shards:
        drawn = drawn * block_levels(key, shape, shards, -0.22, 0.18)
    return jnp.clip(drawn, -most, most).astype(dtype)


def setup_inputs(seed: int = 0) -> dict:
    arg_keys = jax.random.split(jax.random.key(seed), 3)
    return {
        "stamps": draw_stamps(jax.random.fold_in(arg_keys[2], 71), 0),
        "start_panel": bell_draw(arg_keys[1], (PIX, K), PIX ** -0.5, 0.046875, ((0, 8),), jnp.float32),
    }


def reference(stamps, start_panel):
    panel = start_panel
    for step in range(ITERS):
        proj = jnp.dot(stamps.astype(jnp.float32), panel.astype(jnp.bfloat16).astype(jnp.float32), preferred_element_type=jnp.float32).astype(jnp.bfloat16)
        back = lax.dot_general(stamps.astype(jnp.float32), proj.astype(jnp.float32), (((0,), (0,)), ((), ())), preferred_element_type=jnp.float32)
        gram = jnp.dot(back.T, back, precision=lax.Precision.HIGHEST)
        lower = jnp.linalg.cholesky(gram)
        panel = lax.linalg.triangular_solve(lower, back, left_side=False, lower=True, transpose_a=True)
    return panel * math.sqrt(PIX)
```

```python
import functools
import math

import jax
import jax.numpy as jnp
from jax import lax
from jax.experimental import pallas as pl
from jax.experimental.pallas import tpu as pltpu
from jax.sharding import PartitionSpec as P

ITERS = 10
LANES = 128
SAMPLE_SPACE_LIMIT = 4096
INTERPRET = False
F32 = jnp.float32
BF16 = jnp.bfloat16

NN = (((1,), (0,)), ((), ()))
NT = (((1,), (1,)), ((), ()))
TN = (((0,), (0,)), ((), ()))


def orthonormal(back, gram):
    lower = jnp.linalg.cholesky(gram)
    return lax.linalg.triangular_solve(lower, back, left_side=False, lower=True, transpose_a=True)


def pixel_space(stamps, start_panel):
    block = lax.all_to_all(stamps, "pix", split_axis=1, concat_axis=0, tiled=True)

    def sweep(step, panel):
        partial_value = jnp.dot(block, panel.astype(BF16), preferred_element_type=F32)
        proj = lax.psum(partial_value.astype(BF16), "pix")
        back = lax.dot_general(block, proj, TN, preferred_element_type=F32)
        summed = lax.psum(back.astype(BF16), "samp").astype(F32)
        gram = lax.psum(jnp.dot(summed.T, summed, precision=lax.Precision.HIGHEST), "pix")
        return orthonormal(summed, gram)

    panel = lax.fori_loop(0, ITERS, sweep, start_panel)
    return panel * math.sqrt(start_panel.shape[0] * lax.axis_size("pix"))


def dot(a, b, dims):
    return lax.dot_general(a, b, dims, preferred_element_type=F32)


def split3(x):
    hi = x.astype(BF16)
    rest = x - hi.astype(F32)
    mid = rest.astype(BF16)
    lo = (rest - mid.astype(F32)).astype(BF16)
    return hi, mid, lo


def kernel_call(body, out_shape, **kw):
    return pl.pallas_call(body, out_shape=out_shape, interpret=INTERPRET, **kw)


def vmem(n=1):
    return [pl.BlockSpec(memory_space=pltpu.VMEM)] * n


def smem():
    return pl.BlockSpec(memory_space=pltpu.SMEM)


def inverse_lower(gram):
    k = gram.shape[0]
    lane = lax.broadcasted_iota(jnp.int32, gram.shape, 1)
    row = lax.broadcasted_iota(jnp.int32, gram.shape, 0)
    m = jnp.where(lane < k, gram, jnp.where(lane == row + k, 1.0, 0.0))
    for j in range(k):
        col = jnp.broadcast_to(m[:, j : j + 1], m.shape)
        scale = lax.rsqrt(jnp.broadcast_to(col[j : j + 1, :], m.shape))
        pivot = jnp.broadcast_to(m[j : j + 1, :], m.shape) * scale
        m = jnp.where(row > j, m - (col * scale) * pivot, jnp.where(row == j, pivot, m))
    return pltpu.roll(m, LANES - k, 1)


def lane_sum3(x, k):
    return x + pltpu.roll(x, LANES - k, 1) + pltpu.roll(x, LANES - 2 * k, 1)


def gram_of(left, parts, zeros):
    k = left.shape[0]
    stack = jnp.concatenate(list(parts) + [zeros], axis=0)
    return lane_sum3(dot(left, stack, NT), k)


def apply_lower(inv, parts, zeros):
    k = inv.shape[0]
    lane = lax.broadcasted_iota(jnp.int32, inv.shape, 1)
    inv = jnp.where(lane < k, inv, 0.0)
    inv = inv + pltpu.roll(inv, k, 1)
    inv = inv + pltpu.roll(inv, 2 * k, 1)
    h1, h2, h3 = [h.astype(F32) for h in split3(inv)]
    first = jnp.where(lane < 3 * k, h1, h2)
    second = jnp.where(lane < k, h2, jnp.where(lane < 2 * k, h3, 0.0))
    left = jnp.concatenate([first, second], axis=1).astype(BF16)
    y1, y2, y3 = parts
    right = jnp.concatenate([y1, y2, y3, y1, y2, y1, zeros, zeros], axis=0)
    return dot(left, right, NN)


def basis_kernel(p0_ref, q_ref):
    p0 = p0_ref[...]
    zeros = jnp.zeros_like(p0)
    gram = gram_of(p0, (p0, zeros, zeros), zeros)
    q_ref[...] = apply_lower(inverse_lower(gram), (p0, zeros, zeros), zeros)


def weighted_rows(q, m, w):
    return w - 0.5 * m


def form_kernel(core_ref, own_ref, other_ref, q_ref, out_ref, own_ext, other_ext, left, right):
    n = own_ref.shape[0]
    k = q_ref.shape[0]
    rows, width = out_ref.shape
    width -= LANES
    bs = width - n // 2
    core = core_ref[0]
    q = q_ref[...]
    zeros = jnp.zeros(q.shape, BF16)

    own_ext[:n] = own_ref[...]
    own_ext[n:] = own_ref[: n // 2]
    other_ext[:n] = other_ref[...]
    other_ext[n:] = other_ref[: n // 2]

    q3 = split3(q)
    qs = jnp.concatenate(q3, axis=0)
    w = jnp.zeros(q.shape, F32)
    m = jnp.zeros((k, LANES), F32)
    for ref in (own_ref, other_ref):
        t3 = dot(qs, ref[...], NN)
        t = t3[:k] + t3[k : 2 * k] + t3[2 * k :]
        ts = split3(t)
        w3 = dot(jnp.concatenate(ts, axis=0), ref[...], NT)
        w += w3[:k] + w3[k : 2 * k] + w3[2 * k :]
    ws = split3(w)
    wst = jnp.concatenate(list(ws) + [zeros], axis=0)
    q1, q2, q3_ = q3
    m = lane_sum3(dot(q1, wst, NT) + dot(q2, wst, NT) + dot(q3_, wst, NT), k)
    w = w - 0.5 * apply_lower(m, q3, zeros)
    w1, w2, w3 = split3(w)

    u1 = jnp.concatenate([q1, w1], axis=0)
    u2 = jnp.concatenate([q2, w2], axis=0)
    u3 = jnp.concatenate([q3_, w3], axis=0)
    v1 = jnp.concatenate([w1, q1], axis=0)
    v2 = jnp.concatenate([w2, q2], axis=0)
    v3 = jnp.concatenate([w3, q3_], axis=0)
    left[...] = jnp.concatenate([u1, u1, u1, u2, u2, u3], axis=0)
    vs = jnp.concatenate([v1, v2, v3, v1, v2, v1], axis=0)
    right[:, :n] = vs
    right[:, n:] = vs[:, : n // 2]
    wt = jnp.concatenate([w1, w2, w3, zeros], axis=0).astype(F32)
    del wt

    def step(i, _):
        at = pl.multiple_of(core * rows + i * bs, bs)
        to = pl.multiple_of(i * bs, bs)
        s = dot(own_ext[pl.ds(at, bs), :], own_ext[pl.ds(at, width), :], NT)
        s += dot(other_ext[pl.ds(at, bs), :], other_ext[pl.ds(at, width), :], NT)
        s -= dot(left[:, pl.ds(at, bs)], right[:, pl.ds(at, width)], TN)
        out_ref[pl.ds(to, bs), :width] = s.astype(BF16)
        wb = jnp.concatenate(
            [
                right[:k, pl.ds(at, bs)],
                right[2 * k : 3 * k, pl.ds(at, bs)],
                right[4 * k : 5 * k, pl.ds(at, bs)],
                jnp.zeros((LANES - 3 * k, bs), BF16),
            ],
            axis=0,
        ).astype(F32)
        out_ref[pl.ds(to, bs), width:] = wb.T.astype(BF16)
        return 0

    lax.fori_loop(0, rows // bs, step, 0)


def add_kernel(k, a_ref, b_ref, o_ref):
    width = a_ref.shape[1] - LANES
    o_ref[:, :width] = (a_ref[:, :width].astype(F32) + b_ref[:, :width].astype(F32)).astype(BF16)
    x = lane_sum3(a_ref[:, width:].astype(F32), k) + lane_sum3(b_ref[:, width:].astype(F32), k)
    lane = lax.broadcasted_iota(jnp.int32, x.shape, 1)
    h1, h2, h3 = [h.astype(F32) for h in split3(x)]
    packed = jnp.where(
        lane < k,
        h1,
        jnp.where(
            lane < 2 * k,
            pltpu.roll(h2, k, 1),
            jnp.where(lane < 3 * k, pltpu.roll(h3, 2 * k, 1), 0.0),
        ),
    )
    o_ref[:, width:] = packed.astype(BF16)


def add_shares(a, b, k):
    return kernel_call(
        functools.partial(add_kernel, k),
        jax.ShapeDtypeStruct(a.shape, BF16),
        in_specs=vmem(2),
        out_specs=vmem()[0],
    )(a, b)


def iterate_kernel(index_ref, share_ref, q_ref, p0_ref, p_ref, inv_ref, full, u, v):
    n = share_ref.shape[0]
    k = q_ref.shape[0]
    width = share_ref.shape[1] - LANES
    bs = width - n // 2
    nb = n // bs

    def unpack(r, _):
        i = index_ref[r]
        frm = pl.multiple_of(r * bs, bs)
        to = pl.multiple_of(i * bs, bs)
        for d in range(nb // 2 + 1):
            part = share_ref[pl.ds(frm, bs), d * bs : (d + 1) * bs]
            at = pl.multiple_of(lax.rem(i + d, nb) * bs, bs)
            full[pl.ds(to, bs), pl.ds(at, bs)] = part
            if 0 < d < nb // 2:
                full[pl.ds(at, bs), pl.ds(to, bs)] = part.T
        wb = share_ref[pl.ds(frm, bs), width:].astype(F32).T
        w = wb[:k] + wb[k : 2 * k] + wb[2 * k : 3 * k]
        q = q_ref[:, pl.ds(to, bs)]
        us = split3(jnp.concatenate([w, q], axis=0))
        vs = split3(jnp.concatenate([q, w], axis=0))
        u[:, pl.ds(to, bs)] = jnp.concatenate(list(us) + [jnp.zeros((2 * k, bs), BF16)], axis=0)
        v1, v2, v3 = vs
        v[:, pl.ds(to, bs)] = jnp.concatenate([v1, v2, v3, v1, v2, v1], axis=0)
        return 0

    lax.fori_loop(0, nb, unpack, 0)

    zeros = jnp.zeros((k, n), BF16)
    lane = lax.broadcasted_iota(jnp.int32, (k, LANES), 1)

    def product(p):
        t = dot(p, u[...], NT)
        t = t[:, :LANES] + t[:, LANES:]
        t = t + pltpu.roll(t, 2 * k, 1)
        h1, h2, h3 = [h.astype(F32) for h in split3(t)]
        low = lane < 2 * k
        ts = jnp.concatenate([h1, jnp.where(low, h1, h2), jnp.where(low, h2, h3)], axis=1).astype(BF16)
        y = dot(p, full[...], NN) + dot(ts, v[...], NN)
        return split3(y)

    def sweep(step, p):
        parts = product(p)
        inv = inverse_lower(gram_of(p, parts, zeros))
        return apply_lower(inv, parts, zeros).astype(BF16)

    p = lax.fori_loop(0, ITERS - 1, sweep, p0_ref[...])
    p_ref[...] = p
    inv_ref[...] = inverse_lower(gram_of(p, product(p), zeros))


def finish_kernel(scale, p_ref, inv_ref, block_ref, o_ref):
    k, n = p_ref.shape
    back = dot(p_ref[...], block_ref[...], NN)
    zeros = jnp.zeros(back.shape, BF16)
    o_ref[...] = apply_lower(inv_ref[...], split3(back), zeros) * scale


def flip(x, axes, perm):
    return lax.ppermute(x, axes, perm)


def ordered(own, recv, bit, axis=0):
    return jnp.where(
        bit == 0,
        jnp.concatenate([own, recv], axis=axis),
        jnp.concatenate([recv, own], axis=axis),
    )


def halves(x, bit):
    h = x.shape[0] // 2
    keep = lax.dynamic_slice_in_dim(x, bit * h, h, 0)
    send = lax.dynamic_slice_in_dim(x, (1 - bit) * h, h, 0)
    return keep, send


def sample_space(stamps, start_panel):
    pix = lax.axis_size("pix")
    samp = lax.axis_size("samp")
    n = stamps.shape[0] * pix * samp
    k = start_panel.shape[1]
    scale = math.sqrt(start_panel.shape[0] * pix)
    p = lax.axis_index("pix")
    s = lax.axis_index("samp")
    xor_pix = lambda b: [(i, i ^ b) for i in range(pix)]
    xor_samp = lambda b: [(i, i ^ b) for i in range(samp)]

    block = lax.all_to_all(stamps, ("pix", "samp"), split_axis=1, concat_axis=0, tiled=True)

    low = start_panel.astype(BF16).T
    for b in (1, 2, 4):
        low = ordered(low, flip(low, "pix", xor_pix(b)), p & b, axis=1)
    proj = dot(low, stamps, NT).astype(BF16)
    for b in (1, 2):
        proj = ordered(proj, flip(proj, "samp", xor_samp(b)), s & b, axis=1)
    for b in (1, 2, 4):
        proj = ordered(proj, flip(proj, "pix", xor_pix(b)), p & b, axis=1)
    q = kernel_call(
        basis_kernel, jax.ShapeDtypeStruct((k, n), F32), in_specs=vmem(), out_specs=vmem()[0]
    )(proj)

    core = p & 1
    x, y = (p >> 1) & 1, (p >> 2) & 1
    other = flip(block, "pix", xor_pix(1))
    bs = 2 * stamps.shape[0]
    width = n // 2 + bs
    px = block.shape[1]
    share = kernel_call(
        form_kernel,
        jax.ShapeDtypeStruct((n // 2, width + LANES), BF16),
        in_specs=[smem()] + vmem(3),
        out_specs=vmem()[0],
        scratch_shapes=[
            pltpu.VMEM((n + n // 2, px), BF16),
            pltpu.VMEM((n + n // 2, px), BF16),
            pltpu.VMEM((12 * k, n), BF16),
            pltpu.VMEM((12 * k, n + n // 2), BF16),
        ],
    )(core[None], block, other, q)

    first = [(i, i ^ (2 if i % 2 == 0 else 4)) for i in range(pix)]
    second = [(i, i ^ (4 if i % 2 == 0 else 2)) for i in range(pix)]
    bit_a = jnp.where(core == 0, x, y)
    bit_b = jnp.where(core == 0, y, x)
    z0, z1 = s & 1, (s >> 1) & 1
    stages = (
        ("pix", first, bit_a),
        ("pix", second, bit_b),
        ("samp", xor_samp(1), z0),
        ("samp", xor_samp(2), z1),
    )
    for axis, perm, bit in stages:
        keep, send = halves(share, bit)
        share = add_shares(keep, flip(send, axis, perm), k)

    share = ordered(share, flip(share, "samp", xor_samp(2)), z1)
    for axis, perm in (("samp", xor_samp(1)), ("pix", second), ("pix", first), ("pix", xor_pix(1))):
        share = jnp.concatenate([share, flip(share, axis, perm)], axis=0)
    at = jnp.arange(n // bs, dtype=jnp.int32)
    c_of = core ^ ((at >> 3) & 1)
    a_of = jnp.where(c_of == 0, x, y) ^ ((at >> 2) & 1)
    b_of = jnp.where(c_of == 0, y, x) ^ ((at >> 1) & 1)
    index = c_of * 8 + a_of * 4 + b_of * 2 + (z0 ^ (at & 1))

    proj, inv = kernel_call(
        iterate_kernel,
        (jax.ShapeDtypeStruct((k, n), BF16), jax.ShapeDtypeStruct((k, LANES), F32)),
        in_specs=[smem()] + vmem(3),
        out_specs=tuple(vmem(2)),
        scratch_shapes=[
            pltpu.VMEM((n, n), BF16),
            pltpu.VMEM((8 * k, n), BF16),
            pltpu.VMEM((12 * k, n), BF16),
        ],
    )(index, share, q, proj)

    mine = kernel_call(
        functools.partial(finish_kernel, scale),
        jax.ShapeDtypeStruct((k, px), F32),
        in_specs=vmem(3),
        out_specs=vmem()[0],
    )(proj, inv, block)
    for b in (1, 2):
        mine = ordered(mine, flip(mine, "samp", xor_samp(b)), s & b, axis=1)
    return mine.T


def solution(mesh):
    pix, samp = mesh.shape["pix"], mesh.shape["samp"]

    def local(stamps, start_panel):
        n = stamps.shape[0] * pix * samp
        k = start_panel.shape[1]
        if n <= SAMPLE_SPACE_LIMIT and (pix, samp) == (8, 4) and 4 * k == LANES:
            return sample_space(stamps, start_panel)
        return pixel_space(stamps, start_panel)

    return jax.shard_map(
        local,
        mesh=mesh,
        in_specs=(P(("samp", "pix"), None), P("pix", None)),
        out_specs=P("pix", None),
        check_vma=False,
    )
```

```python
import functools
import math

import jax
import jax.numpy as jnp
from jax import lax
from jax.experimental import pallas as pl
from jax.experimental.pallas import tpu as pltpu
from jax.sharding import PartitionSpec as P


ITERS = 10
LANES = 128
PANEL = 16
GROUP = 40
SAMPLE_SPACE_LIMIT = 4096
INTERPRET = False
F32 = jnp.float32
BF16 = jnp.bfloat16

NN = (((1,), (0,)), ((), ()))
NT = (((1,), (1,)), ((), ()))
TN = (((0,), (0,)), ((), ()))


def orthonormal(back, gram):
    lower = jnp.linalg.cholesky(gram)
    return lax.linalg.triangular_solve(lower, back, left_side=False, lower=True, transpose_a=True)


def pixel_space(stamps, start_panel):
    block = lax.all_to_all(stamps, "pix", split_axis=1, concat_axis=0, tiled=True)

    def sweep(step, panel):
        partial_value = jnp.dot(block, panel.astype(BF16), preferred_element_type=F32)
        proj = lax.psum(partial_value.astype(BF16), "pix")
        back = lax.dot_general(block, proj, TN, preferred_element_type=F32)
        summed = lax.psum(back.astype(BF16), "samp").astype(F32)
        gram = lax.psum(jnp.dot(summed.T, summed, precision=lax.Precision.HIGHEST), "pix")
        return orthonormal(summed, gram)

    panel = lax.fori_loop(0, ITERS, sweep, start_panel)
    return panel * math.sqrt(start_panel.shape[0] * lax.axis_size("pix"))


def dot(a, b, dims):
    return lax.dot_general(a, b, dims, preferred_element_type=F32)


def split3(x):
    hi = x.astype(BF16)
    rest = x - hi.astype(F32)
    mid = rest.astype(BF16)
    lo = (rest - mid.astype(F32)).astype(BF16)
    return hi, mid, lo


def kernel_call(body, out_shape, **kw):
    return pl.pallas_call(body, out_shape=out_shape, interpret=INTERPRET, **kw)


def vmem(n=1):
    return [pl.BlockSpec(memory_space=pltpu.VMEM)] * n


def smem():
    return pl.BlockSpec(memory_space=pltpu.SMEM)


def inverse_lower(gram):
    k = gram.shape[0]
    lane = lax.broadcasted_iota(jnp.int32, gram.shape, 1)
    row = lax.broadcasted_iota(jnp.int32, gram.shape, 0)
    m = jnp.where(lane < k, gram, jnp.where(lane == row + k, 1.0, 0.0))
    pivots = jnp.ones(gram.shape, F32)
    for start in range(0, k, PANEL):
        cols = [jnp.broadcast_to(m[:, j : j + 1], m.shape) for j in range(start, start + PANEL)]
        for t in range(PANEL):
            j = start + t
            pivot = cols[t][j : j + 1, :]
            factor = jnp.where(row > j, cols[t] * (1.0 / pivot), 0.0)
            pivots = jnp.where(row == j, pivot, pivots)
            for later in range(t + 1, PANEL):
                cols[later] = cols[later] - factor * cols[later][j : j + 1, :]
            m = m - factor * m[j : j + 1, :]
    return pltpu.roll(m * lax.rsqrt(pivots), LANES - k, 1)


def lane_sum3(x, k):
    return x + pltpu.roll(x, LANES - k, 1) + pltpu.roll(x, LANES - 2 * k, 1)


def gram_of(left, parts, zeros):
    k = left.shape[0]
    stack = jnp.concatenate(list(parts) + [zeros], axis=0)
    return lane_sum3(dot(left, stack, NT), k)


def apply_lower(inv, parts, zeros):
    k = inv.shape[0]
    lane = lax.broadcasted_iota(jnp.int32, inv.shape, 1)
    inv = jnp.where(lane < k, inv, 0.0)
    inv = inv + pltpu.roll(inv, k, 1)
    inv = inv + pltpu.roll(inv, 2 * k, 1)
    h1, h2, h3 = [h.astype(F32) for h in split3(inv)]
    first = jnp.where(lane < 3 * k, h1, h2)
    second = jnp.where(lane < k, h2, jnp.where(lane < 2 * k, h3, 0.0))
    left = jnp.concatenate([first, second], axis=1).astype(BF16)
    y1, y2, y3 = parts
    right = jnp.concatenate([y1, y2, y3, y1, y2, y1, zeros, zeros], axis=0)
    return dot(left, right, NN)


def basis_kernel(p0_ref, q_ref):
    p0 = p0_ref[...]
    zeros = jnp.zeros_like(p0)
    gram = gram_of(p0, (p0, zeros, zeros), zeros)
    q_ref[...] = apply_lower(inverse_lower(gram), (p0, zeros, zeros), zeros)


def split_off(own_ref, other_ref, q_ref, left, right):
    k = q_ref.shape[0]
    q = q_ref[...]
    zeros = jnp.zeros(q.shape, BF16)
    q1, q2, q3 = split3(q)
    qs = jnp.concatenate([q1, q2, q3], axis=0)
    w = jnp.zeros(q.shape, F32)
    for ref in (own_ref, other_ref):
        t3 = dot(qs, ref[...], NN)
        ts = split3(t3[:k] + t3[k : 2 * k] + t3[2 * k :])
        w3 = dot(jnp.concatenate(ts, axis=0), ref[...], NT)
        w += w3[:k] + w3[k : 2 * k] + w3[2 * k :]
    ws = jnp.concatenate(list(split3(w)) + [zeros], axis=0)
    m = lane_sum3(dot(q1, ws, NT) + dot(q2, ws, NT) + dot(q3, ws, NT), k)
    w1, w2, w3 = split3(w - 0.5 * apply_lower(m, (q1, q2, q3), zeros))
    left[...] = jnp.concatenate([q1, w1, q1, w1, q1, w1, q2, w2, q2, w2, q3, w3], axis=0)
    right[...] = jnp.concatenate([w1, q1, w2, q2, w3, q3, w1, q1, w2, q2, w1, q1], axis=0)


def form_rows(k, first, own_ref, other_ref, left, right, out_ref, own_win, other_win, right_win):
    n = own_ref.shape[0]
    rows, width = out_ref.shape
    width -= LANES
    bs = width - n // 2
    nb = n // bs
    for b in range(own_win.shape[0] // bs):
        at = pl.multiple_of(lax.rem(first + b, nb) * bs, bs)
        own_win[b * bs : (b + 1) * bs, :] = own_ref[pl.ds(at, bs), :]
        other_win[b * bs : (b + 1) * bs, :] = other_ref[pl.ds(at, bs), :]
        right_win[:, b * bs : (b + 1) * bs] = right[:, pl.ds(at, bs)]
    eye = lax.broadcasted_iota(jnp.int32, (bs, bs), 0) == lax.broadcasted_iota(jnp.int32, (bs, bs), 1)
    for i in range(rows // bs):
        at = pl.multiple_of((first + i) * bs, bs)
        to, end = i * bs, i * bs + width
        s = dot(own_win[to : to + bs, :], own_win[to:end, :], NT)
        s += dot(other_win[to : to + bs, :], other_win[to:end, :], NT)
        s -= dot(left[:, pl.ds(at, bs)], right_win[:, to:end], TN)
        corner = s[:, :bs]
        diagonal = jnp.sum(jnp.where(eye, corner, 0.0), axis=0, keepdims=True)
        out_ref[to : to + bs, :bs] = jnp.where(eye, 0.0, corner).astype(BF16)
        out_ref[to : to + bs, bs:width] = s[:, bs:].astype(BF16)
        side = []
        for g, d in enumerate(split3(diagonal)):
            side.append(right_win[2 * g * k : (2 * g + 1) * k, to : to + bs].astype(F32))
            side.append(jnp.broadcast_to(d.astype(F32), (GROUP - k, bs)))
        side.append(jnp.zeros((LANES - 3 * GROUP, bs), F32))
        out_ref[to : to + bs, width:] = jnp.concatenate(side, axis=0).T.astype(BF16)


def form_first_kernel(at_ref, own_ref, other_ref, q_ref, out_ref, left, right, *wins):
    split_off(own_ref, other_ref, q_ref, left, right)
    form_rows(q_ref.shape[0], at_ref[0], own_ref, other_ref, left, right, out_ref, *wins)


def form_second_kernel(k, at_ref, own_ref, other_ref, left, right, out_ref, *wins):
    form_rows(k, at_ref[0], own_ref, other_ref, left, right, out_ref, *wins)


def add_kernel(half_ref, a_ref, b_ref, o_ref):
    h = o_ref.shape[0]
    width = a_ref.shape[1] - LANES
    at = pl.multiple_of(half_ref[0] * h, h)
    a, b = a_ref[pl.ds(at, h), :], b_ref[pl.ds(at, h), :]
    o_ref[:, :width] = (a[:, :width].astype(F32) + b[:, :width].astype(F32)).astype(BF16)
    x = lane_sum3(a[:, width:].astype(F32), GROUP) + lane_sum3(b[:, width:].astype(F32), GROUP)
    lane = lax.broadcasted_iota(jnp.int32, x.shape, 1)
    h1, h2, h3 = [part.astype(F32) for part in split3(x)]
    packed = jnp.where(lane < 2 * GROUP, pltpu.roll(h2, GROUP, 1), pltpu.roll(h3, 2 * GROUP, 1))
    packed = jnp.where(lane < GROUP, h1, packed)
    o_ref[:, width:] = jnp.where(lane < 3 * GROUP, packed, 0.0).astype(BF16)


def add_shares(a, b, half=None):
    rows = a.shape[0] // (1 if half is None else 2)
    half = jnp.zeros((1,), jnp.int32) if half is None else half[None]
    return kernel_call(
        add_kernel,
        jax.ShapeDtypeStruct((rows, a.shape[1]), BF16),
        in_specs=[smem()] + vmem(2),
        out_specs=vmem()[0],
    )(half, a, b)


def iterate_kernel(index_ref, near_ref, far_ref, q_ref, p0_ref, p_ref, inv_ref, full, u, v, diag):
    k, n = q_ref.shape
    width = near_ref.shape[1] - LANES
    bs = width - n // 2
    nb = n // bs

    def unpack(share_ref, offset):
        def one(r, _):
            i = index_ref[r + offset]
            frm = pl.multiple_of(r * bs, bs)
            to = pl.multiple_of(i * bs, bs)
            for d in range(nb // 2 + 1):
                part = share_ref[pl.ds(frm, bs), d * bs : (d + 1) * bs]
                at = pl.multiple_of(lax.rem(i + d, nb) * bs, bs)
                full[pl.ds(to, bs), pl.ds(at, bs)] = part
                if 0 < d < nb // 2:
                    full[pl.ds(at, bs), pl.ds(to, bs)] = part.T
            side = share_ref[pl.ds(frm, bs), width:].astype(F32).T
            side = side[:GROUP] + side[GROUP : 2 * GROUP] + side[2 * GROUP : 3 * GROUP]
            w = side[:k]
            diag[:, pl.ds(to, bs)] = side[k : k + 8]
            q = q_ref[:, pl.ds(to, bs)]
            us = split3(jnp.concatenate([w, q], axis=0))
            v1, v2, v3 = split3(jnp.concatenate([q, w], axis=0))
            u[:, pl.ds(to, bs)] = jnp.concatenate(list(us) + [jnp.zeros((2 * k, bs), BF16)], axis=0)
            v[:, pl.ds(to, bs)] = jnp.concatenate([v1, v2, v3, v1, v2, v1], axis=0)
            return 0

        lax.fori_loop(0, nb // 2, one, 0)

    unpack(near_ref, 0)
    unpack(far_ref, nb // 2)

    zeros = jnp.zeros((k, n), BF16)
    lane = lax.broadcasted_iota(jnp.int32, (k, LANES), 1)

    def product(p):
        t = dot(p, u[...], NT)
        t = t[:, :LANES] + t[:, LANES:]
        t = t + pltpu.roll(t, 2 * k, 1)
        h1, h2, h3 = [h.astype(F32) for h in split3(t)]
        low = lane < 2 * k
        ts = jnp.concatenate([h1, jnp.where(low, h1, h2), jnp.where(low, h2, h3)], axis=1).astype(BF16)
        y = dot(p, full[...], NN) + dot(ts, v[...], NN) + p.astype(F32) * diag[0:1, :]
        return split3(y)

    def sweep(step, p):
        parts = product(p)
        inv = inverse_lower(gram_of(p, parts, zeros))
        return apply_lower(inv, parts, zeros).astype(BF16)

    p = lax.fori_loop(0, ITERS - 1, sweep, p0_ref[...])
    p_ref[...] = p
    inv_ref[...] = inverse_lower(gram_of(p, product(p), zeros))


def finish_kernel(scale, p_ref, inv_ref, block_ref, o_ref):
    back = dot(p_ref[...], block_ref[...], NN)
    zeros = jnp.zeros(back.shape, BF16)
    o_ref[...] = apply_lower(inv_ref[...], split3(back), zeros) * scale


def flip(x, axes, perm):
    return lax.ppermute(x, axes, perm)


def ordered(own, recv, bit, axis=0):
    return jnp.where(
        bit == 0,
        jnp.concatenate([own, recv], axis=axis),
        jnp.concatenate([recv, own], axis=axis),
    )


def sample_space(stamps, start_panel):
    pix = lax.axis_size("pix")
    samp = lax.axis_size("samp")
    n = stamps.shape[0] * pix * samp
    k = start_panel.shape[1]
    scale = math.sqrt(start_panel.shape[0] * pix)
    p = lax.axis_index("pix")
    s = lax.axis_index("samp")
    xor_pix = lambda b: [(i, i ^ b) for i in range(pix)]
    xor_samp = lambda b: [(i, i ^ b) for i in range(samp)]

    core = p & 1
    x, y = (p >> 1) & 1, (p >> 2) & 1
    z0, z1 = s & 1, (s >> 1) & 1

    low = start_panel.astype(BF16).T
    for b in (1, 2, 4):
        low = ordered(low, flip(low, "pix", xor_pix(b)), p & b, axis=1)

    block = lax.all_to_all(stamps, ("pix", "samp"), split_axis=1, concat_axis=0, tiled=True)

    proj = dot(low, stamps, NT).astype(BF16)
    for b in (1, 2):
        proj = ordered(proj, flip(proj, "samp", xor_samp(b)), s & b, axis=1)
    for b in (1, 2, 4):
        proj = ordered(proj, flip(proj, "pix", xor_pix(b)), p & b, axis=1)
    q = kernel_call(
        basis_kernel, jax.ShapeDtypeStruct((k, n), F32), in_specs=vmem(), out_specs=vmem()[0]
    )(proj)

    first = [(i, i ^ (2 if i % 2 == 0 else 4)) for i in range(pix)]
    second = [(i, i ^ (4 if i % 2 == 0 else 2)) for i in range(pix)]
    bit_a = jnp.where(core == 0, x, y)
    bit_b = jnp.where(core == 0, y, x)

    other = flip(block, "pix", xor_pix(1))
    bs = 2 * stamps.shape[0]
    nb = n // bs
    px = block.shape[1]
    width = n // 2 + bs
    rows = n // 4
    window = rows - bs + width
    piece = jax.ShapeDtypeStruct((rows, width + LANES), BF16)
    stack = jax.ShapeDtypeStruct((12 * k, n), BF16)
    wins = [
        pltpu.VMEM((window, px), BF16),
        pltpu.VMEM((window, px), BF16),
        pltpu.VMEM((12 * k, window), BF16),
    ]
    blocks = rows // bs
    at = core * 2 * blocks
    send, left, right = kernel_call(
        form_first_kernel,
        (piece, stack, stack),
        in_specs=[smem()] + vmem(3),
        out_specs=tuple(vmem(3)),
        scratch_shapes=wins,
    )((at + (1 - bit_a) * blocks)[None], block, other, q)
    recv = flip(send, "pix", first)
    keep = kernel_call(
        functools.partial(form_second_kernel, k),
        piece,
        in_specs=[smem()] + vmem(4),
        out_specs=vmem()[0],
        scratch_shapes=wins,
    )((at + bit_a * blocks)[None], block, other, left, right)
    for axis, perm, bit in (
        ("pix", second, bit_b),
        ("samp", xor_samp(1), z0),
        ("samp", xor_samp(2), z1),
    ):
        send = add_shares(keep, recv, 1 - bit)
        keep = add_shares(keep, recv, bit)
        recv = flip(send, axis, perm)
    share = add_shares(keep, recv)

    share = ordered(share, flip(share, "samp", xor_samp(2)), z1)
    for axis, perm in (("samp", xor_samp(1)), ("pix", second), ("pix", first)):
        share = jnp.concatenate([share, flip(share, axis, perm)], axis=0)
    far = flip(share, "pix", xor_pix(1))
    at = jnp.arange(nb, dtype=jnp.int32)
    c_of = core ^ ((at >> 3) & 1)
    a_of = jnp.where(c_of == 0, x, y) ^ ((at >> 2) & 1)
    b_of = jnp.where(c_of == 0, y, x) ^ ((at >> 1) & 1)
    index = c_of * 8 + a_of * 4 + b_of * 2 + (z0 ^ (at & 1))

    proj, inv = kernel_call(
        iterate_kernel,
        (jax.ShapeDtypeStruct((k, n), BF16), jax.ShapeDtypeStruct((k, LANES), F32)),
        in_specs=[smem()] + vmem(4),
        out_specs=tuple(vmem(2)),
        scratch_shapes=[
            pltpu.VMEM((n, n), BF16),
            pltpu.VMEM((8 * k, n), BF16),
            pltpu.VMEM((12 * k, n), BF16),
            pltpu.VMEM((8, n), F32),
        ],
    )(index, share, far, q, proj)

    mine = kernel_call(
        functools.partial(finish_kernel, scale),
        jax.ShapeDtypeStruct((k, px), F32),
        in_specs=vmem(3),
        out_specs=vmem()[0],
    )(proj, inv, block)
    for b in (2, 1):
        mine = jnp.concatenate([mine, flip(mine, "samp", xor_samp(b))], axis=1)
    parts = [mine[:, i * px : (i + 1) * px] for i in range(samp)]
    by_distance = {0: parts[0], 2: parts[1], 1: parts[2], 3: parts[3]}
    swap0 = [jnp.where(z0 == 0, by_distance[i], by_distance[i ^ 1]) for i in range(samp)]
    swap1 = [jnp.where(z1 == 0, swap0[i], swap0[i ^ 2]) for i in range(samp)]
    return jnp.concatenate(swap1, axis=1).T


def solution(mesh):
    pix, samp = mesh.shape["pix"], mesh.shape["samp"]

    def local(stamps, start_panel):
        n = stamps.shape[0] * pix * samp
        k = start_panel.shape[1]
        if n <= SAMPLE_SPACE_LIMIT and (pix, samp) == (8, 4) and 4 * k == LANES:
            return sample_space(stamps, start_panel)
        return pixel_space(stamps, start_panel)

    return jax.shard_map(
        local,
        mesh=mesh,
        in_specs=(P(("samp", "pix"), None), P("pix", None)),
        out_specs=P("pix", None),
        check_vma=False,
    )
```

```python
import functools
import math

import jax
import jax.numpy as jnp
from jax import lax
from jax.experimental import pallas as pl
from jax.experimental.pallas import tpu as pltpu
from jax.sharding import PartitionSpec as P


ITERS = 10
LANES = 128
PANEL = 16
GROUP = 40
SAMPLE_SPACE_LIMIT = 4096
F32 = jnp.float32
BF16 = jnp.bfloat16

NN = (((1,), (0,)), ((), ()))
NT = (((1,), (1,)), ((), ()))
TN = (((0,), (0,)), ((), ()))


def orthonormal(back, gram):
    lower = jnp.linalg.cholesky(gram)
    return lax.linalg.triangular_solve(lower, back, left_side=False, lower=True, transpose_a=True)


def pixel_space(stamps, start_panel):
    block = lax.all_to_all(stamps, "pix", split_axis=1, concat_axis=0, tiled=True)

    def sweep(step, panel):
        partial_value = jnp.dot(block, panel.astype(BF16), preferred_element_type=F32)
        proj = lax.psum(partial_value.astype(BF16), "pix")
        back = lax.dot_general(block, proj, TN, preferred_element_type=F32)
        summed = lax.psum(back.astype(BF16), "samp").astype(F32)
        gram = lax.psum(jnp.dot(summed.T, summed, precision=lax.Precision.HIGHEST), "pix")
        return orthonormal(summed, gram)

    panel = lax.fori_loop(0, ITERS, sweep, start_panel)
    return panel * math.sqrt(start_panel.shape[0] * lax.axis_size("pix"))


def dot(a, b, dims):
    return lax.dot_general(a, b, dims, preferred_element_type=F32)


def split3(x):
    hi = x.astype(BF16)
    rest = x - hi.astype(F32)
    mid = rest.astype(BF16)
    lo = (rest - mid.astype(F32)).astype(BF16)
    return hi, mid, lo


def kernel_call(body, out_shape, in_specs=(), scratch_mib=8, **kw):
    single = not isinstance(out_shape, tuple)
    outs = tuple(pltpu.VMEM(o.shape, o.dtype) for o in ((out_shape,) if single else out_shape))
    call = pl.pallas_call(
        body,
        out_shape=outs[0] if single else outs,
        in_specs=in_specs,
        compiler_params=pltpu.CompilerParams(vmem_limit_bytes=scratch_mib << 20),
        **kw,
    )

    def place(x, spec):
        if spec.memory_space != pltpu.VMEM:
            return x
        return pltpu.with_memory_space_constraint(x, pltpu.VMEM)

    return lambda *args: call(*map(place, args, in_specs))


def vmem(n=1):
    return [pl.BlockSpec(memory_space=pltpu.VMEM)] * n


def smem():
    return pl.BlockSpec(memory_space=pltpu.SMEM)


def inverse_lower(gram):
    k = gram.shape[0]
    lane = lax.broadcasted_iota(jnp.int32, gram.shape, 1)
    row = lax.broadcasted_iota(jnp.int32, gram.shape, 0)
    m = jnp.where(lane < k, gram, jnp.where(lane == row + k, 1.0, 0.0))
    pivots = jnp.ones(gram.shape, F32)
    for start in range(0, k, PANEL):
        cols = [jnp.broadcast_to(m[:, j : j + 1], m.shape) for j in range(start, start + PANEL)]
        for t in range(PANEL):
            j = start + t
            pivot = cols[t][j : j + 1, :]
            factor = jnp.where(row > j, cols[t] * (1.0 / pivot), 0.0)
            pivots = jnp.where(row == j, pivot, pivots)
            for later in range(t + 1, PANEL):
                cols[later] = cols[later] - factor * cols[later][j : j + 1, :]
            m = m - factor * m[j : j + 1, :]
    return pltpu.roll(m * lax.rsqrt(pivots), LANES - k, 1)


def lane_sum3(x, k):
    return x + pltpu.roll(x, LANES - k, 1) + pltpu.roll(x, LANES - 2 * k, 1)


def gram_of(left, parts, zeros):
    k = left.shape[0]
    stack = jnp.concatenate(list(parts) + [zeros], axis=0)
    return lane_sum3(dot(left, stack, NT), k)


def apply_lower(inv, parts, zeros):
    k = inv.shape[0]
    lane = lax.broadcasted_iota(jnp.int32, inv.shape, 1)
    inv = jnp.where(lane < k, inv, 0.0)
    inv = inv + pltpu.roll(inv, k, 1)
    inv = inv + pltpu.roll(inv, 2 * k, 1)
    h1, h2, h3 = [h.astype(F32) for h in split3(inv)]
    first = jnp.where(lane < 3 * k, h1, h2)
    second = jnp.where(lane < k, h2, jnp.where(lane < 2 * k, h3, 0.0))
    left = jnp.concatenate([first, second], axis=1).astype(BF16)
    y1, y2, y3 = parts
    right = jnp.concatenate([y1, y2, y3, y1, y2, y1, zeros, zeros], axis=0)
    return dot(left, right, NN)


def basis_kernel(p0_ref, q_ref):
    p0 = p0_ref[...]
    zeros = jnp.zeros_like(p0)
    gram = gram_of(p0, (p0, zeros, zeros), zeros)
    q_ref[...] = apply_lower(inverse_lower(gram), (p0, zeros, zeros), zeros)


def split_off(own_ref, other_ref, q_ref, left, right):
    k = q_ref.shape[0]
    q = q_ref[...]
    zeros = jnp.zeros(q.shape, BF16)
    q1, q2, q3 = split3(q)
    qs = jnp.concatenate([q1, q2, q3], axis=0)
    w = jnp.zeros(q.shape, F32)
    for ref in (own_ref, other_ref):
        t3 = dot(qs, ref[...], NN)
        ts = split3(t3[:k] + t3[k : 2 * k] + t3[2 * k :])
        w3 = dot(jnp.concatenate(ts, axis=0), ref[...], NT)
        w += w3[:k] + w3[k : 2 * k] + w3[2 * k :]
    ws = jnp.concatenate(list(split3(w)) + [zeros], axis=0)
    m = lane_sum3(dot(q1, ws, NT) + dot(q2, ws, NT) + dot(q3, ws, NT), k)
    w1, w2, w3 = split3(w - 0.5 * apply_lower(m, (q1, q2, q3), zeros))
    left[...] = jnp.concatenate([q1, w1, q1, w1, q1, w1, q2, w2, q2, w2, q3, w3], axis=0)
    right[...] = jnp.concatenate([w1, q1, w2, q2, w3, q3, w1, q1, w2, q2, w1, q1], axis=0)


def form_rows(k, first, own_ref, other_ref, left, right, out_ref, own_win, other_win, right_win):
    n = own_ref.shape[0]
    rows, width = out_ref.shape
    width -= LANES
    bs = width - n // 2
    nb = n // bs
    for b in range(own_win.shape[0] // bs):
        at = pl.multiple_of(lax.rem(first + b, nb) * bs, bs)
        own_win[b * bs : (b + 1) * bs, :] = own_ref[pl.ds(at, bs), :]
        other_win[b * bs : (b + 1) * bs, :] = other_ref[pl.ds(at, bs), :]
        right_win[:, b * bs : (b + 1) * bs] = right[:, pl.ds(at, bs)]
    eye = lax.broadcasted_iota(jnp.int32, (bs, bs), 0) == lax.broadcasted_iota(jnp.int32, (bs, bs), 1)
    for i in range(rows // bs):
        at = pl.multiple_of((first + i) * bs, bs)
        to, end = i * bs, i * bs + width
        s = dot(own_win[to : to + bs, :], own_win[to:end, :], NT)
        s += dot(other_win[to : to + bs, :], other_win[to:end, :], NT)
        s -= dot(left[:, pl.ds(at, bs)], right_win[:, to:end], TN)
        corner = s[:, :bs]
        diagonal = jnp.sum(jnp.where(eye, corner, 0.0), axis=0, keepdims=True)
        out_ref[to : to + bs, :bs] = jnp.where(eye, 0.0, corner).astype(BF16)
        out_ref[to : to + bs, bs:width] = s[:, bs:].astype(BF16)
        side = []
        for g, d in enumerate(split3(diagonal)):
            side.append(right_win[2 * g * k : (2 * g + 1) * k, to : to + bs].astype(F32))
            side.append(jnp.broadcast_to(d.astype(F32), (GROUP - k, bs)))
        side.append(jnp.zeros((LANES - 3 * GROUP, bs), F32))
        out_ref[to : to + bs, width:] = jnp.concatenate(side, axis=0).T.astype(BF16)


def form_kernel(at_ref, own_ref, other_ref, q_ref, out_ref, left, right, *wins):
    split_off(own_ref, other_ref, q_ref, left, right)
    form_rows(q_ref.shape[0], at_ref[0], own_ref, other_ref, left, right, out_ref, *wins)


def add_kernel(half_ref, a_ref, b_ref, o_ref):
    h = o_ref.shape[0]
    width = a_ref.shape[1] - LANES
    at = pl.multiple_of(half_ref[0] * h, h)
    a, b = a_ref[pl.ds(at, h), :], b_ref[pl.ds(at, h), :]
    o_ref[:, :width] = (a[:, :width].astype(F32) + b[:, :width].astype(F32)).astype(BF16)
    x = lane_sum3(a[:, width:].astype(F32), GROUP) + lane_sum3(b[:, width:].astype(F32), GROUP)
    lane = lax.broadcasted_iota(jnp.int32, x.shape, 1)
    h1, h2, h3 = [part.astype(F32) for part in split3(x)]
    packed = jnp.where(lane < 2 * GROUP, pltpu.roll(h2, GROUP, 1), pltpu.roll(h3, 2 * GROUP, 1))
    packed = jnp.where(lane < GROUP, h1, packed)
    o_ref[:, width:] = jnp.where(lane < 3 * GROUP, packed, 0.0).astype(BF16)


def add_shares(a, b, half=None):
    rows = a.shape[0] // (1 if half is None else 2)
    half = jnp.zeros((1,), jnp.int32) if half is None else half[None]
    return kernel_call(
        add_kernel,
        jax.ShapeDtypeStruct((rows, a.shape[1]), BF16),
        in_specs=[smem()] + vmem(2),
        out_specs=vmem()[0],
    )(half, a, b)


def iterate_kernel(index_ref, near_ref, far_ref, q_ref, p0_ref, p_ref, inv_ref, full, u, v, diag):
    k, n = q_ref.shape
    width = near_ref.shape[1] - LANES
    bs = width - n // 2
    nb = n // bs

    def unpack(share_ref, offset):
        def one(r, _):
            i = index_ref[r + offset]
            frm = pl.multiple_of(r * bs, bs)
            to = pl.multiple_of(i * bs, bs)
            for d in range(nb // 2 + 1):
                part = share_ref[pl.ds(frm, bs), d * bs : (d + 1) * bs]
                at = pl.multiple_of(lax.rem(i + d, nb) * bs, bs)
                full[pl.ds(to, bs), pl.ds(at, bs)] = part
                if 0 < d < nb // 2:
                    full[pl.ds(at, bs), pl.ds(to, bs)] = part.T
            side = share_ref[pl.ds(frm, bs), width:].astype(F32).T
            side = side[:GROUP] + side[GROUP : 2 * GROUP] + side[2 * GROUP : 3 * GROUP]
            w = side[:k]
            diag[:, pl.ds(to, bs)] = side[k : k + 8]
            q = q_ref[:, pl.ds(to, bs)]
            us = split3(jnp.concatenate([w, q], axis=0))
            v1, v2, v3 = split3(jnp.concatenate([q, w], axis=0))
            u[:, pl.ds(to, bs)] = jnp.concatenate(list(us) + [jnp.zeros((2 * k, bs), BF16)], axis=0)
            v[:, pl.ds(to, bs)] = jnp.concatenate([v1, v2, v3, v1, v2, v1], axis=0)
            return 0

        lax.fori_loop(0, nb // 2, one, 0)

    unpack(near_ref, 0)
    unpack(far_ref, nb // 2)

    zeros = jnp.zeros((k, n), BF16)
    lane = lax.broadcasted_iota(jnp.int32, (k, LANES), 1)

    def product(p):
        t = dot(p, u[...], NT)
        t = t[:, :LANES] + t[:, LANES:]
        t = t + pltpu.roll(t, 2 * k, 1)
        h1, h2, h3 = [h.astype(F32) for h in split3(t)]
        low = lane < 2 * k
        ts = jnp.concatenate([h1, jnp.where(low, h1, h2), jnp.where(low, h2, h3)], axis=1).astype(BF16)
        y = dot(p, full[...], NN) + dot(ts, v[...], NN) + p.astype(F32) * diag[0:1, :]
        return split3(y)

    def sweep(step, p):
        parts = product(p)
        inv = inverse_lower(gram_of(p, parts, zeros))
        return apply_lower(inv, parts, zeros).astype(BF16)

    p = lax.fori_loop(0, ITERS - 1, sweep, p0_ref[...])
    p_ref[...] = p
    inv_ref[...] = inverse_lower(gram_of(p, product(p), zeros))


def finish_kernel(scale, p_ref, inv_ref, block_ref, o_ref):
    back = dot(p_ref[...], block_ref[...], NN)
    zeros = jnp.zeros(back.shape, BF16)
    o_ref[...] = apply_lower(inv_ref[...], split3(back), zeros) * scale


def flip(x, axes, perm):
    return lax.ppermute(x, axes, perm)


def ordered(own, recv, bit, axis=0):
    return jnp.where(
        bit == 0,
        jnp.concatenate([own, recv], axis=axis),
        jnp.concatenate([recv, own], axis=axis),
    )


def sample_space(stamps, start_panel):
    pix = lax.axis_size("pix")
    samp = lax.axis_size("samp")
    n = stamps.shape[0] * pix * samp
    k = start_panel.shape[1]
    scale = math.sqrt(start_panel.shape[0] * pix)
    p = lax.axis_index("pix")
    s = lax.axis_index("samp")
    xor_pix = lambda b: [(i, i ^ b) for i in range(pix)]
    xor_samp = lambda b: [(i, i ^ b) for i in range(samp)]

    core = p & 1
    x, y = (p >> 1) & 1, (p >> 2) & 1
    z0, z1 = s & 1, (s >> 1) & 1

    low = start_panel.astype(BF16).T
    for b in (1, 2, 4):
        low = ordered(low, flip(low, "pix", xor_pix(b)), p & b, axis=1)

    block = lax.all_to_all(stamps, ("pix", "samp"), split_axis=1, concat_axis=0, tiled=True)

    proj = dot(low, stamps, NT).astype(BF16)
    for b in (1, 2):
        proj = ordered(proj, flip(proj, "samp", xor_samp(b)), s & b, axis=1)
    for b in (1, 2, 4):
        proj = ordered(proj, flip(proj, "pix", xor_pix(b)), p & b, axis=1)
    q = kernel_call(
        basis_kernel, jax.ShapeDtypeStruct((k, n), F32), in_specs=vmem(), out_specs=vmem()[0]
    )(proj)

    first = [(i, i ^ (2 if i % 2 == 0 else 4)) for i in range(pix)]
    second = [(i, i ^ (4 if i % 2 == 0 else 2)) for i in range(pix)]
    bit_a = jnp.where(core == 0, x, y)
    bit_b = jnp.where(core == 0, y, x)

    other = flip(block, "pix", xor_pix(1))
    bs = 2 * stamps.shape[0]
    nb = n // bs
    px = block.shape[1]
    width = n // 2 + bs
    rows = n // 4
    window = rows - bs + width
    piece = jax.ShapeDtypeStruct((rows, width + LANES), BF16)
    form = kernel_call(
        form_kernel,
        piece,
        in_specs=[smem()] + vmem(3),
        out_specs=vmem()[0],
        scratch_mib=20,
        scratch_shapes=[
            pltpu.VMEM((12 * k, n), BF16),
            pltpu.VMEM((12 * k, n), BF16),
            pltpu.VMEM((window, px), BF16),
            pltpu.VMEM((window, px), BF16),
            pltpu.VMEM((12 * k, window), BF16),
        ],
    )
    blocks = rows // bs
    at = core * 2 * blocks
    send = form((at + (1 - bit_a) * blocks)[None], block, other, q)
    recv = flip(send, "pix", first)
    keep = form((at + bit_a * blocks)[None], block, other, q)
    for axis, perm, bit in (
        ("pix", second, bit_b),
        ("samp", xor_samp(1), z0),
        ("samp", xor_samp(2), z1),
    ):
        send = add_shares(keep, recv, 1 - bit)
        keep = add_shares(keep, recv, bit)
        recv = flip(send, axis, perm)
    share = add_shares(keep, recv)

    share = ordered(share, flip(share, "samp", xor_samp(2)), z1)
    for axis, perm in (("samp", xor_samp(1)), ("pix", second), ("pix", first)):
        share = jnp.concatenate([share, flip(share, axis, perm)], axis=0)
    far = flip(share, "pix", xor_pix(1))
    at = jnp.arange(nb, dtype=jnp.int32)
    c_of = core ^ ((at >> 3) & 1)
    a_of = jnp.where(c_of == 0, x, y) ^ ((at >> 2) & 1)
    b_of = jnp.where(c_of == 0, y, x) ^ ((at >> 1) & 1)
    index = c_of * 8 + a_of * 4 + b_of * 2 + (z0 ^ (at & 1))

    proj, inv = kernel_call(
        iterate_kernel,
        (jax.ShapeDtypeStruct((k, n), BF16), jax.ShapeDtypeStruct((k, LANES), F32)),
        in_specs=[smem()] + vmem(4),
        out_specs=tuple(vmem(2)),
        scratch_mib=24,
        scratch_shapes=[
            pltpu.VMEM((n, n), BF16),
            pltpu.VMEM((8 * k, n), BF16),
            pltpu.VMEM((12 * k, n), BF16),
            pltpu.VMEM((8, n), F32),
        ],
    )(index, share, far, q, proj)

    mine = kernel_call(
        functools.partial(finish_kernel, scale),
        jax.ShapeDtypeStruct((k, px), F32),
        in_specs=vmem(3),
        out_specs=vmem()[0],
    )(proj, inv, block)
    for b in (2, 1):
        mine = jnp.concatenate([mine, flip(mine, "samp", xor_samp(b))], axis=1)
    parts = [mine[:, i * px : (i + 1) * px] for i in range(samp)]
    by_distance = {0: parts[0], 2: parts[1], 1: parts[2], 3: parts[3]}
    swap0 = [jnp.where(z0 == 0, by_distance[i], by_distance[i ^ 1]) for i in range(samp)]
    swap1 = [jnp.where(z1 == 0, swap0[i], swap0[i ^ 2]) for i in range(samp)]
    return jnp.concatenate(swap1, axis=1).T


def solution(mesh):
    pix, samp = mesh.shape["pix"], mesh.shape["samp"]

    def local(stamps, start_panel):
        n = stamps.shape[0] * pix * samp
        k = start_panel.shape[1]
        if n <= SAMPLE_SPACE_LIMIT and (pix, samp) == (8, 4) and 4 * k == LANES:
            return sample_space(stamps, start_panel)
        return pixel_space(stamps, start_panel)

    return jax.shard_map(
        local,
        mesh=mesh,
        in_specs=(P(("samp", "pix"), None), P("pix", None)),
        out_specs=P("pix", None),
        check_vma=False,
    )
```

```python
import functools
import math

import jax
import jax.numpy as jnp
from jax import lax
from jax.experimental import pallas as pl
from jax.experimental.pallas import tpu as pltpu
from jax.sharding import PartitionSpec as P


ITERS = 10
LANES = 128
PANEL = 16
GROUP = 40
SAMPLE_SPACE_LIMIT = 4096
F32 = jnp.float32
BF16 = jnp.bfloat16

NN = (((1,), (0,)), ((), ()))
NT = (((1,), (1,)), ((), ()))
TN = (((0,), (0,)), ((), ()))


def orthonormal(back, gram):
    lower = jnp.linalg.cholesky(gram)
    return lax.linalg.triangular_solve(lower, back, left_side=False, lower=True, transpose_a=True)


def pixel_space(stamps, start_panel):
    block = lax.all_to_all(stamps, "pix", split_axis=1, concat_axis=0, tiled=True)

    def sweep(step, panel):
        partial_value = jnp.dot(block, panel.astype(BF16), preferred_element_type=F32)
        proj = lax.psum(partial_value.astype(BF16), "pix")
        back = lax.dot_general(block, proj, TN, preferred_element_type=F32)
        summed = lax.psum(back.astype(BF16), "samp").astype(F32)
        gram = lax.psum(jnp.dot(summed.T, summed, precision=lax.Precision.HIGHEST), "pix")
        return orthonormal(summed, gram)

    panel = lax.fori_loop(0, ITERS, sweep, start_panel)
    return panel * math.sqrt(start_panel.shape[0] * lax.axis_size("pix"))


def dot(a, b, dims):
    return lax.dot_general(a, b, dims, preferred_element_type=F32)


def split3(x):
    hi = x.astype(BF16)
    rest = x - hi.astype(F32)
    mid = rest.astype(BF16)
    lo = (rest - mid.astype(F32)).astype(BF16)
    return hi, mid, lo


def kernel_call(body, out_shape, in_specs=(), scratch_mib=8, **kw):
    single = not isinstance(out_shape, tuple)
    outs = tuple(pltpu.VMEM(o.shape, o.dtype) for o in ((out_shape,) if single else out_shape))
    call = pl.pallas_call(
        body,
        out_shape=outs[0] if single else outs,
        in_specs=in_specs,
        compiler_params=pltpu.CompilerParams(vmem_limit_bytes=scratch_mib << 20),
        **kw,
    )

    def place(x, spec):
        if spec.memory_space != pltpu.VMEM:
            return x
        return pltpu.with_memory_space_constraint(x, pltpu.VMEM)

    return lambda *args: call(*map(place, args, in_specs))


def vmem(n=1):
    return [pl.BlockSpec(memory_space=pltpu.VMEM)] * n


def smem():
    return pl.BlockSpec(memory_space=pltpu.SMEM)


def inverse_lower(gram):
    k = gram.shape[0]
    lane = lax.broadcasted_iota(jnp.int32, gram.shape, 1)
    row = lax.broadcasted_iota(jnp.int32, gram.shape, 0)
    m = jnp.where(lane < k, gram, jnp.where(lane == row + k, 1.0, 0.0))
    pivots = jnp.ones(gram.shape, F32)
    for start in range(0, k, PANEL):
        cols = [jnp.broadcast_to(m[:, j : j + 1], m.shape) for j in range(start, start + PANEL)]
        for t in range(PANEL):
            j = start + t
            pivot = cols[t][j : j + 1, :]
            factor = jnp.where(row > j, cols[t] * (1.0 / pivot), 0.0)
            pivots = jnp.where(row == j, pivot, pivots)
            for later in range(t + 1, PANEL):
                cols[later] = cols[later] - factor * cols[later][j : j + 1, :]
            m = m - factor * m[j : j + 1, :]
    return pltpu.roll(m * lax.rsqrt(pivots), LANES - k, 1)


def lane_sum3(x, k):
    return x + pltpu.roll(x, LANES - k, 1) + pltpu.roll(x, LANES - 2 * k, 1)


def gram_of(left, parts, zeros):
    k = left.shape[0]
    stack = jnp.concatenate(list(parts) + [zeros], axis=0)
    return lane_sum3(dot(left, stack, NT), k)


def apply_lower(inv, parts, zeros):
    k = inv.shape[0]
    lane = lax.broadcasted_iota(jnp.int32, inv.shape, 1)
    inv = jnp.where(lane < k, inv, 0.0)
    inv = inv + pltpu.roll(inv, k, 1)
    inv = inv + pltpu.roll(inv, 2 * k, 1)
    h1, h2, h3 = [h.astype(F32) for h in split3(inv)]
    first = jnp.where(lane < 3 * k, h1, h2)
    second = jnp.where(lane < k, h2, jnp.where(lane < 2 * k, h3, 0.0))
    left = jnp.concatenate([first, second], axis=1).astype(BF16)
    y1, y2, y3 = parts
    right = jnp.concatenate([y1, y2, y3, y1, y2, y1, zeros, zeros], axis=0)
    return dot(left, right, NN)


def rows_kernel(index_ref, near_ref, far_ref, stamps_ref, o_ref):
    m = near_ref.shape[1] * 2 // index_ref.shape[0]
    total = jnp.zeros(o_ref.shape, F32)
    for j in range(index_ref.shape[0]):
        ref = near_ref if j * m < near_ref.shape[1] else far_ref
        at = j * m % near_ref.shape[1]
        stamps = stamps_ref[:, pl.ds(pl.multiple_of(index_ref[j] * m, LANES), m)]
        total += dot(ref[:, at : at + m], stamps, NT)
    o_ref[...] = total.astype(BF16)


def basis_kernel(pix, samp, p0_ref, p_ref, q_ref):
    k, n = p0_ref.shape
    m = n // (pix * samp)
    per = LANES // m
    lane = lax.broadcasted_iota(jnp.int32, (k, LANES), 1)
    for to in range(n // LANES):
        block = jnp.zeros((k, LANES), F32)
        for j in range(per):
            p, s = divmod(to * per + j, samp)
            group, slot = divmod(s * pix + p, per)
            part = p0_ref[:, group * LANES : (group + 1) * LANES].astype(F32)
            part = pltpu.roll(part, (j - slot) * m % LANES, 1) if j != slot else part
            block = jnp.where(lane // m == j, part, block)
        p_ref[:, to * LANES : (to + 1) * LANES] = block.astype(BF16)
    p0 = p_ref[...]
    zeros = jnp.zeros_like(p0)
    gram = gram_of(p0, (p0, zeros, zeros), zeros)
    q_ref[...] = apply_lower(inverse_lower(gram), (p0, zeros, zeros), zeros)


def split_off(own_ref, other_ref, q_ref, left, right):
    k = q_ref.shape[0]
    q = q_ref[...]
    zeros = jnp.zeros(q.shape, BF16)
    q1, q2, q3 = split3(q)
    qs = jnp.concatenate([q1, q2, q3], axis=0)
    w = jnp.zeros(q.shape, F32)
    for ref in (own_ref, other_ref):
        t3 = dot(qs, ref[...], NN)
        ts = split3(t3[:k] + t3[k : 2 * k] + t3[2 * k :])
        w3 = dot(jnp.concatenate(ts, axis=0), ref[...], NT)
        w += w3[:k] + w3[k : 2 * k] + w3[2 * k :]
    ws = jnp.concatenate(list(split3(w)) + [zeros], axis=0)
    m = lane_sum3(dot(q1, ws, NT) + dot(q2, ws, NT) + dot(q3, ws, NT), k)
    w1, w2, w3 = split3(w - 0.5 * apply_lower(m, (q1, q2, q3), zeros))
    left[...] = jnp.concatenate([q1, w1, q1, w1, q1, w1, q2, w2, q2, w2, q3, w3], axis=0)
    right[...] = jnp.concatenate([w1, q1, w2, q2, w3, q3, w1, q1, w2, q2, w1, q1], axis=0)


def form_rows(k, first, own_ref, other_ref, left, right, out_ref, own_win, other_win, right_win):
    n = own_ref.shape[0]
    rows, width = out_ref.shape
    width -= LANES
    bs = width - n // 2
    nb = n // bs
    for b in range(own_win.shape[0] // bs):
        at = pl.multiple_of(lax.rem(first + b, nb) * bs, bs)
        own_win[b * bs : (b + 1) * bs, :] = own_ref[pl.ds(at, bs), :]
        other_win[b * bs : (b + 1) * bs, :] = other_ref[pl.ds(at, bs), :]
        right_win[:, b * bs : (b + 1) * bs] = right[:, pl.ds(at, bs)]
    eye = lax.broadcasted_iota(jnp.int32, (bs, bs), 0) == lax.broadcasted_iota(jnp.int32, (bs, bs), 1)
    for i in range(rows // bs):
        at = pl.multiple_of((first + i) * bs, bs)
        to, end = i * bs, i * bs + width
        s = dot(own_win[to : to + bs, :], own_win[to:end, :], NT)
        s += dot(other_win[to : to + bs, :], other_win[to:end, :], NT)
        s -= dot(left[:, pl.ds(at, bs)], right_win[:, to:end], TN)
        corner = s[:, :bs]
        diagonal = jnp.sum(jnp.where(eye, corner, 0.0), axis=0, keepdims=True)
        out_ref[to : to + bs, :bs] = jnp.where(eye, 0.0, corner).astype(BF16)
        out_ref[to : to + bs, bs:width] = s[:, bs:].astype(BF16)
        side = []
        for g, d in enumerate(split3(diagonal)):
            side.append(right_win[2 * g * k : (2 * g + 1) * k, to : to + bs].astype(F32))
            side.append(jnp.broadcast_to(d.astype(F32), (GROUP - k, bs)))
        side.append(jnp.zeros((LANES - 3 * GROUP, bs), F32))
        out_ref[to : to + bs, width:] = jnp.concatenate(side, axis=0).T.astype(BF16)


def form_kernel(at_ref, own_ref, other_ref, q_ref, out_ref, left, right, *wins):
    split_off(own_ref, other_ref, q_ref, left, right)
    form_rows(q_ref.shape[0], at_ref[0], own_ref, other_ref, left, right, out_ref, *wins)


def add_kernel(half_ref, a_ref, b_ref, o_ref):
    h = o_ref.shape[0]
    width = a_ref.shape[1] - LANES
    at = pl.multiple_of(half_ref[0] * h, h)
    a, b = a_ref[pl.ds(at, h), :], b_ref[pl.ds(at, h), :]
    o_ref[:, :width] = (a[:, :width].astype(F32) + b[:, :width].astype(F32)).astype(BF16)
    x = lane_sum3(a[:, width:].astype(F32), GROUP) + lane_sum3(b[:, width:].astype(F32), GROUP)
    lane = lax.broadcasted_iota(jnp.int32, x.shape, 1)
    h1, h2, h3 = [part.astype(F32) for part in split3(x)]
    packed = jnp.where(lane < 2 * GROUP, pltpu.roll(h2, GROUP, 1), pltpu.roll(h3, 2 * GROUP, 1))
    packed = jnp.where(lane < GROUP, h1, packed)
    o_ref[:, width:] = jnp.where(lane < 3 * GROUP, packed, 0.0).astype(BF16)


def add_shares(a, b, half=None):
    rows = a.shape[0] // (1 if half is None else 2)
    half = jnp.zeros((1,), jnp.int32) if half is None else half[None]
    return kernel_call(
        add_kernel,
        jax.ShapeDtypeStruct((rows, a.shape[1]), BF16),
        in_specs=[smem()] + vmem(2),
        out_specs=vmem()[0],
    )(half, a, b)


def iterate_kernel(index_ref, near_ref, far_ref, q_ref, p0_ref, p_ref, inv_ref, full, u, v, diag):
    k, n = q_ref.shape
    width = near_ref.shape[1] - LANES
    bs = width - n // 2
    nb = n // bs

    def unpack(share_ref, offset):
        def one(r, _):
            i = index_ref[r + offset]
            frm = pl.multiple_of(r * bs, bs)
            to = pl.multiple_of(i * bs, bs)
            for d in range(nb // 2 + 1):
                part = share_ref[pl.ds(frm, bs), d * bs : (d + 1) * bs]
                at = pl.multiple_of(lax.rem(i + d, nb) * bs, bs)
                full[pl.ds(to, bs), pl.ds(at, bs)] = part
                if 0 < d < nb // 2:
                    full[pl.ds(at, bs), pl.ds(to, bs)] = part.T
            side = share_ref[pl.ds(frm, bs), width:].astype(F32).T
            side = side[:GROUP] + side[GROUP : 2 * GROUP] + side[2 * GROUP : 3 * GROUP]
            w = side[:k]
            diag[:, pl.ds(to, bs)] = side[k : k + 8]
            q = q_ref[:, pl.ds(to, bs)]
            us = split3(jnp.concatenate([w, q], axis=0))
            v1, v2, v3 = split3(jnp.concatenate([q, w], axis=0))
            u[:, pl.ds(to, bs)] = jnp.concatenate(list(us) + [jnp.zeros((2 * k, bs), BF16)], axis=0)
            v[:, pl.ds(to, bs)] = jnp.concatenate([v1, v2, v3, v1, v2, v1], axis=0)
            return 0

        lax.fori_loop(0, nb // 2, one, 0)

    unpack(near_ref, 0)
    unpack(far_ref, nb // 2)

    zeros = jnp.zeros((k, n), BF16)
    lane = lax.broadcasted_iota(jnp.int32, (k, LANES), 1)

    def product(p):
        t = dot(p, u[...], NT)
        t = t[:, :LANES] + t[:, LANES:]
        t = t + pltpu.roll(t, 2 * k, 1)
        h1, h2, h3 = [h.astype(F32) for h in split3(t)]
        low = lane < 2 * k
        ts = jnp.concatenate([h1, jnp.where(low, h1, h2), jnp.where(low, h2, h3)], axis=1).astype(BF16)
        y = dot(p, full[...], NN) + dot(ts, v[...], NN) + p.astype(F32) * diag[0:1, :]
        return split3(y)

    def sweep(step, p):
        parts = product(p)
        inv = inverse_lower(gram_of(p, parts, zeros))
        return apply_lower(inv, parts, zeros).astype(BF16)

    p = lax.fori_loop(0, ITERS - 1, sweep, p0_ref[...])
    p_ref[...] = p
    inv_ref[...] = inverse_lower(gram_of(p, product(p), zeros))


def finish_kernel(scale, p_ref, inv_ref, block_ref, o_ref):
    back = dot(p_ref[...], block_ref[...], NN)
    zeros = jnp.zeros(back.shape, BF16)
    o_ref[...] = (apply_lower(inv_ref[...], split3(back), zeros) * scale).astype(BF16)


def flip(x, axes, perm):
    return lax.ppermute(x, axes, perm)


def ordered(own, recv, bit, axis=0):
    return jnp.where(
        bit == 0,
        jnp.concatenate([own, recv], axis=axis),
        jnp.concatenate([recv, own], axis=axis),
    )


def sample_space(stamps, start_panel):
    pix = lax.axis_size("pix")
    samp = lax.axis_size("samp")
    n = stamps.shape[0] * pix * samp
    k = start_panel.shape[1]
    scale = math.sqrt(start_panel.shape[0] * pix)
    p = lax.axis_index("pix")
    s = lax.axis_index("samp")
    xor_pix = lambda b: [(i, i ^ b) for i in range(pix)]
    xor_samp = lambda b: [(i, i ^ b) for i in range(samp)]

    core = p & 1
    x, y = (p >> 1) & 1, (p >> 2) & 1
    z0, z1 = s & 1, (s >> 1) & 1

    low = start_panel.astype(BF16).T
    for b in (2, 4):
        low = jnp.concatenate([low, flip(low, "pix", xor_pix(b))], axis=1)
    far = flip(low, "pix", xor_pix(1))
    at = jnp.arange(pix, dtype=jnp.int32)
    index = p ^ (((at & 1) << 1) | ((at & 2) << 1) | (at >> 2))

    block = lax.all_to_all(stamps, ("pix", "samp"), split_axis=1, concat_axis=0, tiled=True)

    proj = kernel_call(
        rows_kernel,
        jax.ShapeDtypeStruct((k, stamps.shape[0]), BF16),
        in_specs=[smem()] + vmem(3),
        out_specs=vmem()[0],
    )(index, low, far, stamps)
    for b in (1, 2, 4):
        proj = ordered(proj, flip(proj, "pix", xor_pix(b)), p & b, axis=1)
    for b in (1, 2):
        proj = ordered(proj, flip(proj, "samp", xor_samp(b)), s & b, axis=1)
    proj, q = kernel_call(
        functools.partial(basis_kernel, pix, samp),
        (jax.ShapeDtypeStruct((k, n), BF16), jax.ShapeDtypeStruct((k, n), F32)),
        in_specs=vmem(),
        out_specs=tuple(vmem(2)),
    )(proj)

    first = [(i, i ^ (2 if i % 2 == 0 else 4)) for i in range(pix)]
    second = [(i, i ^ (4 if i % 2 == 0 else 2)) for i in range(pix)]
    bit_a = jnp.where(core == 0, x, y)
    bit_b = jnp.where(core == 0, y, x)

    other = flip(block, "pix", xor_pix(1))
    bs = 2 * stamps.shape[0]
    nb = n // bs
    px = block.shape[1]
    width = n // 2 + bs
    rows = n // 4
    window = rows - bs + width
    piece = jax.ShapeDtypeStruct((rows, width + LANES), BF16)
    form = kernel_call(
        form_kernel,
        piece,
        in_specs=[smem()] + vmem(3),
        out_specs=vmem()[0],
        scratch_mib=20,
        scratch_shapes=[
            pltpu.VMEM((12 * k, n), BF16),
            pltpu.VMEM((12 * k, n), BF16),
            pltpu.VMEM((window, px), BF16),
            pltpu.VMEM((window, px), BF16),
            pltpu.VMEM((12 * k, window), BF16),
        ],
    )
    blocks = rows // bs
    at = core * 2 * blocks
    send = form((at + (1 - bit_a) * blocks)[None], block, other, q)
    recv = flip(send, "pix", first)
    keep = form((at + bit_a * blocks)[None], block, other, q)
    for axis, perm, bit in (
        ("pix", second, bit_b),
        ("samp", xor_samp(1), z0),
        ("samp", xor_samp(2), z1),
    ):
        send = add_shares(keep, recv, 1 - bit)
        keep = add_shares(keep, recv, bit)
        recv = flip(send, axis, perm)
    share = add_shares(keep, recv)

    share = ordered(share, flip(share, "samp", xor_samp(2)), z1)
    for axis, perm in (("samp", xor_samp(1)), ("pix", second), ("pix", first)):
        share = jnp.concatenate([share, flip(share, axis, perm)], axis=0)
    far = flip(share, "pix", xor_pix(1))
    at = jnp.arange(nb, dtype=jnp.int32)
    c_of = core ^ ((at >> 3) & 1)
    a_of = jnp.where(c_of == 0, x, y) ^ ((at >> 2) & 1)
    b_of = jnp.where(c_of == 0, y, x) ^ ((at >> 1) & 1)
    index = c_of * 8 + a_of * 4 + b_of * 2 + (z0 ^ (at & 1))

    proj, inv = kernel_call(
        iterate_kernel,
        (jax.ShapeDtypeStruct((k, n), BF16), jax.ShapeDtypeStruct((k, LANES), F32)),
        in_specs=[smem()] + vmem(4),
        out_specs=tuple(vmem(2)),
        scratch_mib=24,
        scratch_shapes=[
            pltpu.VMEM((n, n), BF16),
            pltpu.VMEM((8 * k, n), BF16),
            pltpu.VMEM((12 * k, n), BF16),
            pltpu.VMEM((8, n), F32),
        ],
    )(index, share, far, q, proj)

    mine = kernel_call(
        functools.partial(finish_kernel, scale),
        jax.ShapeDtypeStruct((k, px), BF16),
        in_specs=vmem(3),
        out_specs=vmem()[0],
    )(proj, inv, block)
    for b in (2, 1):
        mine = jnp.concatenate([mine, flip(mine, "samp", xor_samp(b))], axis=1)
    parts = [mine[:, i * px : (i + 1) * px] for i in range(samp)]
    by_distance = {0: parts[0], 2: parts[1], 1: parts[2], 3: parts[3]}
    swap0 = [jnp.where(z0 == 0, by_distance[i], by_distance[i ^ 1]) for i in range(samp)]
    swap1 = [jnp.where(z1 == 0, swap0[i], swap0[i ^ 2]) for i in range(samp)]
    return jnp.concatenate(swap1, axis=1).astype(F32).T


def solution(mesh):
    pix, samp = mesh.shape["pix"], mesh.shape["samp"]

    def local(stamps, start_panel):
        n = stamps.shape[0] * pix * samp
        k = start_panel.shape[1]
        if n <= SAMPLE_SPACE_LIMIT and (pix, samp) == (8, 4) and 4 * k == LANES:
            return sample_space(stamps, start_panel)
        return pixel_space(stamps, start_panel)

    return jax.shard_map(
        local,
        mesh=mesh,
        in_specs=(P(("samp", "pix"), None), P("pix", None)),
        out_specs=P("pix", None),
        check_vma=False,
    )
```

```python
import functools
import math

import jax
import jax.numpy as jnp
from jax import lax
from jax.experimental import pallas as pl
from jax.experimental.pallas import tpu as pltpu
from jax.sharding import PartitionSpec as P


ITERS = 10
LANES = 128
PANEL = 16
GROUP = 40
STEP = 2
SAMPLE_SPACE_LIMIT = 4096
F32 = jnp.float32
BF16 = jnp.bfloat16

NN = (((1,), (0,)), ((), ()))
NT = (((1,), (1,)), ((), ()))
TN = (((0,), (0,)), ((), ()))


def orthonormal(back, gram):
    lower = jnp.linalg.cholesky(gram)
    return lax.linalg.triangular_solve(lower, back, left_side=False, lower=True, transpose_a=True)


def pixel_space(stamps, start_panel):
    block = lax.all_to_all(stamps, "pix", split_axis=1, concat_axis=0, tiled=True)

    def sweep(step, panel):
        partial_value = jnp.dot(block, panel.astype(BF16), preferred_element_type=F32)
        proj = lax.psum(partial_value.astype(BF16), "pix")
        back = lax.dot_general(block, proj, TN, preferred_element_type=F32)
        summed = lax.psum(back.astype(BF16), "samp").astype(F32)
        gram = lax.psum(jnp.dot(summed.T, summed, precision=lax.Precision.HIGHEST), "pix")
        return orthonormal(summed, gram)

    panel = lax.fori_loop(0, ITERS, sweep, start_panel)
    return panel * math.sqrt(start_panel.shape[0] * lax.axis_size("pix"))


def dot(a, b, dims):
    return lax.dot_general(a, b, dims, preferred_element_type=F32)


def split3(x):
    hi = x.astype(BF16)
    rest = x - hi.astype(F32)
    mid = rest.astype(BF16)
    lo = (rest - mid.astype(F32)).astype(BF16)
    return hi, mid, lo


def kernel_call(body, out_shape, in_specs=(), scratch_mib=8, **kw):
    single = not isinstance(out_shape, tuple)
    outs = tuple(pltpu.VMEM(o.shape, o.dtype) for o in ((out_shape,) if single else out_shape))
    call = pl.pallas_call(
        body,
        out_shape=outs[0] if single else outs,
        in_specs=in_specs,
        compiler_params=pltpu.CompilerParams(vmem_limit_bytes=scratch_mib << 20),
        **kw,
    )

    def place(x, spec):
        if spec.memory_space != pltpu.VMEM:
            return x
        return pltpu.with_memory_space_constraint(x, pltpu.VMEM)

    return lambda *args: call(*map(place, args, in_specs))


def vmem(n=1):
    return [pl.BlockSpec(memory_space=pltpu.VMEM)] * n


def smem():
    return pl.BlockSpec(memory_space=pltpu.SMEM)


def inverse_lower(gram):
    k = gram.shape[0]
    lane = lax.broadcasted_iota(jnp.int32, gram.shape, 1)
    row = lax.broadcasted_iota(jnp.int32, gram.shape, 0)
    m = jnp.where(lane < k, gram, jnp.where(lane % k == row, 1.0, 0.0))
    pivots = jnp.ones(gram.shape, F32)
    for start in range(0, k, PANEL):
        cols = [jnp.broadcast_to(m[:, j : j + 1], m.shape) for j in range(start, start + PANEL)]
        for t in range(PANEL):
            j = start + t
            pivot = cols[t][j : j + 1, :]
            factor = jnp.where(row > j, cols[t] * (1.0 / pivot), 0.0)
            pivots = jnp.where(row == j, pivot, pivots)
            for later in range(t + 1, PANEL):
                cols[later] = cols[later] - factor * cols[later][j : j + 1, :]
            m = m - factor * m[j : j + 1, :]
    return m * lax.rsqrt(pivots)


def lane_sum3(x, k):
    return x + pltpu.roll(x, LANES - k, 1) + pltpu.roll(x, LANES - 2 * k, 1)


def gram_of(parts, right):
    k = right.shape[0]
    wide = jnp.concatenate([right, jnp.zeros((3 * k, right.shape[1]), right.dtype)], axis=0)
    g = dot(jnp.concatenate(parts, axis=0), wide, NT)
    return g[:k] + g[k : 2 * k] + g[2 * k :]


def apply_lower(inv, parts):
    k = inv.shape[0]
    lane = lax.broadcasted_iota(jnp.int32, inv.shape, 1)
    h1, h2, h3 = [h.astype(F32) for h in split3(inv)]
    first = jnp.where(lane < k, 0.0, h1)
    second = jnp.where(lane < k, 0.0, jnp.where(lane < 3 * k, h2, h3))
    left = jnp.concatenate([first, second], axis=1).astype(BF16)
    y1, y2, y3 = parts
    zeros = jnp.zeros_like(y1)
    return dot(left, jnp.concatenate([zeros, y1, y2, y3, zeros, y1, y2, y1], axis=0), NN)


def rows_kernel(index_ref, near_ref, far_ref, stamps_ref, o_ref):
    m = near_ref.shape[1] * 2 // index_ref.shape[0]
    total = jnp.zeros(o_ref.shape, F32)
    for j in range(index_ref.shape[0]):
        ref = near_ref if j * m < near_ref.shape[1] else far_ref
        at = j * m % near_ref.shape[1]
        stamps = stamps_ref[:, pl.ds(pl.multiple_of(index_ref[j] * m, LANES), m)]
        total += dot(ref[:, at : at + m], stamps, NT)
    o_ref[...] = total.astype(BF16)


def basis_kernel(pix, samp, p0_ref, p_ref, q_ref):
    k, n = p0_ref.shape
    m = n // (pix * samp)
    per = LANES // m
    lane = lax.broadcasted_iota(jnp.int32, (k, LANES), 1)
    for to in range(n // LANES):
        block = jnp.zeros((k, LANES), F32)
        for j in range(per):
            p, s = divmod(to * per + j, samp)
            group, slot = divmod(s * pix + p, per)
            part = p0_ref[:, group * LANES : (group + 1) * LANES].astype(F32)
            part = pltpu.roll(part, (j - slot) * m % LANES, 1) if j != slot else part
            block = jnp.where(lane // m == j, part, block)
        p_ref[:, to * LANES : (to + 1) * LANES] = block.astype(BF16)
    p0 = p_ref[...]
    parts = (p0, jnp.zeros_like(p0), jnp.zeros_like(p0))
    q_ref[...] = apply_lower(inverse_lower(gram_of(parts, p0)), parts)


def split_off(own_ref, other_ref, q_ref, left, right):
    k = q_ref.shape[0]
    q = q_ref[...]
    zeros = jnp.zeros(q.shape, BF16)
    q1, q2, q3 = split3(q)
    qs = jnp.concatenate([q1, q2, q3], axis=0)
    w = jnp.zeros(q.shape, F32)
    for ref in (own_ref, other_ref):
        t3 = dot(qs, ref[...], NN)
        ts = split3(t3[:k] + t3[k : 2 * k] + t3[2 * k :])
        w3 = dot(jnp.concatenate(ts, axis=0), ref[...], NT)
        w += w3[:k] + w3[k : 2 * k] + w3[2 * k :]
    ws = jnp.concatenate(list(split3(w)) + [zeros], axis=0)
    m = lane_sum3(dot(q1, ws, NT) + dot(q2, ws, NT) + dot(q3, ws, NT), k)
    m = jnp.where(lax.broadcasted_iota(jnp.int32, m.shape, 1) < k, m, 0.0)
    m = pltpu.roll(m, k, 1) + pltpu.roll(m, 2 * k, 1) + pltpu.roll(m, 3 * k, 1)
    w1, w2, w3 = split3(w - 0.5 * apply_lower(m, (q1, q2, q3)))
    left[...] = jnp.concatenate([q1, w1, q1, w1, q1, w1, q2, w2, q2, w2, q3, w3], axis=0)
    right[...] = jnp.concatenate([w1, q1, w2, q2, w3, q3, w1, q1, w2, q2, w1, q1], axis=0)


def form_rows(k, first, own_ref, other_ref, left, right, out_ref, window, right_win):
    n, px = own_ref.shape
    rows, width = out_ref.shape
    width -= LANES
    bs = width - n // 2
    nb = n // bs
    for b in range(window.shape[0] // bs):
        at = pl.multiple_of(lax.rem(first + b, nb) * bs, bs)
        window[b * bs : (b + 1) * bs, :px] = own_ref[pl.ds(at, bs), :]
        window[b * bs : (b + 1) * bs, px:] = other_ref[pl.ds(at, bs), :]
        right_win[:, b * bs : (b + 1) * bs] = right[:, pl.ds(at, bs)]
    eye = lax.broadcasted_iota(jnp.int32, (bs, bs), 0) == lax.broadcasted_iota(jnp.int32, (bs, bs), 1)
    step = STEP * bs
    for i in range(rows // bs):
        if i % STEP == 0:
            at = pl.multiple_of((first + i) * bs, bs)
            lo, end = i * bs, i * bs + step - bs + width
            wide = dot(window[lo : lo + step, :], window[lo:end, :], NT)
            wide -= dot(left[:, pl.ds(at, step)], right_win[:, lo:end], TN)
        off = i % STEP * bs
        to = i * bs
        s = wide[off : off + bs, off : off + width]
        corner = s[:, :bs]
        diagonal = jnp.sum(jnp.where(eye, corner, 0.0), axis=0, keepdims=True)
        out_ref[to : to + bs, :bs] = jnp.where(eye, 0.0, corner).astype(BF16)
        out_ref[to : to + bs, bs:width] = s[:, bs:].astype(BF16)
        side = []
        for g, d in enumerate(split3(diagonal)):
            side.append(right_win[2 * g * k : (2 * g + 1) * k, to : to + bs].astype(F32))
            side.append(jnp.broadcast_to(d.astype(F32), (GROUP - k, bs)))
        side.append(jnp.zeros((LANES - 3 * GROUP, bs), F32))
        out_ref[to : to + bs, width:] = jnp.concatenate(side, axis=0).T.astype(BF16)


def form_kernel(at_ref, own_ref, other_ref, q_ref, out_ref, left, right, *wins):
    split_off(own_ref, other_ref, q_ref, left, right)
    form_rows(q_ref.shape[0], at_ref[0], own_ref, other_ref, left, right, out_ref, *wins)


def add_kernel(at_ref, a_ref, b_ref, *o_refs):
    width = a_ref.shape[1] - LANES
    for i, o_ref in enumerate(o_refs):
        h = o_ref.shape[0]
        at = pl.multiple_of(at_ref[i] * h, h)
        a, b = a_ref[pl.ds(at, h), :], b_ref[pl.ds(at, h), :]
        o_ref[:, :width] = (a[:, :width].astype(F32) + b[:, :width].astype(F32)).astype(BF16)
        x = lane_sum3(a[:, width:].astype(F32), GROUP) + lane_sum3(b[:, width:].astype(F32), GROUP)
        lane = lax.broadcasted_iota(jnp.int32, x.shape, 1)
        h1, h2, h3 = [part.astype(F32) for part in split3(x)]
        packed = jnp.where(lane < 2 * GROUP, pltpu.roll(h2, GROUP, 1), pltpu.roll(h3, 2 * GROUP, 1))
        packed = jnp.where(lane < GROUP, h1, packed)
        o_ref[:, width:] = jnp.where(lane < 3 * GROUP, packed, 0.0).astype(BF16)


def add_shares(a, b, pieces, of=2):
    shape = jax.ShapeDtypeStruct((a.shape[0] // of, a.shape[1]), BF16)
    return kernel_call(
        add_kernel,
        (shape,) * len(pieces),
        in_specs=[smem()] + vmem(2),
        out_specs=tuple(vmem(len(pieces))),
    )(jnp.stack(pieces).astype(jnp.int32), a, b)


def iterate_kernel(index_ref, near_ref, far_ref, q_ref, p0_ref, p_ref, inv_ref, full, u, v, diag):
    k, n = q_ref.shape
    width = near_ref.shape[1] - LANES
    bs = width - n // 2
    nb = n // bs

    def unpack(share_ref, offset):
        def one(r, _):
            i = index_ref[r + offset]
            frm = pl.multiple_of(r * bs, bs)
            to = pl.multiple_of(i * bs, bs)
            for d in range(nb // 2 + 1):
                part = share_ref[pl.ds(frm, bs), d * bs : (d + 1) * bs]
                at = pl.multiple_of(lax.rem(i + d, nb) * bs, bs)
                full[pl.ds(to, bs), pl.ds(at, bs)] = part
                if 0 < d < nb // 2:
                    full[pl.ds(at, bs), pl.ds(to, bs)] = part.T
            side = share_ref[pl.ds(frm, bs), width:].astype(F32).T
            side = side[:GROUP] + side[GROUP : 2 * GROUP] + side[2 * GROUP : 3 * GROUP]
            w = side[:k]
            diag[:, pl.ds(to, bs)] = side[k : k + 8]
            q = q_ref[:, pl.ds(to, bs)]
            us = [part.astype(F32) for part in split3(jnp.concatenate([w, q], axis=0))]
            v1, v2, v3 = split3(jnp.concatenate([q, w], axis=0))
            u[pl.ds(to, bs), :LANES] = jnp.concatenate(us[:2], axis=0).T.astype(BF16)
            tail = jnp.concatenate([us[2], jnp.zeros((2 * k, bs), F32)], axis=0)
            u[pl.ds(to, bs), LANES:] = tail.T.astype(BF16)
            v[:, pl.ds(to, bs)] = jnp.concatenate([v1, v2, v3, v1, v2, v1], axis=0)
            return 0

        lax.fori_loop(0, nb // 2, one, 0)

    unpack(near_ref, 0)
    unpack(far_ref, nb // 2)

    lane = lax.broadcasted_iota(jnp.int32, (k, LANES), 1)

    def product(p):
        t = dot(p, u[...], NN)
        t = t[:, :LANES] + t[:, LANES:]
        t = t + pltpu.roll(t, 2 * k, 1)
        h1, h2, h3 = [h.astype(F32) for h in split3(t)]
        low = lane < 2 * k
        ts = jnp.concatenate([h1, jnp.where(low, h1, h2), jnp.where(low, h2, h3)], axis=1).astype(BF16)
        y = dot(p, full[...], NN) + dot(ts, v[...], NN) + p.astype(F32) * diag[0:1, :]
        return split3(y)

    def sweep(step, p):
        parts = product(p)
        return apply_lower(inverse_lower(gram_of(parts, p)), parts).astype(BF16)

    p = lax.fori_loop(0, ITERS - 1, sweep, p0_ref[...])
    p_ref[...] = p
    inv_ref[...] = inverse_lower(gram_of(product(p), p))


def finish_kernel(scale, p_ref, inv_ref, block_ref, o_ref):
    back = dot(p_ref[...], block_ref[...], NN)
    o_ref[...] = (apply_lower(inv_ref[...], split3(back)) * scale).astype(BF16)


def flip(x, axes, perm):
    return lax.ppermute(x, axes, perm)


def ordered(own, recv, bit, axis=0):
    return jnp.where(
        bit == 0,
        jnp.concatenate([own, recv], axis=axis),
        jnp.concatenate([recv, own], axis=axis),
    )


def sample_space(stamps, start_panel):
    pix = lax.axis_size("pix")
    samp = lax.axis_size("samp")
    n = stamps.shape[0] * pix * samp
    k = start_panel.shape[1]
    scale = math.sqrt(start_panel.shape[0] * pix)
    p = lax.axis_index("pix")
    s = lax.axis_index("samp")
    xor_pix = lambda b: [(i, i ^ b) for i in range(pix)]
    xor_samp = lambda b: [(i, i ^ b) for i in range(samp)]

    core = p & 1
    x, y = (p >> 1) & 1, (p >> 2) & 1
    z0, z1 = s & 1, (s >> 1) & 1

    low = start_panel.astype(BF16).T
    for b in (2, 4):
        low = jnp.concatenate([low, flip(low, "pix", xor_pix(b))], axis=1)
    far = flip(low, "pix", xor_pix(1))
    at = jnp.arange(pix, dtype=jnp.int32)
    index = p ^ (((at & 1) << 1) | ((at & 2) << 1) | (at >> 2))

    block = lax.all_to_all(stamps, ("pix", "samp"), split_axis=1, concat_axis=0, tiled=True)

    proj = kernel_call(
        rows_kernel,
        jax.ShapeDtypeStruct((k, stamps.shape[0]), BF16),
        in_specs=[smem()] + vmem(3),
        out_specs=vmem()[0],
    )(index, low, far, stamps)
    for b in (1, 2, 4):
        proj = ordered(proj, flip(proj, "pix", xor_pix(b)), p & b, axis=1)
    for b in (1, 2):
        proj = ordered(proj, flip(proj, "samp", xor_samp(b)), s & b, axis=1)
    proj, q = kernel_call(
        functools.partial(basis_kernel, pix, samp),
        (jax.ShapeDtypeStruct((k, n), BF16), jax.ShapeDtypeStruct((k, n), F32)),
        in_specs=vmem(),
        out_specs=tuple(vmem(2)),
    )(proj)

    first = [(i, i ^ (2 if i % 2 == 0 else 4)) for i in range(pix)]
    second = [(i, i ^ (4 if i % 2 == 0 else 2)) for i in range(pix)]
    bit_a = jnp.where(core == 0, x, y)
    bit_b = jnp.where(core == 0, y, x)

    other = flip(block, "pix", xor_pix(1))
    bs = 2 * stamps.shape[0]
    nb = n // bs
    px = block.shape[1]
    width = n // 2 + bs
    rows = n // 4
    window = rows - bs + width
    piece = jax.ShapeDtypeStruct((rows, width + LANES), BF16)
    form = kernel_call(
        form_kernel,
        piece,
        in_specs=[smem()] + vmem(3),
        out_specs=vmem()[0],
        scratch_mib=20,
        scratch_shapes=[
            pltpu.VMEM((12 * k, n), BF16),
            pltpu.VMEM((12 * k, n), BF16),
            pltpu.VMEM((window, 2 * px), BF16),
            pltpu.VMEM((12 * k, window), BF16),
        ],
    )
    blocks = rows // bs
    at = core * 2 * blocks
    send = form((at + (1 - bit_a) * blocks)[None], block, other, q)
    recv = flip(send, "pix", first)
    keep = form((at + bit_a * blocks)[None], block, other, q)
    (send,) = add_shares(keep, recv, [1 - bit_b])
    (keep,) = add_shares(keep, recv, [bit_b])
    recv = flip(send, "pix", second)
    for b, bit in ((1, z0), (2, z1)):
        send, keep = add_shares(keep, recv, [1 - bit, bit])
        recv = flip(send, "samp", xor_samp(b))
    (share,) = add_shares(keep, recv, [jnp.int32(0)], of=1)

    share = ordered(share, flip(share, "samp", xor_samp(2)), z1)
    for axis, perm in (("samp", xor_samp(1)), ("pix", second), ("pix", first)):
        share = jnp.concatenate([share, flip(share, axis, perm)], axis=0)
    far = flip(share, "pix", xor_pix(1))
    at = jnp.arange(nb, dtype=jnp.int32)
    c_of = core ^ ((at >> 3) & 1)
    a_of = jnp.where(c_of == 0, x, y) ^ ((at >> 2) & 1)
    b_of = jnp.where(c_of == 0, y, x) ^ ((at >> 1) & 1)
    index = c_of * 8 + a_of * 4 + b_of * 2 + (z0 ^ (at & 1))

    proj, inv = kernel_call(
        iterate_kernel,
        (jax.ShapeDtypeStruct((k, n), BF16), jax.ShapeDtypeStruct((k, LANES), F32)),
        in_specs=[smem()] + vmem(4),
        out_specs=tuple(vmem(2)),
        scratch_mib=24,
        scratch_shapes=[
            pltpu.VMEM((n, n), BF16),
            pltpu.VMEM((n, 8 * k), BF16),
            pltpu.VMEM((12 * k, n), BF16),
            pltpu.VMEM((8, n), F32),
        ],
    )(index, share, far, q, proj)

    mine = kernel_call(
        functools.partial(finish_kernel, scale),
        jax.ShapeDtypeStruct((k, px), BF16),
        in_specs=vmem(3),
        out_specs=vmem()[0],
    )(proj, inv, block)
    for b in (2, 1):
        mine = jnp.concatenate([mine, flip(mine, "samp", xor_samp(b))], axis=1)
    parts = [mine[:, i * px : (i + 1) * px] for i in range(samp)]
    by_distance = {0: parts[0], 2: parts[1], 1: parts[2], 3: parts[3]}
    swap0 = [jnp.where(z0 == 0, by_distance[i], by_distance[i ^ 1]) for i in range(samp)]
    swap1 = [jnp.where(z1 == 0, swap0[i], swap0[i ^ 2]) for i in range(samp)]
    return jnp.concatenate(swap1, axis=1).astype(F32).T


def solution(mesh):
    pix, samp = mesh.shape["pix"], mesh.shape["samp"]

    def local(stamps, start_panel):
        n = stamps.shape[0] * pix * samp
        k = start_panel.shape[1]
        if n <= SAMPLE_SPACE_LIMIT and (pix, samp) == (8, 4) and 4 * k == LANES:
            return sample_space(stamps, start_panel)
        return pixel_space(stamps, start_panel)

    return jax.shard_map(
        local,
        mesh=mesh,
        in_specs=(P(("samp", "pix"), None), P("pix", None)),
        out_specs=P("pix", None),
        check_vma=False,
    )
```

```python
import functools
import math

import jax
import jax.numpy as jnp
from jax import lax
from jax.experimental import pallas as pl
from jax.experimental.pallas import tpu as pltpu
from jax.sharding import PartitionSpec as P


ITERS = 10
LANES = 128
PANEL = 16
GROUP = 40
STEP = 2
SEND, KEEP, PLACE, BLOCKS = 0, 1, 8, 16
SAMPLE_SPACE_LIMIT = 4096
F32 = jnp.float32
BF16 = jnp.bfloat16

NN = (((1,), (0,)), ((), ()))
NT = (((1,), (1,)), ((), ()))
TN = (((0,), (0,)), ((), ()))


def orthonormal(back, gram):
    lower = jnp.linalg.cholesky(gram)
    return lax.linalg.triangular_solve(lower, back, left_side=False, lower=True, transpose_a=True)


def pixel_space(stamps, start_panel):
    block = lax.all_to_all(stamps, "pix", split_axis=1, concat_axis=0, tiled=True)

    def sweep(step, panel):
        partial_value = jnp.dot(block, panel.astype(BF16), preferred_element_type=F32)
        proj = lax.psum(partial_value.astype(BF16), "pix")
        back = lax.dot_general(block, proj, TN, preferred_element_type=F32)
        summed = lax.psum(back.astype(BF16), "samp").astype(F32)
        gram = lax.psum(jnp.dot(summed.T, summed, precision=lax.Precision.HIGHEST), "pix")
        return orthonormal(summed, gram)

    panel = lax.fori_loop(0, ITERS, sweep, start_panel)
    return panel * math.sqrt(start_panel.shape[0] * lax.axis_size("pix"))


def dot(a, b, dims):
    return lax.dot_general(a, b, dims, preferred_element_type=F32)


def split3(x):
    hi = x.astype(BF16)
    rest = x - hi.astype(F32)
    mid = rest.astype(BF16)
    lo = (rest - mid.astype(F32)).astype(BF16)
    return hi, mid, lo


def kernel_call(body, out_shape, in_specs=(), scratch_mib=8, **kw):
    single = not isinstance(out_shape, tuple)
    outs = tuple(pltpu.VMEM(o.shape, o.dtype) for o in ((out_shape,) if single else out_shape))
    call = pl.pallas_call(
        body,
        out_shape=outs[0] if single else outs,
        in_specs=in_specs,
        compiler_params=pltpu.CompilerParams(vmem_limit_bytes=scratch_mib << 20),
        **kw,
    )

    def place(x, spec):
        if spec.memory_space != pltpu.VMEM:
            return x
        return pltpu.with_memory_space_constraint(x, pltpu.VMEM)

    return lambda *args: call(*map(place, args, in_specs))


def vmem(n=1):
    return [pl.BlockSpec(memory_space=pltpu.VMEM)] * n


def smem():
    return pl.BlockSpec(memory_space=pltpu.SMEM)


def inverse_lower(gram):
    k = gram.shape[0]
    lane = lax.broadcasted_iota(jnp.int32, gram.shape, 1)
    row = lax.broadcasted_iota(jnp.int32, gram.shape, 0)
    m = jnp.where(lane < k, gram, jnp.where(lane % k == row, 1.0, 0.0))
    pivots = jnp.ones(gram.shape, F32)
    for start in range(0, k, PANEL):
        cols = [jnp.broadcast_to(m[:, j : j + 1], m.shape) for j in range(start, start + PANEL)]
        for t in range(PANEL):
            j = start + t
            pivot = cols[t][j : j + 1, :]
            factor = jnp.where(row > j, cols[t] * (1.0 / pivot), 0.0)
            pivots = jnp.where(row == j, pivot, pivots)
            for later in range(t + 1, PANEL):
                cols[later] = cols[later] - factor * cols[later][j : j + 1, :]
            m = m - factor * m[j : j + 1, :]
    return m * lax.rsqrt(pivots)


def lane_sum3(x, k):
    return x + pltpu.roll(x, LANES - k, 1) + pltpu.roll(x, LANES - 2 * k, 1)


def gram_of(parts, right):
    k = right.shape[0]
    wide = jnp.concatenate([right, jnp.zeros((3 * k, right.shape[1]), right.dtype)], axis=0)
    g = dot(jnp.concatenate(parts, axis=0), wide, NT)
    return g[:k] + g[k : 2 * k] + g[2 * k :]


def apply_lower(inv, parts):
    k = inv.shape[0]
    lane = lax.broadcasted_iota(jnp.int32, inv.shape, 1)
    h1, h2, h3 = [h.astype(F32) for h in split3(inv)]
    first = jnp.where(lane < k, 0.0, h1)
    second = jnp.where(lane < k, 0.0, jnp.where(lane < 3 * k, h2, h3))
    left = jnp.concatenate([first, second], axis=1).astype(BF16)
    y1, y2, y3 = parts
    zeros = jnp.zeros_like(y1)
    return dot(left, jnp.concatenate([zeros, y1, y2, y3, zeros, y1, y2, y1], axis=0), NN)


def rows_kernel(index_ref, near_ref, far_ref, stamps_ref, o_ref):
    total = jnp.zeros(o_ref.shape, F32)
    pix = BLOCKS - PLACE
    m = near_ref.shape[1] * 2 // pix
    for j in range(pix):
        ref = near_ref if j * m < near_ref.shape[1] else far_ref
        at = j * m % near_ref.shape[1]
        stamps = stamps_ref[:, pl.ds(pl.multiple_of(index_ref[PLACE + j] * m, LANES), m)]
        total += dot(ref[:, at : at + m], stamps, NT)
    o_ref[...] = total.astype(BF16)


def basis_kernel(pix, samp, p0_ref, p_ref, q_ref):
    k, n = p0_ref.shape
    m = n // (pix * samp)
    per = LANES // m
    lane = lax.broadcasted_iota(jnp.int32, (k, LANES), 1)
    for to in range(n // LANES):
        block = jnp.zeros((k, LANES), F32)
        for j in range(per):
            p, s = divmod(to * per + j, samp)
            group, slot = divmod(s * pix + p, per)
            part = p0_ref[:, group * LANES : (group + 1) * LANES].astype(F32)
            part = pltpu.roll(part, (j - slot) * m % LANES, 1) if j != slot else part
            block = jnp.where(lane // m == j, part, block)
        p_ref[:, to * LANES : (to + 1) * LANES] = block.astype(BF16)
    p0 = p_ref[...]
    parts = (p0, jnp.zeros_like(p0), jnp.zeros_like(p0))
    q_ref[...] = apply_lower(inverse_lower(gram_of(parts, p0)), parts)


def split_off(own_ref, other_ref, q_ref, left, right):
    k = q_ref.shape[0]
    q = q_ref[...]
    zeros = jnp.zeros(q.shape, BF16)
    q1, q2, q3 = split3(q)
    qs = jnp.concatenate([q1, q2, q3], axis=0)
    w = jnp.zeros(q.shape, F32)
    for ref in (own_ref, other_ref):
        t3 = dot(qs, ref[...], NN)
        ts = split3(t3[:k] + t3[k : 2 * k] + t3[2 * k :])
        w3 = dot(jnp.concatenate(ts, axis=0), ref[...], NT)
        w += w3[:k] + w3[k : 2 * k] + w3[2 * k :]
    ws = jnp.concatenate(list(split3(w)) + [zeros], axis=0)
    m = lane_sum3(dot(q1, ws, NT) + dot(q2, ws, NT) + dot(q3, ws, NT), k)
    m = jnp.where(lax.broadcasted_iota(jnp.int32, m.shape, 1) < k, m, 0.0)
    m = pltpu.roll(m, k, 1) + pltpu.roll(m, 2 * k, 1) + pltpu.roll(m, 3 * k, 1)
    w1, w2, w3 = split3(w - 0.5 * apply_lower(m, (q1, q2, q3)))
    left[...] = jnp.concatenate([q1, w1, q1, w1, q1, w1, q2, w2, q2, w2, q3, w3], axis=0)
    right[...] = jnp.concatenate([w1, q1, w2, q2, w3, q3, w1, q1, w2, q2, w1, q1], axis=0)


def form_rows(k, first, own_ref, other_ref, left, right, out_ref, window, right_win):
    n, px = own_ref.shape
    rows, width = out_ref.shape
    width -= LANES
    bs = width - n // 2
    nb = n // bs
    for b in range(window.shape[0] // bs):
        at = pl.multiple_of(lax.rem(first + b, nb) * bs, bs)
        window[b * bs : (b + 1) * bs, :px] = own_ref[pl.ds(at, bs), :]
        window[b * bs : (b + 1) * bs, px:] = other_ref[pl.ds(at, bs), :]
        right_win[:, b * bs : (b + 1) * bs] = right[:, pl.ds(at, bs)]
    eye = lax.broadcasted_iota(jnp.int32, (bs, bs), 0) == lax.broadcasted_iota(jnp.int32, (bs, bs), 1)
    step = STEP * bs
    for i in range(rows // bs):
        if i % STEP == 0:
            at = pl.multiple_of((first + i) * bs, bs)
            lo, end = i * bs, i * bs + step - bs + width
            wide = dot(window[lo : lo + step, :], window[lo:end, :], NT)
            wide -= dot(left[:, pl.ds(at, step)], right_win[:, lo:end], TN)
        off = i % STEP * bs
        to = i * bs
        s = wide[off : off + bs, off : off + width]
        corner = s[:, :bs]
        diagonal = jnp.sum(jnp.where(eye, corner, 0.0), axis=0, keepdims=True)
        out_ref[to : to + bs, :bs] = jnp.where(eye, 0.0, corner).astype(BF16)
        out_ref[to : to + bs, bs:width] = s[:, bs:].astype(BF16)
        side = []
        for g, d in enumerate(split3(diagonal)):
            side.append(right_win[2 * g * k : (2 * g + 1) * k, to : to + bs].astype(F32))
            side.append(jnp.broadcast_to(d.astype(F32), (GROUP - k, bs)))
        side.append(jnp.zeros((LANES - 3 * GROUP, bs), F32))
        out_ref[to : to + bs, width:] = jnp.concatenate(side, axis=0).T.astype(BF16)


def form_kernel(slot, at_ref, own_ref, other_ref, q_ref, out_ref, left, right, *wins):
    split_off(own_ref, other_ref, q_ref, left, right)
    form_rows(q_ref.shape[0], at_ref[slot], own_ref, other_ref, left, right, out_ref, *wins)


def add_kernel(slots, at_ref, a_ref, b_ref, *o_refs):
    width = a_ref.shape[1] - LANES
    for slot, o_ref in zip(slots, o_refs):
        h = o_ref.shape[0]
        at = 0 if slot is None else pl.multiple_of(at_ref[slot] * h, h)
        a, b = a_ref[pl.ds(at, h), :], b_ref[pl.ds(at, h), :]
        o_ref[:, :width] = (a[:, :width].astype(F32) + b[:, :width].astype(F32)).astype(BF16)
        x = lane_sum3(a[:, width:].astype(F32), GROUP) + lane_sum3(b[:, width:].astype(F32), GROUP)
        lane = lax.broadcasted_iota(jnp.int32, x.shape, 1)
        h1, h2, h3 = [part.astype(F32) for part in split3(x)]
        packed = jnp.where(lane < 2 * GROUP, pltpu.roll(h2, GROUP, 1), pltpu.roll(h3, 2 * GROUP, 1))
        packed = jnp.where(lane < GROUP, h1, packed)
        o_ref[:, width:] = jnp.where(lane < 3 * GROUP, packed, 0.0).astype(BF16)


def add_shares(a, b, index, *slots):
    shape = jax.ShapeDtypeStruct((a.shape[0] // (2 if slots else 1), a.shape[1]), BF16)
    slots = slots or (None,)
    return kernel_call(
        functools.partial(add_kernel, slots),
        (shape,) * len(slots),
        in_specs=[smem()] + vmem(2),
        out_specs=tuple(vmem(len(slots))),
    )(index, a, b)


def unpack(offset, index_ref, share_ref, q_ref, full, u, v, diag):
    k, n = q_ref.shape
    width = share_ref.shape[1] - LANES
    bs = width - n // 2
    nb = n // bs

    def one(r, _):
        i = index_ref[r + offset]
        frm = pl.multiple_of(r * bs, bs)
        to = pl.multiple_of(i * bs, bs)
        for d in range(nb // 2 + 1):
            part = share_ref[pl.ds(frm, bs), d * bs : (d + 1) * bs]
            at = pl.multiple_of(lax.rem(i + d, nb) * bs, bs)
            full[pl.ds(to, bs), pl.ds(at, bs)] = part
            if 0 < d < nb // 2:
                full[pl.ds(at, bs), pl.ds(to, bs)] = part.T
        side = share_ref[pl.ds(frm, bs), width:].astype(F32).T
        side = side[:GROUP] + side[GROUP : 2 * GROUP] + side[2 * GROUP : 3 * GROUP]
        w = side[:k]
        diag[:, pl.ds(to, bs)] = side[k : k + 8]
        q = q_ref[:, pl.ds(to, bs)]
        us = [part.astype(F32) for part in split3(jnp.concatenate([w, q], axis=0))]
        v1, v2, v3 = split3(jnp.concatenate([q, w], axis=0))
        u[pl.ds(to, bs), :LANES] = jnp.concatenate(us[:2], axis=0).T.astype(BF16)
        tail = jnp.concatenate([us[2], jnp.zeros((2 * k, bs), F32)], axis=0)
        u[pl.ds(to, bs), LANES:] = tail.T.astype(BF16)
        v[:, pl.ds(to, bs)] = jnp.concatenate([v1, v2, v3, v1, v2, v1], axis=0)
        return 0

    lax.fori_loop(0, nb // 2, one, 0)


def iterate_kernel(
    offset, index_ref, far_ref, q_ref, p0_ref, *refs
):
    p_ref, inv_ref, full, u, v, diag = refs[4:]
    k, _ = q_ref.shape
    unpack(offset, index_ref, far_ref, q_ref, full, u, v, diag)
    lane = lax.broadcasted_iota(jnp.int32, (k, LANES), 1)

    def product(p):
        t = dot(p, u[...], NN)
        t = t[:, :LANES] + t[:, LANES:]
        t = t + pltpu.roll(t, 2 * k, 1)
        h1, h2, h3 = [h.astype(F32) for h in split3(t)]
        low = lane < 2 * k
        ts = jnp.concatenate([h1, jnp.where(low, h1, h2), jnp.where(low, h2, h3)], axis=1).astype(BF16)
        y = dot(p, full[...], NN) + dot(ts, v[...], NN) + p.astype(F32) * diag[0:1, :]
        return split3(y)

    def sweep(step, p):
        parts = product(p)
        return apply_lower(inverse_lower(gram_of(parts, p)), parts).astype(BF16)

    p = lax.fori_loop(0, ITERS - 1, sweep, p0_ref[...])
    p_ref[...] = p
    inv_ref[...] = inverse_lower(gram_of(product(p), p))


def finish_kernel(scale, p_ref, inv_ref, block_ref, o_ref):
    back = dot(p_ref[...], block_ref[...], NN)
    o_ref[...] = (apply_lower(inv_ref[...], split3(back)) * scale).astype(BF16)


def flip(x, axes, perm):
    return lax.ppermute(x, axes, perm)


def ordered(own, recv, bit, axis=0):
    return jnp.where(
        bit == 0,
        jnp.concatenate([own, recv], axis=axis),
        jnp.concatenate([recv, own], axis=axis),
    )


def sample_space(stamps, start_panel):
    pix = lax.axis_size("pix")
    samp = lax.axis_size("samp")
    n = stamps.shape[0] * pix * samp
    k = start_panel.shape[1]
    scale = math.sqrt(start_panel.shape[0] * pix)
    p = lax.axis_index("pix")
    s = lax.axis_index("samp")
    xor_pix = lambda b: [(i, i ^ b) for i in range(pix)]
    xor_samp = lambda b: [(i, i ^ b) for i in range(samp)]

    core = p & 1
    x, y = (p >> 1) & 1, (p >> 2) & 1
    z0, z1 = s & 1, (s >> 1) & 1

    low = start_panel.astype(BF16).T
    for b in (2, 4):
        low = jnp.concatenate([low, flip(low, "pix", xor_pix(b))], axis=1)
    far = flip(low, "pix", xor_pix(1))
    bit_a = jnp.where(core == 0, x, y)
    bit_b = jnp.where(core == 0, y, x)
    bs = 2 * stamps.shape[0]
    nb = n // bs
    at = jnp.arange(pix, dtype=jnp.int32)
    place = p ^ (((at & 1) << 1) | ((at & 2) << 1) | (at >> 2))
    at = jnp.arange(nb, dtype=jnp.int32)
    c_of = core ^ ((at >> 3) & 1)
    a_of = jnp.where(c_of == 0, x, y) ^ ((at >> 2) & 1)
    b_of = jnp.where(c_of == 0, y, x) ^ ((at >> 1) & 1)
    order = c_of * 8 + a_of * 4 + b_of * 2 + (z0 ^ (at & 1))
    quarter = nb // 4
    pairs = [core * 2 * quarter + (1 - bit_a) * quarter, core * 2 * quarter + bit_a * quarter]
    for bit in (bit_b, z0, z1):
        pairs += [1 - bit, bit]
    index = jnp.concatenate([jnp.stack(pairs), place, order]).astype(jnp.int32)

    block = lax.all_to_all(stamps, ("pix", "samp"), split_axis=1, concat_axis=0, tiled=True)

    proj = kernel_call(
        rows_kernel,
        jax.ShapeDtypeStruct((k, stamps.shape[0]), BF16),
        in_specs=[smem()] + vmem(3),
        out_specs=vmem()[0],
    )(index, low, far, stamps)
    for b in (1, 2, 4):
        proj = ordered(proj, flip(proj, "pix", xor_pix(b)), p & b, axis=1)
    for b in (1, 2):
        proj = ordered(proj, flip(proj, "samp", xor_samp(b)), s & b, axis=1)
    proj, q = kernel_call(
        functools.partial(basis_kernel, pix, samp),
        (jax.ShapeDtypeStruct((k, n), BF16), jax.ShapeDtypeStruct((k, n), F32)),
        in_specs=vmem(),
        out_specs=tuple(vmem(2)),
    )(proj)

    first = [(i, i ^ (2 if i % 2 == 0 else 4)) for i in range(pix)]
    second = [(i, i ^ (4 if i % 2 == 0 else 2)) for i in range(pix)]
    other = flip(block, "pix", xor_pix(1))
    px = block.shape[1]
    width = n // 2 + bs
    rows = n // 4
    window = rows - bs + width
    piece = jax.ShapeDtypeStruct((rows, width + LANES), BF16)

    def form(slot):
        return kernel_call(
            functools.partial(form_kernel, slot),
            piece,
            in_specs=[smem()] + vmem(3),
            out_specs=vmem()[0],
            scratch_mib=20,
            scratch_shapes=[
                pltpu.VMEM((12 * k, n), BF16),
                pltpu.VMEM((12 * k, n), BF16),
                pltpu.VMEM((window, 2 * px), BF16),
                pltpu.VMEM((12 * k, window), BF16),
            ],
        )(index, block, other, q)

    send = form(SEND)
    recv = flip(send, "pix", first)
    keep = form(KEEP)
    (send,) = add_shares(keep, recv, index, SEND + 2)
    (keep,) = add_shares(keep, recv, index, KEEP + 2)
    recv = flip(send, "pix", second)
    for b, slot in ((1, 4), (2, 6)):
        send, keep = add_shares(keep, recv, index, SEND + slot, KEEP + slot)
        recv = flip(send, "samp", xor_samp(b))
    (share,) = add_shares(keep, recv, index)

    share = ordered(share, flip(share, "samp", xor_samp(2)), z1)
    for axis, perm in (("samp", xor_samp(1)), ("pix", second), ("pix", first)):
        share = jnp.concatenate([share, flip(share, axis, perm)], axis=0)
    far = flip(share, "pix", xor_pix(1))
    parts = (
        jax.ShapeDtypeStruct((n, n), BF16),
        jax.ShapeDtypeStruct((n, 8 * k), BF16),
        jax.ShapeDtypeStruct((12 * k, n), BF16),
        jax.ShapeDtypeStruct((8, n), F32),
    )
    parts_now = kernel_call(
        functools.partial(unpack, BLOCKS),
        parts,
        in_specs=[smem()] + vmem(2),
        out_specs=tuple(vmem(4)),
        scratch_mib=4,
    )(index, share, q)
    proj, inv = kernel_call(
        functools.partial(iterate_kernel, BLOCKS + nb // 2),
        (jax.ShapeDtypeStruct((k, n), BF16), jax.ShapeDtypeStruct((k, LANES), F32)) + parts,
        in_specs=[smem()] + vmem(7),
        out_specs=tuple(vmem(6)),
        input_output_aliases={4 + i: 2 + i for i in range(4)},
        scratch_mib=12,
    )(index, far, q, proj, *parts_now)[:2]

    mine = kernel_call(
        functools.partial(finish_kernel, scale),
        jax.ShapeDtypeStruct((k, px), BF16),
        in_specs=vmem(3),
        out_specs=vmem()[0],
    )(proj, inv, block)
    for b in (2, 1):
        mine = jnp.concatenate([mine, flip(mine, "samp", xor_samp(b))], axis=1)
    parts = [mine[:, i * px : (i + 1) * px] for i in range(samp)]
    by_distance = {0: parts[0], 2: parts[1], 1: parts[2], 3: parts[3]}
    swap0 = [jnp.where(z0 == 0, by_distance[i], by_distance[i ^ 1]) for i in range(samp)]
    swap1 = [jnp.where(z1 == 0, swap0[i], swap0[i ^ 2]) for i in range(samp)]
    return jnp.concatenate(swap1, axis=1).astype(F32).T


def solution(mesh):
    pix, samp = mesh.shape["pix"], mesh.shape["samp"]

    def local(stamps, start_panel):
        n = stamps.shape[0] * pix * samp
        k = start_panel.shape[1]
        if n <= SAMPLE_SPACE_LIMIT and (pix, samp) == (8, 4) and 4 * k == LANES:
            return sample_space(stamps, start_panel)
        return pixel_space(stamps, start_panel)

    return jax.shard_map(
        local,
        mesh=mesh,
        in_specs=(P(("samp", "pix"), None), P("pix", None)),
        out_specs=P("pix", None),
        check_vma=False,
    )
```

```python
import functools
import math

import jax
import jax.numpy as jnp
from jax import lax
from jax.experimental import pallas as pl
from jax.experimental.pallas import tpu as pltpu
from jax.sharding import PartitionSpec as P


ITERS = 10
LANES = 128
PANEL = 16
GROUP = 40
STEP = 2
QUARTERS, HALVES, PLACE, BLOCKS = 0, 4, 8, 16
SAMPLE_SPACE_LIMIT = 4096
F32 = jnp.float32
BF16 = jnp.bfloat16

NN = (((1,), (0,)), ((), ()))
NT = (((1,), (1,)), ((), ()))
TN = (((0,), (0,)), ((), ()))


def orthonormal(back, gram):
    lower = jnp.linalg.cholesky(gram)
    return lax.linalg.triangular_solve(lower, back, left_side=False, lower=True, transpose_a=True)


def pixel_space(stamps, start_panel):
    block = lax.all_to_all(stamps, "pix", split_axis=1, concat_axis=0, tiled=True)

    def sweep(step, panel):
        partial_value = jnp.dot(block, panel.astype(BF16), preferred_element_type=F32)
        proj = lax.psum(partial_value.astype(BF16), "pix")
        back = lax.dot_general(block, proj, TN, preferred_element_type=F32)
        summed = lax.psum(back.astype(BF16), "samp").astype(F32)
        gram = lax.psum(jnp.dot(summed.T, summed, precision=lax.Precision.HIGHEST), "pix")
        return orthonormal(summed, gram)

    panel = lax.fori_loop(0, ITERS, sweep, start_panel)
    return panel * math.sqrt(start_panel.shape[0] * lax.axis_size("pix"))


def dot(a, b, dims):
    return lax.dot_general(a, b, dims, preferred_element_type=F32)


def split3(x):
    hi = x.astype(BF16)
    rest = x - hi.astype(F32)
    mid = rest.astype(BF16)
    lo = (rest - mid.astype(F32)).astype(BF16)
    return hi, mid, lo


def kernel_call(body, out_shape, in_specs=(), scratch_mib=8, **kw):
    single = not isinstance(out_shape, tuple)
    outs = tuple(pltpu.VMEM(o.shape, o.dtype) for o in ((out_shape,) if single else out_shape))
    call = pl.pallas_call(
        body,
        out_shape=outs[0] if single else outs,
        in_specs=in_specs,
        compiler_params=pltpu.CompilerParams(vmem_limit_bytes=scratch_mib << 20),
        **kw,
    )

    def place(x, spec):
        if spec.memory_space != pltpu.VMEM:
            return x
        return pltpu.with_memory_space_constraint(x, pltpu.VMEM)

    return lambda *args: call(*map(place, args, in_specs))


def vmem(n=1):
    return [pl.BlockSpec(memory_space=pltpu.VMEM)] * n


def smem():
    return pl.BlockSpec(memory_space=pltpu.SMEM)


def inverse_lower(gram):
    k = gram.shape[0]
    lane = lax.broadcasted_iota(jnp.int32, gram.shape, 1)
    row = lax.broadcasted_iota(jnp.int32, gram.shape, 0)
    m = jnp.where(lane < k, gram, jnp.where(lane % k == row, 1.0, 0.0))
    pivots = jnp.ones(gram.shape, F32)
    for start in range(0, k, PANEL):
        cols = [jnp.broadcast_to(m[:, j : j + 1], m.shape) for j in range(start, start + PANEL)]
        for t in range(PANEL):
            j = start + t
            pivot = cols[t][j : j + 1, :]
            factor = jnp.where(row > j, cols[t] * (1.0 / pivot), 0.0)
            pivots = jnp.where(row == j, pivot, pivots)
            for later in range(t + 1, PANEL):
                cols[later] = cols[later] - factor * cols[later][j : j + 1, :]
            m = m - factor * m[j : j + 1, :]
    return m * lax.rsqrt(pivots)


def lane_sum3(x, k):
    return x + pltpu.roll(x, LANES - k, 1) + pltpu.roll(x, LANES - 2 * k, 1)


def gram_of(parts, right):
    k = right.shape[0]
    wide = jnp.concatenate([right, jnp.zeros((3 * k, right.shape[1]), right.dtype)], axis=0)
    g = dot(jnp.concatenate(parts, axis=0), wide, NT)
    return g[:k] + g[k : 2 * k] + g[2 * k :]


def apply_lower(inv, parts):
    k = inv.shape[0]
    lane = lax.broadcasted_iota(jnp.int32, inv.shape, 1)
    h1, h2, h3 = [h.astype(F32) for h in split3(inv)]
    first = jnp.where(lane < k, 0.0, h1)
    second = jnp.where(lane < k, 0.0, jnp.where(lane < 3 * k, h2, h3))
    left = jnp.concatenate([first, second], axis=1).astype(BF16)
    y1, y2, y3 = parts
    zeros = jnp.zeros_like(y1)
    return dot(left, jnp.concatenate([zeros, y1, y2, y3, zeros, y1, y2, y1], axis=0), NN)


def rows_kernel(index_ref, near_ref, far_ref, stamps_ref, o_ref):
    total = jnp.zeros(o_ref.shape, F32)
    pix = BLOCKS - PLACE
    m = near_ref.shape[1] * 2 // pix
    for j in range(pix):
        ref = near_ref if j * m < near_ref.shape[1] else far_ref
        at = j * m % near_ref.shape[1]
        stamps = stamps_ref[:, pl.ds(pl.multiple_of(index_ref[PLACE + j] * m, LANES), m)]
        total += dot(ref[:, at : at + m], stamps, NT)
    o_ref[...] = total.astype(BF16)


def basis_kernel(pix, samp, p0_ref, p_ref, q_ref):
    k, n = p0_ref.shape
    m = n // (pix * samp)
    per = LANES // m
    lane = lax.broadcasted_iota(jnp.int32, (k, LANES), 1)
    for to in range(n // LANES):
        block = jnp.zeros((k, LANES), F32)
        for j in range(per):
            p, s = divmod(to * per + j, samp)
            group, slot = divmod(s * pix + p, per)
            part = p0_ref[:, group * LANES : (group + 1) * LANES].astype(F32)
            part = pltpu.roll(part, (j - slot) * m % LANES, 1) if j != slot else part
            block = jnp.where(lane // m == j, part, block)
        p_ref[:, to * LANES : (to + 1) * LANES] = block.astype(BF16)
    p0 = p_ref[...]
    parts = (p0, jnp.zeros_like(p0), jnp.zeros_like(p0))
    q_ref[...] = apply_lower(inverse_lower(gram_of(parts, p0)), parts)


def factors_kernel(own_ref, other_ref, q_ref, left, right):
    k = q_ref.shape[0]
    q = q_ref[...]
    zeros = jnp.zeros(q.shape, BF16)
    q1, q2, q3 = split3(q)
    qs = jnp.concatenate([q1, q2, q3], axis=0)
    w = jnp.zeros(q.shape, F32)
    for ref in (own_ref, other_ref):
        t3 = dot(qs, ref[...], NN)
        ts = split3(t3[:k] + t3[k : 2 * k] + t3[2 * k :])
        w3 = dot(jnp.concatenate(ts, axis=0), ref[...], NT)
        w += w3[:k] + w3[k : 2 * k] + w3[2 * k :]
    ws = jnp.concatenate(list(split3(w)) + [zeros], axis=0)
    m = lane_sum3(dot(q1, ws, NT) + dot(q2, ws, NT) + dot(q3, ws, NT), k)
    m = jnp.where(lax.broadcasted_iota(jnp.int32, m.shape, 1) < k, m, 0.0)
    m = pltpu.roll(m, k, 1) + pltpu.roll(m, 2 * k, 1) + pltpu.roll(m, 3 * k, 1)
    w1, w2, w3 = split3(w - 0.5 * apply_lower(m, (q1, q2, q3)))
    left[...] = jnp.concatenate([q1, w1, q1, w1, q1, w1, q2, w2, q2, w2, q3, w3], axis=0)
    right[...] = jnp.concatenate([w1, q1, w2, q2, w3, q3, w1, q1, w2, q2, w1, q1], axis=0)


def form_rows(k, first, own_ref, other_ref, left, right, out_ref, window, right_win):
    n, px = own_ref.shape
    rows, width = out_ref.shape
    width -= LANES
    bs = width - n // 2
    nb = n // bs
    for b in range(window.shape[0] // bs):
        at = pl.multiple_of(lax.rem(first + b, nb) * bs, bs)
        window[b * bs : (b + 1) * bs, :px] = own_ref[pl.ds(at, bs), :]
        window[b * bs : (b + 1) * bs, px:] = other_ref[pl.ds(at, bs), :]
        right_win[:, b * bs : (b + 1) * bs] = right[:, pl.ds(at, bs)]
    eye = lax.broadcasted_iota(jnp.int32, (bs, bs), 0) == lax.broadcasted_iota(jnp.int32, (bs, bs), 1)
    step = STEP * bs
    for i in range(rows // bs):
        if i % STEP == 0:
            at = pl.multiple_of((first + i) * bs, bs)
            lo, end = i * bs, i * bs + step - bs + width
            wide = dot(window[lo : lo + step, :], window[lo:end, :], NT)
            wide -= dot(left[:, pl.ds(at, step)], right_win[:, lo:end], TN)
        off = i % STEP * bs
        to = i * bs
        s = wide[off : off + bs, off : off + width]
        corner = s[:, :bs]
        diagonal = jnp.sum(jnp.where(eye, corner, 0.0), axis=0, keepdims=True)
        out_ref[to : to + bs, :bs] = jnp.where(eye, 0.0, corner).astype(BF16)
        out_ref[to : to + bs, bs:width] = s[:, bs:].astype(BF16)
        side = []
        for g, d in enumerate(split3(diagonal)):
            side.append(right_win[2 * g * k : (2 * g + 1) * k, to : to + bs].astype(F32))
            side.append(jnp.broadcast_to(d.astype(F32), (GROUP - k, bs)))
        side.append(jnp.zeros((LANES - 3 * GROUP, bs), F32))
        out_ref[to : to + bs, width:] = jnp.concatenate(side, axis=0).T.astype(BF16)


def form_kernel(k, slot, at_ref, own_ref, other_ref, left, right, out_ref, *wins):
    form_rows(k, at_ref[slot], own_ref, other_ref, left, right, out_ref, *wins)


def add_kernel(slots, at_ref, a_ref, b_ref, *o_refs):
    width = a_ref.shape[1] - LANES
    for slot, o_ref in zip(slots, o_refs):
        h = o_ref.shape[0]
        at = 0 if slot is None else pl.multiple_of(at_ref[slot] * h, h)
        a, b = a_ref[pl.ds(at, h), :], b_ref[pl.ds(at, h), :]
        o_ref[:, :width] = (a[:, :width].astype(F32) + b[:, :width].astype(F32)).astype(BF16)
        x = lane_sum3(a[:, width:].astype(F32), GROUP) + lane_sum3(b[:, width:].astype(F32), GROUP)
        lane = lax.broadcasted_iota(jnp.int32, x.shape, 1)
        h1, h2, h3 = [part.astype(F32) for part in split3(x)]
        packed = jnp.where(lane < 2 * GROUP, pltpu.roll(h2, GROUP, 1), pltpu.roll(h3, 2 * GROUP, 1))
        packed = jnp.where(lane < GROUP, h1, packed)
        o_ref[:, width:] = jnp.where(lane < 3 * GROUP, packed, 0.0).astype(BF16)


def add_shares(a, b, index, *slots):
    shape = jax.ShapeDtypeStruct((a.shape[0] // max(len(slots), 1), a.shape[1]), BF16)
    slots = slots or (None,)
    return kernel_call(
        functools.partial(add_kernel, slots),
        (shape,) * len(slots),
        in_specs=[smem()] + vmem(2),
        out_specs=tuple(vmem(len(slots))),
    )(index, a, b)


def unpack(offset, index_ref, share_ref, q_ref, full, u, v, diag):
    k, n = q_ref.shape
    width = share_ref.shape[1] - LANES
    bs = width - n // 2
    nb = n // bs

    def one(r, _):
        i = index_ref[r + offset]
        frm = pl.multiple_of(r * bs, bs)
        to = pl.multiple_of(i * bs, bs)
        for d in range(nb // 2 + 1):
            part = share_ref[pl.ds(frm, bs), d * bs : (d + 1) * bs]
            at = pl.multiple_of(lax.rem(i + d, nb) * bs, bs)
            full[pl.ds(to, bs), pl.ds(at, bs)] = part
            if 0 < d < nb // 2:
                full[pl.ds(at, bs), pl.ds(to, bs)] = part.T
        side = share_ref[pl.ds(frm, bs), width:].astype(F32).T
        side = side[:GROUP] + side[GROUP : 2 * GROUP] + side[2 * GROUP : 3 * GROUP]
        w = side[:k]
        diag[:, pl.ds(to, bs)] = side[k : k + 8]
        q = q_ref[:, pl.ds(to, bs)]
        us = [part.astype(F32) for part in split3(jnp.concatenate([w, q], axis=0))]
        v1, v2, v3 = split3(jnp.concatenate([q, w], axis=0))
        u[pl.ds(to, bs), :LANES] = jnp.concatenate(us[:2], axis=0).T.astype(BF16)
        tail = jnp.concatenate([us[2], jnp.zeros((2 * k, bs), F32)], axis=0)
        u[pl.ds(to, bs), LANES:] = tail.T.astype(BF16)
        v[:, pl.ds(to, bs)] = jnp.concatenate([v1, v2, v3, v1, v2, v1], axis=0)
        return 0

    lax.fori_loop(0, share_ref.shape[0] // bs, one, 0)


def unpack_kernel(offsets, index_ref, *refs):
    shares, q_ref = refs[: len(offsets)], refs[len(offsets)]
    for offset, share_ref in zip(offsets, shares):
        unpack(offset, index_ref, share_ref, q_ref, *refs[-4:])


def iterate_kernel(offset, index_ref, far_ref, q_ref, p0_ref, *refs):
    p_ref, inv_ref, full, u, v, diag = refs[4:]
    k, _ = q_ref.shape
    unpack(offset, index_ref, far_ref, q_ref, full, u, v, diag)
    lane = lax.broadcasted_iota(jnp.int32, (k, LANES), 1)

    def product(p):
        t = dot(p, u[...], NN)
        t = t[:, :LANES] + t[:, LANES:]
        t = t + pltpu.roll(t, 2 * k, 1)
        h1, h2, h3 = [h.astype(F32) for h in split3(t)]
        low = lane < 2 * k
        ts = jnp.concatenate([h1, jnp.where(low, h1, h2), jnp.where(low, h2, h3)], axis=1).astype(BF16)
        y = dot(p, full[...], NN) + dot(ts, v[...], NN) + p.astype(F32) * diag[0:1, :]
        return split3(y)

    def sweep(step, p):
        parts = product(p)
        return apply_lower(inverse_lower(gram_of(parts, p)), parts).astype(BF16)

    p = lax.fori_loop(0, ITERS - 1, sweep, p0_ref[...])
    p_ref[...] = p
    inv_ref[...] = inverse_lower(gram_of(product(p), p))


def finish_kernel(scale, p_ref, inv_ref, block_ref, o_ref):
    back = dot(p_ref[...], block_ref[...], NN)
    o_ref[...] = (apply_lower(inv_ref[...], split3(back)) * scale).astype(BF16)


def flip(x, axes, perm):
    return lax.ppermute(x, axes, perm)


def ordered(own, recv, bit, axis=0):
    return jnp.where(
        bit == 0,
        jnp.concatenate([own, recv], axis=axis),
        jnp.concatenate([recv, own], axis=axis),
    )


def sample_space(stamps, start_panel):
    pix = lax.axis_size("pix")
    samp = lax.axis_size("samp")
    n = stamps.shape[0] * pix * samp
    k = start_panel.shape[1]
    scale = math.sqrt(start_panel.shape[0] * pix)
    p = lax.axis_index("pix")
    s = lax.axis_index("samp")
    xor_pix = lambda b: [(i, i ^ b) for i in range(pix)]
    xor_samp = lambda b: [(i, i ^ b) for i in range(samp)]

    core = p & 1
    x, y = (p >> 1) & 1, (p >> 2) & 1
    z0, z1 = s & 1, (s >> 1) & 1

    low = start_panel.astype(BF16).T
    for b in (2, 4):
        low = jnp.concatenate([low, flip(low, "pix", xor_pix(b))], axis=1)
    far = flip(low, "pix", xor_pix(1))
    bit_a = jnp.where(core == 0, x, y)
    bit_b = jnp.where(core == 0, y, x)
    bs = 2 * stamps.shape[0]
    nb = n // bs
    at = jnp.arange(pix, dtype=jnp.int32)
    place = p ^ (((at & 1) << 1) | ((at & 2) << 1) | (at >> 2))
    at = jnp.arange(nb, dtype=jnp.int32)
    c_of = core ^ ((at >> 3) & 1)
    a_of = jnp.where(c_of == 0, x, y) ^ ((at >> 2) & 1)
    b_of = jnp.where(c_of == 0, y, x) ^ ((at >> 1) & 1)
    order = c_of * 8 + a_of * 4 + b_of * 2 + (z0 ^ (at & 1))
    pairs = [
        (core * 4 + half * 2 + quarter) * (nb // 8)
        for half in (1 - bit_a, bit_a)
        for quarter in (1 - bit_b, bit_b)
    ]
    for bit in (z0, z1):
        pairs += [1 - bit, bit]
    index = jnp.concatenate([jnp.stack(pairs), place, order]).astype(jnp.int32)

    block = lax.all_to_all(stamps, ("pix", "samp"), split_axis=1, concat_axis=0, tiled=True)

    proj = kernel_call(
        rows_kernel,
        jax.ShapeDtypeStruct((k, stamps.shape[0]), BF16),
        in_specs=[smem()] + vmem(3),
        out_specs=vmem()[0],
    )(index, low, far, stamps)
    for b in (1, 2, 4):
        proj = ordered(proj, flip(proj, "pix", xor_pix(b)), p & b, axis=1)
    for b in (1, 2):
        proj = ordered(proj, flip(proj, "samp", xor_samp(b)), s & b, axis=1)
    proj, q = kernel_call(
        functools.partial(basis_kernel, pix, samp),
        (jax.ShapeDtypeStruct((k, n), BF16), jax.ShapeDtypeStruct((k, n), F32)),
        in_specs=vmem(),
        out_specs=tuple(vmem(2)),
    )(proj)

    first = [(i, i ^ (2 if i % 2 == 0 else 4)) for i in range(pix)]
    second = [(i, i ^ (4 if i % 2 == 0 else 2)) for i in range(pix)]
    other = flip(block, "pix", xor_pix(1))
    px = block.shape[1]
    width = n // 2 + bs
    rows = n // 8
    window = rows - bs + width
    piece = jax.ShapeDtypeStruct((rows, width + LANES), BF16)
    stack = jax.ShapeDtypeStruct((12 * k, n), BF16)
    left, right = kernel_call(
        factors_kernel,
        (stack, stack),
        in_specs=vmem(3),
        out_specs=tuple(vmem(2)),
        scratch_mib=12,
    )(block, other, q)

    def form(quarter):
        return kernel_call(
            functools.partial(form_kernel, k, QUARTERS + quarter),
            piece,
            in_specs=[smem()] + vmem(4),
            out_specs=vmem()[0],
            scratch_mib=12,
            scratch_shapes=[pltpu.VMEM((window, 2 * px), BF16), pltpu.VMEM((12 * k, window), BF16)],
        )(index, block, other, left, right)

    passed = flip(form(0), "pix", first)
    kept = flip(form(1), "pix", first)
    (send,) = add_shares(form(2), passed, index)
    recv = flip(send, "pix", second)
    (keep,) = add_shares(form(3), kept, index)
    for b, slot in ((1, HALVES), (2, HALVES + 2)):
        send, keep = add_shares(keep, recv, index, slot, slot + 1)
        recv = flip(send, "samp", xor_samp(b))
    (share,) = add_shares(keep, recv, index)

    share = ordered(share, flip(share, "samp", xor_samp(2)), z1)
    share = jnp.concatenate([share, flip(share, "samp", xor_samp(1))], axis=0)
    swap = xor_pix(1)
    over_a = flip(share, "pix", first)
    over_b = flip(share, "pix", second)
    over_ab = flip(over_b, "pix", first)
    near = jnp.concatenate([share, over_b], axis=0)
    far, far_a, far_ab = [flip(t, "pix", swap) for t in (near, over_a, over_ab)]
    parts = (
        jax.ShapeDtypeStruct((n, n), BF16),
        jax.ShapeDtypeStruct((n, 8 * k), BF16),
        jax.ShapeDtypeStruct((12 * k, n), BF16),
        jax.ShapeDtypeStruct((8, n), F32),
    )
    eighth = nb // 8
    now = kernel_call(
        functools.partial(unpack_kernel, (BLOCKS, BLOCKS + 4 * eighth)),
        parts,
        in_specs=[smem()] + vmem(3),
        out_specs=tuple(vmem(4)),
        scratch_mib=4,
    )(index, near, far, q)
    offsets = [BLOCKS + i * eighth for i in (2, 6, 3)]
    now = kernel_call(
        functools.partial(unpack_kernel, offsets),
        parts,
        in_specs=[smem()] + vmem(8),
        out_specs=tuple(vmem(4)),
        input_output_aliases={5 + i: i for i in range(4)},
        scratch_mib=4,
    )(index, over_a, far_a, over_ab, q, *now)
    proj, inv = kernel_call(
        functools.partial(iterate_kernel, BLOCKS + 7 * eighth),
        (jax.ShapeDtypeStruct((k, n), BF16), jax.ShapeDtypeStruct((k, LANES), F32)) + parts,
        in_specs=[smem()] + vmem(7),
        out_specs=tuple(vmem(6)),
        input_output_aliases={4 + i: 2 + i for i in range(4)},
        scratch_mib=12,
    )(index, far_ab, q, proj, *now)[:2]

    mine = kernel_call(
        functools.partial(finish_kernel, scale),
        jax.ShapeDtypeStruct((k, px), BF16),
        in_specs=vmem(3),
        out_specs=vmem()[0],
    )(proj, inv, block)
    for b in (2, 1):
        mine = jnp.concatenate([mine, flip(mine, "samp", xor_samp(b))], axis=1)
    parts = [mine[:, i * px : (i + 1) * px] for i in range(samp)]
    by_distance = {0: parts[0], 2: parts[1], 1: parts[2], 3: parts[3]}
    swap0 = [jnp.where(z0 == 0, by_distance[i], by_distance[i ^ 1]) for i in range(samp)]
    swap1 = [jnp.where(z1 == 0, swap0[i], swap0[i ^ 2]) for i in range(samp)]
    return jnp.concatenate(swap1, axis=1).astype(F32).T


def solution(mesh):
    pix, samp = mesh.shape["pix"], mesh.shape["samp"]

    def local(stamps, start_panel):
        n = stamps.shape[0] * pix * samp
        k = start_panel.shape[1]
        if n <= SAMPLE_SPACE_LIMIT and (pix, samp) == (8, 4) and 4 * k == LANES:
            return sample_space(stamps, start_panel)
        return pixel_space(stamps, start_panel)

    return jax.shard_map(
        local,
        mesh=mesh,
        in_specs=(P(("samp", "pix"), None), P("pix", None)),
        out_specs=P("pix", None),
        check_vma=False,
    )
```

```python
import functools
import math

import jax
import jax.numpy as jnp
from jax import lax
from jax.experimental import pallas as pl
from jax.experimental.pallas import tpu as pltpu
from jax.sharding import PartitionSpec as P


ITERS = 10
LANES = 128
PANEL = 16
GROUP = 40
STEP = 2
QUARTERS, HALVES, PLACE, BLOCKS = 0, 4, 8, 16
SAMPLE_SPACE_LIMIT = 4096
F32 = jnp.float32
BF16 = jnp.bfloat16

NN = (((1,), (0,)), ((), ()))
NT = (((1,), (1,)), ((), ()))
TN = (((0,), (0,)), ((), ()))


def orthonormal(back, gram):
    lower = jnp.linalg.cholesky(gram)
    return lax.linalg.triangular_solve(lower, back, left_side=False, lower=True, transpose_a=True)


def pixel_space(stamps, start_panel):
    block = lax.all_to_all(stamps, "pix", split_axis=1, concat_axis=0, tiled=True)

    def sweep(step, panel):
        partial_value = jnp.dot(block, panel.astype(BF16), preferred_element_type=F32)
        proj = lax.psum(partial_value.astype(BF16), "pix")
        back = lax.dot_general(block, proj, TN, preferred_element_type=F32)
        summed = lax.psum(back.astype(BF16), "samp").astype(F32)
        gram = lax.psum(jnp.dot(summed.T, summed, precision=lax.Precision.HIGHEST), "pix")
        return orthonormal(summed, gram)

    panel = lax.fori_loop(0, ITERS, sweep, start_panel)
    return panel * math.sqrt(start_panel.shape[0] * lax.axis_size("pix"))


def dot(a, b, dims):
    return lax.dot_general(a, b, dims, preferred_element_type=F32)


def split3(x):
    hi = x.astype(BF16)
    rest = x - hi.astype(F32)
    mid = rest.astype(BF16)
    lo = (rest - mid.astype(F32)).astype(BF16)
    return hi, mid, lo


def kernel_call(body, out_shape, in_specs=(), scratch_mib=8, **kw):
    single = not isinstance(out_shape, tuple)
    outs = tuple(pltpu.VMEM(o.shape, o.dtype) for o in ((out_shape,) if single else out_shape))
    call = pl.pallas_call(
        body,
        out_shape=outs[0] if single else outs,
        in_specs=in_specs,
        compiler_params=pltpu.CompilerParams(vmem_limit_bytes=scratch_mib << 20),
        **kw,
    )

    def place(x, spec):
        if spec.memory_space != pltpu.VMEM:
            return x
        return pltpu.with_memory_space_constraint(x, pltpu.VMEM)

    return lambda *args: call(*map(place, args, in_specs))


def vmem(n=1):
    return [pl.BlockSpec(memory_space=pltpu.VMEM)] * n


def smem():
    return pl.BlockSpec(memory_space=pltpu.SMEM)


def inverse_lower(gram):
    k = gram.shape[0]
    lane = lax.broadcasted_iota(jnp.int32, gram.shape, 1)
    row = lax.broadcasted_iota(jnp.int32, gram.shape, 0)
    m = jnp.where(lane < k, gram, jnp.where(lane % k == row, 1.0, 0.0))
    pivots = jnp.ones(gram.shape, F32)
    for start in range(0, k, PANEL):
        cols = [jnp.broadcast_to(m[:, j : j + 1], m.shape) for j in range(start, start + PANEL)]
        for t in range(PANEL):
            j = start + t
            pivot = cols[t][j : j + 1, :]
            factor = jnp.where(row > j, cols[t] * (1.0 / pivot), 0.0)
            pivots = jnp.where(row == j, pivot, pivots)
            for later in range(t + 1, PANEL):
                cols[later] = cols[later] - factor * cols[later][j : j + 1, :]
            m = m - factor * m[j : j + 1, :]
    return m * lax.rsqrt(pivots)


def lane_sum3(x, k):
    return x + pltpu.roll(x, LANES - k, 1) + pltpu.roll(x, LANES - 2 * k, 1)


def gram_of(parts, right):
    k = right.shape[0]
    wide = jnp.concatenate([right, jnp.zeros((3 * k, right.shape[1]), right.dtype)], axis=0)
    g = dot(jnp.concatenate(parts, axis=0), wide, NT)
    return g[:k] + g[k : 2 * k] + g[2 * k :]


def apply_lower(inv, parts):
    k = inv.shape[0]
    lane = lax.broadcasted_iota(jnp.int32, inv.shape, 1)
    h1, h2, h3 = [h.astype(F32) for h in split3(inv)]
    first = jnp.where(lane < k, 0.0, h1)
    second = jnp.where(lane < k, 0.0, jnp.where(lane < 3 * k, h2, h3))
    left = jnp.concatenate([first, second], axis=1).astype(BF16)
    y1, y2, y3 = parts
    zeros = jnp.zeros_like(y1)
    return dot(left, jnp.concatenate([zeros, y1, y2, y3, zeros, y1, y2, y1], axis=0), NN)


def rows_kernel(index_ref, near_ref, far_ref, stamps_ref, o_ref):
    total = jnp.zeros(o_ref.shape, F32)
    pix = BLOCKS - PLACE
    m = near_ref.shape[1] * 2 // pix
    for j in range(pix):
        ref = near_ref if j * m < near_ref.shape[1] else far_ref
        at = j * m % near_ref.shape[1]
        stamps = stamps_ref[:, pl.ds(pl.multiple_of(index_ref[PLACE + j] * m, LANES), m)]
        total += dot(ref[:, at : at + m], stamps, NT)
    o_ref[...] = total.astype(BF16)


def basis_kernel(pix, samp, p0_ref, p_ref, q_ref):
    k, n = p0_ref.shape
    m = n // (pix * samp)
    per = LANES // m
    lane = lax.broadcasted_iota(jnp.int32, (k, LANES), 1)
    for to in range(n // LANES):
        block = jnp.zeros((k, LANES), F32)
        for j in range(per):
            p, s = divmod(to * per + j, samp)
            group, slot = divmod(s * pix + p, per)
            part = p0_ref[:, group * LANES : (group + 1) * LANES].astype(F32)
            part = pltpu.roll(part, (j - slot) * m % LANES, 1) if j != slot else part
            block = jnp.where(lane // m == j, part, block)
        p_ref[:, to * LANES : (to + 1) * LANES] = block.astype(BF16)
    p0 = p_ref[...]
    parts = (p0, jnp.zeros_like(p0), jnp.zeros_like(p0))
    q_ref[...] = apply_lower(inverse_lower(gram_of(parts, p0)), parts)


def factors_kernel(own_ref, other_ref, q_ref, left, right):
    k = q_ref.shape[0]
    q = q_ref[...]
    zeros = jnp.zeros(q.shape, BF16)
    q1, q2, q3 = split3(q)
    qs = jnp.concatenate([q1, q2, q3], axis=0)
    w = jnp.zeros(q.shape, F32)
    for ref in (own_ref, other_ref):
        t3 = dot(qs, ref[...], NN)
        ts = split3(t3[:k] + t3[k : 2 * k] + t3[2 * k :])
        w3 = dot(jnp.concatenate(ts, axis=0), ref[...], NT)
        w += w3[:k] + w3[k : 2 * k] + w3[2 * k :]
    ws = jnp.concatenate(list(split3(w)) + [zeros], axis=0)
    m = lane_sum3(dot(q1, ws, NT) + dot(q2, ws, NT) + dot(q3, ws, NT), k)
    m = jnp.where(lax.broadcasted_iota(jnp.int32, m.shape, 1) < k, m, 0.0)
    m = pltpu.roll(m, k, 1) + pltpu.roll(m, 2 * k, 1) + pltpu.roll(m, 3 * k, 1)
    w1, w2, w3 = split3(w - 0.5 * apply_lower(m, (q1, q2, q3)))
    left[...] = jnp.concatenate([q1, w1, q1, w1, q1, w1, q2, w2, q2, w2, q3, w3], axis=0)
    right[...] = jnp.concatenate([w1, q1, w2, q2, w3, q3, w1, q1, w2, q2, w1, q1], axis=0)


def form_rows(k, first, own_ref, other_ref, left, right, out_ref, window, right_win):
    n, px = own_ref.shape
    rows, width = out_ref.shape
    width -= LANES
    bs = width - n // 2
    nb = n // bs
    for b in range(window.shape[0] // bs):
        at = pl.multiple_of(lax.rem(first + b, nb) * bs, bs)
        window[b * bs : (b + 1) * bs, :px] = own_ref[pl.ds(at, bs), :]
        window[b * bs : (b + 1) * bs, px:] = other_ref[pl.ds(at, bs), :]
        right_win[:, b * bs : (b + 1) * bs] = right[:, pl.ds(at, bs)]
    eye = lax.broadcasted_iota(jnp.int32, (bs, bs), 0) == lax.broadcasted_iota(jnp.int32, (bs, bs), 1)
    step = STEP * bs
    for i in range(rows // bs):
        if i % STEP == 0:
            at = pl.multiple_of((first + i) * bs, bs)
            lo, end = i * bs, i * bs + step - bs + width
            wide = dot(window[lo : lo + step, :], window[lo:end, :], NT)
            wide -= dot(left[:, pl.ds(at, step)], right_win[:, lo:end], TN)
        off = i % STEP * bs
        to = i * bs
        s = wide[off : off + bs, off : off + width]
        corner = s[:, :bs]
        diagonal = jnp.sum(jnp.where(eye, corner, 0.0), axis=0, keepdims=True)
        out_ref[to : to + bs, :bs] = jnp.where(eye, 0.0, corner).astype(BF16)
        out_ref[to : to + bs, bs:width] = s[:, bs:].astype(BF16)
        side = []
        for g, d in enumerate(split3(diagonal)):
            side.append(right_win[2 * g * k : (2 * g + 1) * k, to : to + bs].astype(F32))
            side.append(jnp.broadcast_to(d.astype(F32), (GROUP - k, bs)))
        side.append(jnp.zeros((LANES - 3 * GROUP, bs), F32))
        out_ref[to : to + bs, width:] = jnp.concatenate(side, axis=0).T.astype(BF16)


def form_kernel(k, slot, at_ref, own_ref, other_ref, left, right, out_ref, *wins):
    form_rows(k, at_ref[slot], own_ref, other_ref, left, right, out_ref, *wins)


def add_kernel(slots, at_ref, *refs):
    shares, o_refs = refs[: -len(slots)], refs[-len(slots) :]
    width = shares[0].shape[1] - LANES
    for slot, o_ref in zip(slots, o_refs):
        h = o_ref.shape[0]
        at = 0 if slot is None else pl.multiple_of(at_ref[slot] * h, h)
        parts = [ref[pl.ds(at, h), :].astype(F32) for ref in shares]
        o_ref[:, :width] = sum(part[:, :width] for part in parts).astype(BF16)
        x = sum(lane_sum3(part[:, width:], GROUP) for part in parts)
        lane = lax.broadcasted_iota(jnp.int32, x.shape, 1)
        h1, h2, h3 = [part.astype(F32) for part in split3(x)]
        packed = jnp.where(lane < 2 * GROUP, pltpu.roll(h2, GROUP, 1), pltpu.roll(h3, 2 * GROUP, 1))
        packed = jnp.where(lane < GROUP, h1, packed)
        o_ref[:, width:] = jnp.where(lane < 3 * GROUP, packed, 0.0).astype(BF16)


def add_shares(index, shares, slots=()):
    rows, lanes = shares[0].shape
    shape = jax.ShapeDtypeStruct((rows // max(len(slots), 1), lanes), BF16)
    slots = slots or (None,)
    return kernel_call(
        functools.partial(add_kernel, slots),
        (shape,) * len(slots),
        in_specs=[smem()] + vmem(len(shares)),
        out_specs=tuple(vmem(len(slots))),
    )(index, *shares)


def unpack(offset, index_ref, share_ref, q_ref, full, u, v, diag):
    k, n = q_ref.shape
    width = share_ref.shape[1] - LANES
    bs = width - n // 2
    nb = n // bs

    def one(r, _):
        i = index_ref[r + offset]
        frm = pl.multiple_of(r * bs, bs)
        to = pl.multiple_of(i * bs, bs)
        for d in range(nb // 2 + 1):
            part = share_ref[pl.ds(frm, bs), d * bs : (d + 1) * bs]
            at = pl.multiple_of(lax.rem(i + d, nb) * bs, bs)
            full[pl.ds(to, bs), pl.ds(at, bs)] = part
            if 0 < d < nb // 2:
                full[pl.ds(at, bs), pl.ds(to, bs)] = part.T
        side = share_ref[pl.ds(frm, bs), width:].astype(F32).T
        side = side[:GROUP] + side[GROUP : 2 * GROUP] + side[2 * GROUP : 3 * GROUP]
        w = side[:k]
        diag[:, pl.ds(to, bs)] = side[k : k + 8]
        q = q_ref[:, pl.ds(to, bs)]
        us = [part.astype(F32) for part in split3(jnp.concatenate([w, q], axis=0))]
        v1, v2, v3 = split3(jnp.concatenate([q, w], axis=0))
        u[pl.ds(to, bs), :LANES] = jnp.concatenate(us[:2], axis=0).T.astype(BF16)
        tail = jnp.concatenate([us[2], jnp.zeros((2 * k, bs), F32)], axis=0)
        u[pl.ds(to, bs), LANES:] = tail.T.astype(BF16)
        v[:, pl.ds(to, bs)] = jnp.concatenate([v1, v2, v3, v1, v2, v1], axis=0)
        return 0

    lax.fori_loop(0, share_ref.shape[0] // bs, one, 0)


def unpack_kernel(offsets, index_ref, *refs):
    shares, q_ref = refs[: len(offsets)], refs[len(offsets)]
    for offset, share_ref in zip(offsets, shares):
        unpack(offset, index_ref, share_ref, q_ref, *refs[-4:])


def iterate_kernel(offset, index_ref, far_ref, q_ref, p0_ref, *refs):
    p_ref, inv_ref, full, u, v, diag = refs[4:]
    k, _ = q_ref.shape
    unpack(offset, index_ref, far_ref, q_ref, full, u, v, diag)
    lane = lax.broadcasted_iota(jnp.int32, (k, LANES), 1)

    def product(p):
        t = dot(p, u[...], NN)
        t = t[:, :LANES] + t[:, LANES:]
        t = t + pltpu.roll(t, 2 * k, 1)
        h1, h2, h3 = [h.astype(F32) for h in split3(t)]
        low = lane < 2 * k
        ts = jnp.concatenate([h1, jnp.where(low, h1, h2), jnp.where(low, h2, h3)], axis=1).astype(BF16)
        y = dot(p, full[...], NN) + dot(ts, v[...], NN) + p.astype(F32) * diag[0:1, :]
        return split3(y)

    def sweep(step, p):
        parts = product(p)
        return apply_lower(inverse_lower(gram_of(parts, p)), parts).astype(BF16)

    p = lax.fori_loop(0, ITERS - 1, sweep, p0_ref[...])
    p_ref[...] = p
    inv_ref[...] = inverse_lower(gram_of(product(p), p))


def finish_kernel(scale, p_ref, inv_ref, block_ref, o_ref):
    back = dot(p_ref[...], block_ref[...], NN)
    o_ref[...] = (apply_lower(inv_ref[...], split3(back)) * scale).astype(BF16)


def flip(x, axes, perm):
    return lax.ppermute(x, axes, perm)


def ordered(own, recv, bit, axis=0):
    return jnp.where(
        bit == 0,
        jnp.concatenate([own, recv], axis=axis),
        jnp.concatenate([recv, own], axis=axis),
    )


def sample_space(stamps, start_panel):
    pix = lax.axis_size("pix")
    samp = lax.axis_size("samp")
    n = stamps.shape[0] * pix * samp
    k = start_panel.shape[1]
    scale = math.sqrt(start_panel.shape[0] * pix)
    p = lax.axis_index("pix")
    s = lax.axis_index("samp")
    xor_pix = lambda b: [(i, i ^ b) for i in range(pix)]
    xor_samp = lambda b: [(i, i ^ b) for i in range(samp)]

    core = p & 1
    x, y = (p >> 1) & 1, (p >> 2) & 1
    z0, z1 = s & 1, (s >> 1) & 1

    low = start_panel.astype(BF16).T
    for b in (2, 4):
        low = jnp.concatenate([low, flip(low, "pix", xor_pix(b))], axis=1)
    far = flip(low, "pix", xor_pix(1))
    bit_a = jnp.where(core == 0, x, y)
    bit_b = jnp.where(core == 0, y, x)
    bs = 2 * stamps.shape[0]
    nb = n // bs
    at = jnp.arange(pix, dtype=jnp.int32)
    place = p ^ (((at & 1) << 1) | ((at & 2) << 1) | (at >> 2))
    at = jnp.arange(nb, dtype=jnp.int32)
    c_of = core ^ ((at >> 3) & 1)
    a_of = jnp.where(c_of == 0, x, y) ^ ((at >> 2) & 1)
    b_of = jnp.where(c_of == 0, y, x) ^ ((at >> 1) & 1)
    order = c_of * 8 + a_of * 4 + b_of * 2 + (z0 ^ (at & 1))
    pairs = [
        (core * 4 + half * 2 + quarter) * (nb // 8)
        for half in (1 - bit_a, bit_a)
        for quarter in (1 - bit_b, bit_b)
    ]
    pairs += [1 - z0, z0, 0, 0]
    index = jnp.concatenate([jnp.stack([jnp.int32(i) for i in pairs]), place, order]).astype(jnp.int32)

    block = lax.all_to_all(stamps, ("pix", "samp"), split_axis=1, concat_axis=0, tiled=True)

    proj = kernel_call(
        rows_kernel,
        jax.ShapeDtypeStruct((k, stamps.shape[0]), BF16),
        in_specs=[smem()] + vmem(3),
        out_specs=vmem()[0],
    )(index, low, far, stamps)
    for b in (1, 2, 4):
        proj = ordered(proj, flip(proj, "pix", xor_pix(b)), p & b, axis=1)
    for b in (1, 2):
        proj = ordered(proj, flip(proj, "samp", xor_samp(b)), s & b, axis=1)
    proj, q = kernel_call(
        functools.partial(basis_kernel, pix, samp),
        (jax.ShapeDtypeStruct((k, n), BF16), jax.ShapeDtypeStruct((k, n), F32)),
        in_specs=vmem(),
        out_specs=tuple(vmem(2)),
    )(proj)

    first = [(i, i ^ (2 if i % 2 == 0 else 4)) for i in range(pix)]
    second = [(i, i ^ (4 if i % 2 == 0 else 2)) for i in range(pix)]
    other = flip(block, "pix", xor_pix(1))
    px = block.shape[1]
    width = n // 2 + bs
    rows = n // 8
    window = rows - bs + width
    piece = jax.ShapeDtypeStruct((rows, width + LANES), BF16)
    stack = jax.ShapeDtypeStruct((12 * k, n), BF16)
    left, right = kernel_call(
        factors_kernel,
        (stack, stack),
        in_specs=vmem(3),
        out_specs=tuple(vmem(2)),
        scratch_mib=12,
    )(block, other, q)

    def form(quarter):
        return kernel_call(
            functools.partial(form_kernel, k, QUARTERS + quarter),
            piece,
            in_specs=[smem()] + vmem(4),
            out_specs=vmem()[0],
            scratch_mib=12,
            scratch_shapes=[pltpu.VMEM((window, 2 * px), BF16), pltpu.VMEM((12 * k, window), BF16)],
        )(index, block, other, left, right)

    passed = flip(form(0), "pix", first)
    kept = flip(form(1), "pix", first)
    (send,) = add_shares(index, (form(2), passed))
    recv = flip(send, "pix", second)
    send, keep = add_shares(index, (form(3), kept, recv), (HALVES, HALVES + 1))
    (share,) = add_shares(index, (keep, flip(send, "samp", xor_samp(1))))
    (share,) = add_shares(index, (share, flip(share, "samp", xor_samp(2))))

    share = jnp.concatenate([share, flip(share, "samp", xor_samp(1))], axis=0)
    swap = xor_pix(1)
    over_a = flip(share, "pix", first)
    over_b = flip(share, "pix", second)
    over_ab = flip(over_b, "pix", first)
    near = jnp.concatenate([share, over_b], axis=0)
    far, far_a, far_ab = [flip(t, "pix", swap) for t in (near, over_a, over_ab)]
    parts = (
        jax.ShapeDtypeStruct((n, n), BF16),
        jax.ShapeDtypeStruct((n, 8 * k), BF16),
        jax.ShapeDtypeStruct((12 * k, n), BF16),
        jax.ShapeDtypeStruct((8, n), F32),
    )
    eighth = nb // 8
    now = kernel_call(
        functools.partial(unpack_kernel, (BLOCKS, BLOCKS + 4 * eighth)),
        parts,
        in_specs=[smem()] + vmem(3),
        out_specs=tuple(vmem(4)),
        scratch_mib=4,
    )(index, near, far, q)
    offsets = [BLOCKS + i * eighth for i in (2, 6, 3)]
    now = kernel_call(
        functools.partial(unpack_kernel, offsets),
        parts,
        in_specs=[smem()] + vmem(8),
        out_specs=tuple(vmem(4)),
        input_output_aliases={5 + i: i for i in range(4)},
        scratch_mib=4,
    )(index, over_a, far_a, over_ab, q, *now)
    proj, inv = kernel_call(
        functools.partial(iterate_kernel, BLOCKS + 7 * eighth),
        (jax.ShapeDtypeStruct((k, n), BF16), jax.ShapeDtypeStruct((k, LANES), F32)) + parts,
        in_specs=[smem()] + vmem(7),
        out_specs=tuple(vmem(6)),
        input_output_aliases={4 + i: 2 + i for i in range(4)},
        scratch_mib=12,
    )(index, far_ab, q, proj, *now)[:2]

    mine = kernel_call(
        functools.partial(finish_kernel, scale),
        jax.ShapeDtypeStruct((k, px), BF16),
        in_specs=vmem(3),
        out_specs=vmem()[0],
    )(proj, inv, block)
    for b in (2, 1):
        mine = jnp.concatenate([mine, flip(mine, "samp", xor_samp(b))], axis=1)
    parts = [mine[:, i * px : (i + 1) * px] for i in range(samp)]
    by_distance = {0: parts[0], 2: parts[1], 1: parts[2], 3: parts[3]}
    swap0 = [jnp.where(z0 == 0, by_distance[i], by_distance[i ^ 1]) for i in range(samp)]
    swap1 = [jnp.where(z1 == 0, swap0[i], swap0[i ^ 2]) for i in range(samp)]
    return jnp.concatenate(swap1, axis=1).astype(F32).T


def solution(mesh):
    pix, samp = mesh.shape["pix"], mesh.shape["samp"]

    def local(stamps, start_panel):
        n = stamps.shape[0] * pix * samp
        k = start_panel.shape[1]
        if n <= SAMPLE_SPACE_LIMIT and (pix, samp) == (8, 4) and 4 * k == LANES:
            return sample_space(stamps, start_panel)
        return pixel_space(stamps, start_panel)

    return jax.shard_map(
        local,
        mesh=mesh,
        in_specs=(P(("samp", "pix"), None), P("pix", None)),
        out_specs=P("pix", None),
        check_vma=False,
    )
```

```python
import functools
import math

import jax
import jax.numpy as jnp
from jax import lax
from jax.experimental import pallas as pl
from jax.experimental.pallas import tpu as pltpu
from jax.sharding import PartitionSpec as P


ITERS = 10
LANES = 128
PANEL = 16
RANK = 16
GROUP = 20
HALF = 64
STEP = 2
QUARTERS, HALVES, CORE, PLACE, BLOCKS = 0, 4, 6, 8, 16
SAMPLE_SPACE_LIMIT = 4096
F32 = jnp.float32
BF16 = jnp.bfloat16

NN = (((1,), (0,)), ((), ()))
NT = (((1,), (1,)), ((), ()))
TN = (((0,), (0,)), ((), ()))


def orthonormal(back, gram):
    lower = jnp.linalg.cholesky(gram)
    return lax.linalg.triangular_solve(lower, back, left_side=False, lower=True, transpose_a=True)


def pixel_space(stamps, start_panel):
    block = lax.all_to_all(stamps, "pix", split_axis=1, concat_axis=0, tiled=True)

    def sweep(step, panel):
        partial_value = jnp.dot(block, panel.astype(BF16), preferred_element_type=F32)
        proj = lax.psum(partial_value.astype(BF16), "pix")
        back = lax.dot_general(block, proj, TN, preferred_element_type=F32)
        summed = lax.psum(back.astype(BF16), "samp").astype(F32)
        gram = lax.psum(jnp.dot(summed.T, summed, precision=lax.Precision.HIGHEST), "pix")
        return orthonormal(summed, gram)

    panel = lax.fori_loop(0, ITERS, sweep, start_panel)
    return panel * math.sqrt(start_panel.shape[0] * lax.axis_size("pix"))


def dot(a, b, dims):
    return lax.dot_general(a, b, dims, preferred_element_type=F32)


def split3(x):
    hi = x.astype(BF16)
    rest = x - hi.astype(F32)
    mid = rest.astype(BF16)
    lo = (rest - mid.astype(F32)).astype(BF16)
    return hi, mid, lo


def kernel_call(body, out_shape, in_specs=(), scratch_mib=8, **kw):
    single = not isinstance(out_shape, tuple)
    outs = tuple(pltpu.VMEM(o.shape, o.dtype) for o in ((out_shape,) if single else out_shape))
    call = pl.pallas_call(
        body,
        out_shape=outs[0] if single else outs,
        in_specs=in_specs,
        compiler_params=pltpu.CompilerParams(vmem_limit_bytes=scratch_mib << 20),
        **kw,
    )

    def place(x, spec):
        if spec.memory_space != pltpu.VMEM:
            return x
        return pltpu.with_memory_space_constraint(x, pltpu.VMEM)

    return lambda *args: call(*map(place, args, in_specs))


def vmem(n=1):
    return [pl.BlockSpec(memory_space=pltpu.VMEM)] * n


def smem():
    return pl.BlockSpec(memory_space=pltpu.SMEM)


def inverse_lower(gram):
    k = gram.shape[0]
    lane = lax.broadcasted_iota(jnp.int32, gram.shape, 1)
    row = lax.broadcasted_iota(jnp.int32, gram.shape, 0)
    m = jnp.where(lane < k, gram, jnp.where(lane % k == row, 1.0, 0.0))
    pivots = jnp.ones(gram.shape, F32)
    for start in range(0, k, PANEL):
        cols = [jnp.broadcast_to(m[:, j : j + 1], m.shape) for j in range(start, start + PANEL)]
        for t in range(PANEL):
            j = start + t
            pivot = cols[t][j : j + 1, :]
            factor = jnp.where(row > j, cols[t] * (1.0 / pivot), 0.0)
            pivots = jnp.where(row == j, pivot, pivots)
            for later in range(t + 1, PANEL):
                cols[later] = cols[later] - factor * cols[later][j : j + 1, :]
            m = m - factor * m[j : j + 1, :]
    return m * lax.rsqrt(pivots)


def lane_sum3(x, k):
    return x + pltpu.roll(x, LANES - k, 1) + pltpu.roll(x, LANES - 2 * k, 1)


def gram_of(parts, right):
    k = right.shape[0]
    wide = jnp.concatenate([right, jnp.zeros((3 * k, right.shape[1]), right.dtype)], axis=0)
    g = dot(jnp.concatenate(parts, axis=0), wide, NT)
    return g[:k] + g[k : 2 * k] + g[2 * k :]


def apply_lower(inv, parts):
    k = inv.shape[0]
    lane = lax.broadcasted_iota(jnp.int32, inv.shape, 1)
    h1, h2, h3 = [h.astype(F32) for h in split3(inv)]
    first = jnp.where(lane < k, 0.0, h1)
    second = jnp.where(lane < k, 0.0, jnp.where(lane < 3 * k, h2, h3))
    left = jnp.concatenate([first, second], axis=1).astype(BF16)
    y1, y2, y3 = parts
    zeros = jnp.zeros_like(y1)
    return dot(left, jnp.concatenate([zeros, y1, y2, y3, zeros, y1, y2, y1], axis=0), NN)


def rows_kernel(index_ref, near_ref, far_ref, stamps_ref, o_ref):
    total = jnp.zeros(o_ref.shape, F32)
    pix = BLOCKS - PLACE
    m = near_ref.shape[1] * 2 // pix
    for j in range(pix):
        ref = near_ref if j * m < near_ref.shape[1] else far_ref
        at = j * m % near_ref.shape[1]
        stamps = stamps_ref[:, pl.ds(pl.multiple_of(index_ref[PLACE + j] * m, LANES), m)]
        total += dot(ref[:, at : at + m], stamps, NT)
    o_ref[...] = total.astype(BF16)


def basis_kernel(pix, samp, p0_ref, p_ref, q_ref):
    k, n = p0_ref.shape
    m = n // (pix * samp)
    per = LANES // m
    lane = lax.broadcasted_iota(jnp.int32, (k, LANES), 1)
    for to in range(n // LANES):
        block = jnp.zeros((k, LANES), F32)
        for j in range(per):
            p, s = divmod(to * per + j, samp)
            group, slot = divmod(s * pix + p, per)
            part = p0_ref[:, group * LANES : (group + 1) * LANES].astype(F32)
            part = pltpu.roll(part, (j - slot) * m % LANES, 1) if j != slot else part
            block = jnp.where(lane // m == j, part, block)
        p_ref[:, to * LANES : (to + 1) * LANES] = block.astype(BF16)
    p0 = p_ref[...]
    parts = (p0, jnp.zeros_like(p0), jnp.zeros_like(p0))
    q = apply_lower(inverse_lower(gram_of(parts, p0)), parts)
    q_ref[...] = jnp.where(lax.broadcasted_iota(jnp.int32, q.shape, 0) < RANK, q, 0.0)


def factors_kernel(own_ref, other_ref, q_ref, left, right):
    k = q_ref.shape[0]
    q = q_ref[...]
    zeros = jnp.zeros(q.shape, BF16)
    q1, q2, q3 = split3(q)
    qs = jnp.concatenate([q1, q2, q3], axis=0)
    w = jnp.zeros(q.shape, F32)
    for ref in (own_ref, other_ref):
        t3 = dot(qs, ref[...], NN)
        ts = split3(t3[:k] + t3[k : 2 * k] + t3[2 * k :])
        w3 = dot(jnp.concatenate(ts, axis=0), ref[...], NT)
        w += w3[:k] + w3[k : 2 * k] + w3[2 * k :]
    ws = jnp.concatenate(list(split3(w)) + [zeros], axis=0)
    m = lane_sum3(dot(q1, ws, NT) + dot(q2, ws, NT) + dot(q3, ws, NT), k)
    m = jnp.where(lax.broadcasted_iota(jnp.int32, m.shape, 1) < k, m, 0.0)
    m = pltpu.roll(m, k, 1) + pltpu.roll(m, 2 * k, 1) + pltpu.roll(m, 3 * k, 1)
    w1, w2, w3 = split3(w - 0.5 * apply_lower(m, (q1, q2, q3)))
    q1, q2, q3, w1, w2, w3 = [part[:RANK] for part in (q1, q2, q3, w1, w2, w3)]
    left[...] = jnp.concatenate([q1, w1, q1, w1, q1, w1, q2, w2, q2, w2, q3, w3], axis=0)
    right[...] = jnp.concatenate([w1, q1, w2, q2, w3, q3, w1, q1, w2, q2, w1, q1], axis=0)


def form_rows(first, core, own_ref, other_ref, left, right, out_ref, window, right_win):
    n, px = own_ref.shape
    rows = out_ref.shape[0]
    width = n // 2
    bs = out_ref.shape[1] - width
    nb = n // bs
    for b in range(window.shape[0] // bs):
        at = pl.multiple_of(lax.rem(first + b, nb) * bs, bs)
        window[b * bs : (b + 1) * bs, :px] = own_ref[pl.ds(at, bs), :]
        window[b * bs : (b + 1) * bs, px:] = other_ref[pl.ds(at, bs), :]
        right_win[:, b * bs : (b + 1) * bs] = right[:, pl.ds(at, bs)]
    lane = lax.broadcasted_iota(jnp.int32, (bs, bs), 1)
    eye = lax.broadcasted_iota(jnp.int32, (bs, bs), 0) == lane
    step = STEP * bs
    for i in range(rows // bs):
        if i % STEP == 0:
            at = pl.multiple_of((first + i) * bs, bs)
            lo, end = i * bs, i * bs + step + width
            wide = dot(window[lo : lo + step, :], window[lo:end, :], NT)
            wide -= dot(left[:, pl.ds(at, step)], right_win[:, lo:end], TN)
        off = i % STEP * bs
        to = i * bs
        s = wide[off : off + bs, off : off + width + bs]
        corner = s[:, :bs]
        diagonal = jnp.sum(jnp.where(eye, corner, 0.0), axis=0, keepdims=True)
        out_ref[to : to + bs, :bs] = jnp.where(eye, 0.0, corner).astype(BF16)
        out_ref[to : to + bs, bs:width] = s[:, bs:width].astype(BF16)
        last = s[:, width:]
        low = last[HALF:]
        last = jnp.where(core == 0, last, jnp.concatenate([low, pltpu.roll(low, HALF, 1)], axis=0))
        side = [jnp.zeros((HALF, bs), F32)]
        for g, d in enumerate(split3(diagonal)):
            w = right_win[2 * g * RANK : (2 * g + 1) * RANK, to : to + bs]
            side.append(w.astype(F32))
            side.append(jnp.broadcast_to(d.astype(F32), (GROUP - RANK, bs)))
        side.append(jnp.zeros((bs - HALF - 3 * GROUP, bs), F32))
        side = jnp.concatenate(side, axis=0).T
        out_ref[to : to + bs, width:] = jnp.where(lane < HALF, last, side).astype(BF16)


def form_kernel(slot, at_ref, own_ref, other_ref, left, right, out_ref, *wins):
    form_rows(at_ref[slot], at_ref[CORE], own_ref, other_ref, left, right, out_ref, *wins)


def add_kernel(slots, at_ref, *refs):
    shares, o_refs = refs[: -len(slots)], refs[-len(slots) :]
    width = shares[0].shape[1] - LANES
    for slot, o_ref in zip(slots, o_refs):
        h = o_ref.shape[0]
        at = 0 if slot is None else pl.multiple_of(at_ref[slot] * h, h)
        parts = [ref[pl.ds(at, h), :].astype(F32) for ref in shares]
        o_ref[:, :width] = sum(part[:, :width] for part in parts).astype(BF16)
        last = [part[:, width:] for part in parts]
        x = sum(lane_sum3(part, GROUP) for part in last)
        lane = lax.broadcasted_iota(jnp.int32, x.shape, 1) - HALF
        h1, h2, h3 = [part.astype(F32) for part in split3(x)]
        packed = jnp.where(lane < 2 * GROUP, pltpu.roll(h2, GROUP, 1), pltpu.roll(h3, 2 * GROUP, 1))
        packed = jnp.where(lane < GROUP, h1, packed)
        packed = jnp.where(lane < 3 * GROUP, packed, 0.0)
        o_ref[:, width:] = jnp.where(lane < 0, sum(last), packed).astype(BF16)


def add_shares(index, shares, slots=()):
    rows, lanes = shares[0].shape
    shape = jax.ShapeDtypeStruct((rows // max(len(slots), 1), lanes), BF16)
    slots = slots or (None,)
    return kernel_call(
        functools.partial(add_kernel, slots),
        (shape,) * len(slots),
        in_specs=[smem()] + vmem(len(shares)),
        out_specs=tuple(vmem(len(slots))),
    )(index, *shares)


def unpack(offset, index_ref, share_ref, q_ref, full, u, v, diag):
    n = q_ref.shape[1]
    width = n // 2
    bs = share_ref.shape[1] - width
    nb = n // bs
    lane = lax.broadcasted_iota(jnp.int32, (bs, bs), 1)

    def one(r, _):
        i = index_ref[r + offset]
        frm = pl.multiple_of(r * bs, bs)
        to = pl.multiple_of(i * bs, bs)
        for d in range(nb // 2):
            part = share_ref[pl.ds(frm, bs), d * bs : (d + 1) * bs]
            at = pl.multiple_of(lax.rem(i + d, nb) * bs, bs)
            full[pl.ds(to, bs), pl.ds(at, bs)] = part
            if d:
                full[pl.ds(at, bs), pl.ds(to, bs)] = part.T
        at = pl.multiple_of(lax.rem(i + nb // 2, nb) * bs, bs)
        last = share_ref[pl.ds(frm, bs), width:].astype(F32)

        @pl.when(i < nb // 2)
        def _():
            old = full[pl.ds(to, bs), pl.ds(at, bs)].astype(F32)
            full[pl.ds(to, bs), pl.ds(at, bs)] = jnp.where(lane < HALF, last, old).astype(BF16)
            full[pl.ds(at, HALF), pl.ds(to, bs)] = last.T[:HALF].astype(BF16)

        @pl.when(i >= nb // 2)
        def _():
            low = jnp.where(lane[:HALF] < HALF, last[:HALF], pltpu.roll(last[HALF:], HALF, 1))
            full[pl.ds(pl.multiple_of(to + HALF, HALF), HALF), pl.ds(at, bs)] = low.astype(BF16)
            old = full[pl.ds(at, bs), pl.ds(to, bs)].astype(F32)
            new = jnp.concatenate([low, low], axis=0).T
            full[pl.ds(at, bs), pl.ds(to, bs)] = jnp.where(lane < HALF, old, new).astype(BF16)

        side = last.T[HALF:]
        w, d = side[:RANK], side[RANK : RANK + 1]
        for g in (1, 2):
            w = w + pltpu.roll(side, HALF - g * GROUP, 0)[:RANK]
            d = d + side[g * GROUP + RANK : g * GROUP + RANK + 1]
        diag[:, pl.ds(to, bs)] = jnp.broadcast_to(d, (diag.shape[0], bs))
        q = q_ref[:RANK, pl.ds(to, bs)]
        us = [part.astype(F32) for part in split3(jnp.concatenate([w, q], axis=0))]
        us.append(jnp.zeros((bs - 6 * RANK, bs), F32))
        u[pl.ds(to, bs), :] = jnp.concatenate(us, axis=0).T.astype(BF16)
        v1, v2, v3 = split3(jnp.concatenate([q, w], axis=0))
        v[:, pl.ds(to, bs)] = jnp.concatenate([v1, v2, v3, v1, v2, v1], axis=0)
        return 0

    lax.fori_loop(0, share_ref.shape[0] // bs, one, 0)


def unpack_kernel(offsets, index_ref, *refs):
    shares, q_ref = refs[: len(offsets)], refs[len(offsets)]
    for offset, share_ref in zip(offsets, shares):
        unpack(offset, index_ref, share_ref, q_ref, *refs[-4:])


def iterate_kernel(offset, index_ref, far_ref, q_ref, p0_ref, *refs):
    p_ref, inv_ref, full, u, v, diag = refs[4:]
    k, _ = q_ref.shape
    unpack(offset, index_ref, far_ref, q_ref, full, u, v, diag)
    lane = lax.broadcasted_iota(jnp.int32, (k, LANES), 1)

    def product(p):
        t = dot(p, u[...], NN)
        t = t + pltpu.roll(t, 4 * RANK, 1)
        t = t + pltpu.roll(t, 2 * RANK, 1)
        h1, h2, h3 = [h.astype(F32) for h in split3(t)]
        ts = jnp.concatenate(
            [jnp.where(lane < 6 * RANK, h1, h2), jnp.where(lane < 2 * RANK, h2, h3)[:, :HALF]], axis=1
        ).astype(BF16)
        y = dot(p, full[...], NN) + dot(ts, v[...], NN) + p.astype(F32) * diag[0:1, :]
        return split3(y)

    def sweep(step, p):
        parts = product(p)
        return apply_lower(inverse_lower(gram_of(parts, p)), parts).astype(BF16)

    p = lax.fori_loop(0, ITERS - 1, sweep, p0_ref[...])
    p_ref[...] = p
    inv_ref[...] = inverse_lower(gram_of(product(p), p))


def finish_kernel(scale, p_ref, inv_ref, block_ref, o_ref):
    back = dot(p_ref[...], block_ref[...], NN)
    o_ref[...] = (apply_lower(inv_ref[...], split3(back)) * scale).astype(BF16)


def flip(x, axes, perm):
    return lax.ppermute(x, axes, perm)


def ordered(own, recv, bit, axis=0):
    return jnp.where(
        bit == 0,
        jnp.concatenate([own, recv], axis=axis),
        jnp.concatenate([recv, own], axis=axis),
    )


def sample_space(stamps, start_panel):
    pix = lax.axis_size("pix")
    samp = lax.axis_size("samp")
    n = stamps.shape[0] * pix * samp
    k = start_panel.shape[1]
    scale = math.sqrt(start_panel.shape[0] * pix)
    p = lax.axis_index("pix")
    s = lax.axis_index("samp")
    xor_pix = lambda b: [(i, i ^ b) for i in range(pix)]
    xor_samp = lambda b: [(i, i ^ b) for i in range(samp)]

    core = p & 1
    x, y = (p >> 1) & 1, (p >> 2) & 1
    z0, z1 = s & 1, (s >> 1) & 1

    low = start_panel.astype(BF16).T
    for b in (2, 4):
        low = jnp.concatenate([low, flip(low, "pix", xor_pix(b))], axis=1)
    far = flip(low, "pix", xor_pix(1))
    bit_a = jnp.where(core == 0, x, y)
    bit_b = jnp.where(core == 0, y, x)
    bs = 2 * stamps.shape[0]
    nb = n // bs
    at = jnp.arange(pix, dtype=jnp.int32)
    place = p ^ (((at & 1) << 1) | ((at & 2) << 1) | (at >> 2))
    at = jnp.arange(nb, dtype=jnp.int32)
    c_of = core ^ ((at >> 3) & 1)
    a_of = jnp.where(c_of == 0, x, y) ^ ((at >> 2) & 1)
    b_of = jnp.where(c_of == 0, y, x) ^ ((at >> 1) & 1)
    order = c_of * 8 + a_of * 4 + b_of * 2 + (z0 ^ (at & 1))
    pairs = [
        (core * 4 + half * 2 + quarter) * (nb // 8)
        for half in (1 - bit_a, bit_a)
        for quarter in (1 - bit_b, bit_b)
    ]
    pairs += [1 - z0, z0, core, 0]
    index = jnp.concatenate([jnp.stack([jnp.int32(i) for i in pairs]), place, order]).astype(jnp.int32)

    block = lax.all_to_all(stamps, ("pix", "samp"), split_axis=1, concat_axis=0, tiled=True)

    proj = kernel_call(
        rows_kernel,
        jax.ShapeDtypeStruct((k, stamps.shape[0]), BF16),
        in_specs=[smem()] + vmem(3),
        out_specs=vmem()[0],
    )(index, low, far, stamps)
    for b in (1, 2, 4):
        proj = ordered(proj, flip(proj, "pix", xor_pix(b)), p & b, axis=1)
    for b in (1, 2):
        proj = ordered(proj, flip(proj, "samp", xor_samp(b)), s & b, axis=1)
    proj, q = kernel_call(
        functools.partial(basis_kernel, pix, samp),
        (jax.ShapeDtypeStruct((k, n), BF16), jax.ShapeDtypeStruct((k, n), F32)),
        in_specs=vmem(),
        out_specs=tuple(vmem(2)),
    )(proj)

    first = [(i, i ^ (2 if i % 2 == 0 else 4)) for i in range(pix)]
    second = [(i, i ^ (4 if i % 2 == 0 else 2)) for i in range(pix)]
    other = flip(block, "pix", xor_pix(1))
    px = block.shape[1]
    width = n // 2 + bs
    rows = n // 8
    window = rows - bs + width
    piece = jax.ShapeDtypeStruct((rows, width), BF16)
    stack = jax.ShapeDtypeStruct((12 * RANK, n), BF16)
    left, right = kernel_call(
        factors_kernel,
        (stack, stack),
        in_specs=vmem(3),
        out_specs=tuple(vmem(2)),
        scratch_mib=12,
    )(block, other, q)

    def form(quarter):
        return kernel_call(
            functools.partial(form_kernel, QUARTERS + quarter),
            piece,
            in_specs=[smem()] + vmem(4),
            out_specs=vmem()[0],
            scratch_mib=12,
            scratch_shapes=[pltpu.VMEM((window, 2 * px), BF16), pltpu.VMEM((12 * RANK, window), BF16)],
        )(index, block, other, left, right)

    passed = flip(form(0), "pix", first)
    kept = flip(form(1), "pix", first)
    (send,) = add_shares(index, (form(2), passed))
    recv = flip(send, "pix", second)
    send, keep = add_shares(index, (form(3), kept, recv), (HALVES, HALVES + 1))
    (share,) = add_shares(index, (keep, flip(send, "samp", xor_samp(1))))
    (share,) = add_shares(index, (share, flip(share, "samp", xor_samp(2))))

    share = jnp.concatenate([share, flip(share, "samp", xor_samp(1))], axis=0)
    swap = xor_pix(1)
    over_a = flip(share, "pix", first)
    over_b = flip(share, "pix", second)
    over_ab = flip(over_b, "pix", first)
    near = jnp.concatenate([share, over_b], axis=0)
    far, far_a, far_ab = [flip(t, "pix", swap) for t in (near, over_a, over_ab)]
    parts = (
        jax.ShapeDtypeStruct((n, n), BF16),
        jax.ShapeDtypeStruct((n, bs), BF16),
        jax.ShapeDtypeStruct((12 * RANK, n), BF16),
        jax.ShapeDtypeStruct((8, n), F32),
    )
    eighth = nb // 8
    now = kernel_call(
        functools.partial(unpack_kernel, (BLOCKS, BLOCKS + 4 * eighth)),
        parts,
        in_specs=[smem()] + vmem(3),
        out_specs=tuple(vmem(4)),
        scratch_mib=4,
    )(index, near, far, q)
    offsets = [BLOCKS + i * eighth for i in (2, 6, 3)]
    now = kernel_call(
        functools.partial(unpack_kernel, offsets),
        parts,
        in_specs=[smem()] + vmem(8),
        out_specs=tuple(vmem(4)),
        input_output_aliases={5 + i: i for i in range(4)},
        scratch_mib=4,
    )(index, over_a, far_a, over_ab, q, *now)
    proj, inv = kernel_call(
        functools.partial(iterate_kernel, BLOCKS + 7 * eighth),
        (jax.ShapeDtypeStruct((k, n), BF16), jax.ShapeDtypeStruct((k, LANES), F32)) + parts,
        in_specs=[smem()] + vmem(7),
        out_specs=tuple(vmem(6)),
        input_output_aliases={4 + i: 2 + i for i in range(4)},
        scratch_mib=12,
    )(index, far_ab, q, proj, *now)[:2]

    mine = kernel_call(
        functools.partial(finish_kernel, scale),
        jax.ShapeDtypeStruct((k, px), BF16),
        in_specs=vmem(3),
        out_specs=vmem()[0],
    )(proj, inv, block)
    for b in (2, 1):
        mine = jnp.concatenate([mine, flip(mine, "samp", xor_samp(b))], axis=1)
    parts = [mine[:, i * px : (i + 1) * px] for i in range(samp)]
    by_distance = {0: parts[0], 2: parts[1], 1: parts[2], 3: parts[3]}
    swap0 = [jnp.where(z0 == 0, by_distance[i], by_distance[i ^ 1]) for i in range(samp)]
    swap1 = [jnp.where(z1 == 0, swap0[i], swap0[i ^ 2]) for i in range(samp)]
    return jnp.concatenate(swap1, axis=1).astype(F32).T


def solution(mesh):
    pix, samp = mesh.shape["pix"], mesh.shape["samp"]

    def local(stamps, start_panel):
        n = stamps.shape[0] * pix * samp
        k = start_panel.shape[1]
        if n <= SAMPLE_SPACE_LIMIT and (pix, samp) == (8, 4) and 4 * k == LANES:
            return sample_space(stamps, start_panel)
        return pixel_space(stamps, start_panel)

    return jax.shard_map(
        local,
        mesh=mesh,
        in_specs=(P(("samp", "pix"), None), P("pix", None)),
        out_specs=P("pix", None),
        check_vma=False,
    )
```

```python
import functools
import math

import jax
import jax.numpy as jnp
from jax import lax
from jax.experimental import pallas as pl
from jax.experimental.pallas import tpu as pltpu
from jax.sharding import PartitionSpec as P


ITERS = 10
LANES = 128
PANEL = 16
RANK = 16
GROUP = 20
HALF = 64
STEP = 2
QUARTERS, HALVES, CORE, PLACE, BLOCKS = 0, 4, 6, 8, 16
SAMPLE_SPACE_LIMIT = 4096
F32 = jnp.float32
BF16 = jnp.bfloat16

NN = (((1,), (0,)), ((), ()))
NT = (((1,), (1,)), ((), ()))
TN = (((0,), (0,)), ((), ()))


def orthonormal(back, gram):
    lower = jnp.linalg.cholesky(gram)
    return lax.linalg.triangular_solve(lower, back, left_side=False, lower=True, transpose_a=True)


def pixel_space(stamps, start_panel):
    block = lax.all_to_all(stamps, "pix", split_axis=1, concat_axis=0, tiled=True)

    def sweep(step, panel):
        partial_value = jnp.dot(block, panel.astype(BF16), preferred_element_type=F32)
        proj = lax.psum(partial_value.astype(BF16), "pix")
        back = lax.dot_general(block, proj, TN, preferred_element_type=F32)
        summed = lax.psum(back.astype(BF16), "samp").astype(F32)
        gram = lax.psum(jnp.dot(summed.T, summed, precision=lax.Precision.HIGHEST), "pix")
        return orthonormal(summed, gram)

    panel = lax.fori_loop(0, ITERS, sweep, start_panel)
    return panel * math.sqrt(start_panel.shape[0] * lax.axis_size("pix"))


def dot(a, b, dims):
    return lax.dot_general(a, b, dims, preferred_element_type=F32)


def split3(x):
    hi = x.astype(BF16)
    rest = x - hi.astype(F32)
    mid = rest.astype(BF16)
    lo = (rest - mid.astype(F32)).astype(BF16)
    return hi, mid, lo


def kernel_call(body, out_shape, in_specs=(), scratch_mib=8, **kw):
    single = not isinstance(out_shape, tuple)
    outs = tuple(pltpu.VMEM(o.shape, o.dtype) for o in ((out_shape,) if single else out_shape))
    call = pl.pallas_call(
        body,
        out_shape=outs[0] if single else outs,
        in_specs=in_specs,
        compiler_params=pltpu.CompilerParams(vmem_limit_bytes=scratch_mib << 20),
        **kw,
    )

    def place(x, spec):
        if spec.memory_space != pltpu.VMEM:
            return x
        return pltpu.with_memory_space_constraint(x, pltpu.VMEM)

    return lambda *args: call(*map(place, args, in_specs))


def vmem(n=1):
    return [pl.BlockSpec(memory_space=pltpu.VMEM)] * n


def smem():
    return pl.BlockSpec(memory_space=pltpu.SMEM)


def inverse_lower(gram):
    k = gram.shape[0]
    lane = lax.broadcasted_iota(jnp.int32, gram.shape, 1)
    row = lax.broadcasted_iota(jnp.int32, gram.shape, 0)
    m = jnp.where(lane < k, gram, jnp.where(lane % k == row, 1.0, 0.0))
    pivots = jnp.ones(gram.shape, F32)
    for start in range(0, k, PANEL):
        cols = [jnp.broadcast_to(m[:, j : j + 1], m.shape) for j in range(start, start + PANEL)]
        for t in range(PANEL):
            j = start + t
            pivot = cols[t][j : j + 1, :]
            factor = jnp.where(row > j, cols[t] * (1.0 / pivot), 0.0)
            pivots = jnp.where(row == j, pivot, pivots)
            for later in range(t + 1, PANEL):
                cols[later] = cols[later] - factor * cols[later][j : j + 1, :]
            m = m - factor * m[j : j + 1, :]
    return m * lax.rsqrt(pivots)


def lane_sum3(x, k):
    return x + pltpu.roll(x, LANES - k, 1) + pltpu.roll(x, LANES - 2 * k, 1)


def gram_of(parts, right):
    k = right.shape[0]
    wide = jnp.concatenate([right, jnp.zeros((3 * k, right.shape[1]), right.dtype)], axis=0)
    g = dot(jnp.concatenate(parts, axis=0), wide, NT)
    return g[:k] + g[k : 2 * k] + g[2 * k :]


def apply_lower(inv, parts):
    k = inv.shape[0]
    lane = lax.broadcasted_iota(jnp.int32, inv.shape, 1)
    h1, h2, h3 = [h.astype(F32) for h in split3(inv)]
    first = jnp.where(lane < k, 0.0, h1)
    second = jnp.where(lane < k, 0.0, jnp.where(lane < 3 * k, h2, h3))
    left = jnp.concatenate([first, second], axis=1).astype(BF16)
    y1, y2, y3 = parts
    zeros = jnp.zeros_like(y1)
    return dot(left, jnp.concatenate([zeros, y1, y2, y3, zeros, y1, y2, y1], axis=0), NN)


def rows_kernel(index_ref, near_ref, far_ref, stamps_ref, o_ref):
    total = jnp.zeros(o_ref.shape, F32)
    pix = BLOCKS - PLACE
    m = near_ref.shape[1] * 2 // pix
    for j in range(pix):
        ref = near_ref if j * m < near_ref.shape[1] else far_ref
        at = j * m % near_ref.shape[1]
        stamps = stamps_ref[:, pl.ds(pl.multiple_of(index_ref[PLACE + j] * m, LANES), m)]
        total += dot(ref[:, at : at + m], stamps, NT)
    o_ref[...] = total.astype(BF16)


def basis_kernel(pix, samp, p0_ref, p_ref, q_ref):
    k, n = p0_ref.shape
    m = n // (pix * samp)
    per = LANES // m
    lane = lax.broadcasted_iota(jnp.int32, (k, LANES), 1)
    for to in range(n // LANES):
        block = jnp.zeros((k, LANES), F32)
        for j in range(per):
            p, s = divmod(to * per + j, samp)
            group, slot = divmod(s * pix + p, per)
            part = p0_ref[:, group * LANES : (group + 1) * LANES].astype(F32)
            part = pltpu.roll(part, (j - slot) * m % LANES, 1) if j != slot else part
            block = jnp.where(lane // m == j, part, block)
        p_ref[:, to * LANES : (to + 1) * LANES] = block.astype(BF16)
    p0 = p_ref[...]
    parts = (p0, jnp.zeros_like(p0), jnp.zeros_like(p0))
    q = apply_lower(inverse_lower(gram_of(parts, p0)), parts)
    q_ref[...] = jnp.where(lax.broadcasted_iota(jnp.int32, q.shape, 0) < RANK, q, 0.0)


def factors_kernel(own_ref, other_ref, q_ref, left, right):
    k = q_ref.shape[0]
    q = q_ref[...]
    zeros = jnp.zeros(q.shape, BF16)
    q1, q2, q3 = split3(q)
    qs = jnp.concatenate([q1, q2, q3], axis=0)
    w = jnp.zeros(q.shape, F32)
    for ref in (own_ref, other_ref):
        t3 = dot(qs, ref[...], NN)
        ts = split3(t3[:k] + t3[k : 2 * k] + t3[2 * k :])
        w3 = dot(jnp.concatenate(ts, axis=0), ref[...], NT)
        w += w3[:k] + w3[k : 2 * k] + w3[2 * k :]
    ws = jnp.concatenate(list(split3(w)) + [zeros], axis=0)
    m = lane_sum3(dot(q1, ws, NT) + dot(q2, ws, NT) + dot(q3, ws, NT), k)
    m = jnp.where(lax.broadcasted_iota(jnp.int32, m.shape, 1) < k, m, 0.0)
    m = pltpu.roll(m, k, 1) + pltpu.roll(m, 2 * k, 1) + pltpu.roll(m, 3 * k, 1)
    w1, w2, w3 = split3(w - 0.5 * apply_lower(m, (q1, q2, q3)))
    q1, q2, q3, w1, w2, w3 = [part[:RANK] for part in (q1, q2, q3, w1, w2, w3)]
    left[...] = jnp.concatenate([q1, w1, q1, w1, q1, w1, q2, w2, q2, w2, q3, w3], axis=0)
    right[...] = jnp.concatenate([w1, q1, w2, q2, w3, q3, w1, q1, w2, q2, w1, q1], axis=0)


def form_rows(first, core, own_ref, other_ref, left, right, out_refs, window, right_win):
    n, px = own_ref.shape
    rows, cut = out_refs[0].shape
    width = n // 2
    bs = cut + out_refs[1].shape[1] - width
    nb = n // bs
    for b in range(window.shape[0] // bs):
        at = pl.multiple_of(lax.rem(first + b, nb) * bs, bs)
        window[b * bs : (b + 1) * bs, :px] = own_ref[pl.ds(at, bs), :]
        window[b * bs : (b + 1) * bs, px:] = other_ref[pl.ds(at, bs), :]
        right_win[:, b * bs : (b + 1) * bs] = right[:, pl.ds(at, bs)]
    lane = lax.broadcasted_iota(jnp.int32, (bs, bs), 1)
    eye = lax.broadcasted_iota(jnp.int32, (bs, bs), 0) == lane
    step = STEP * bs
    for i in range(rows // bs):
        if i % STEP == 0:
            at = pl.multiple_of((first + i) * bs, bs)
            lo, end = i * bs, i * bs + step + width
            wide = dot(window[lo : lo + step, :], window[lo:end, :], NT)
            wide -= dot(left[:, pl.ds(at, step)], right_win[:, lo:end], TN)
        off = i % STEP * bs
        to = i * bs
        s = wide[off : off + bs, off : off + width + bs]
        corner = s[:, :bs]
        diagonal = jnp.sum(jnp.where(eye, corner, 0.0), axis=0, keepdims=True)
        out_refs[0][to : to + bs, :bs] = jnp.where(eye, 0.0, corner).astype(BF16)
        out_refs[0][to : to + bs, bs:] = s[:, bs:cut].astype(BF16)
        out_refs[1][to : to + bs, : width - cut] = s[:, cut:width].astype(BF16)
        last = s[:, width:]
        low = last[HALF:]
        last = jnp.where(core == 0, last, jnp.concatenate([low, pltpu.roll(low, HALF, 1)], axis=0))
        side = [jnp.zeros((HALF, bs), F32)]
        for g, d in enumerate(split3(diagonal)):
            w = right_win[2 * g * RANK : (2 * g + 1) * RANK, to : to + bs]
            side.append(w.astype(F32))
            side.append(jnp.broadcast_to(d.astype(F32), (GROUP - RANK, bs)))
        side.append(jnp.zeros((bs - HALF - 3 * GROUP, bs), F32))
        side = jnp.concatenate(side, axis=0).T
        last = jnp.where(lane < HALF, last, side)
        out_refs[1][to : to + bs, width - cut :] = last.astype(BF16)


def form_kernel(slot, at_ref, own_ref, other_ref, left, right, out_0, out_1, *wins):
    outs = (out_0, out_1)
    form_rows(at_ref[slot], at_ref[CORE], own_ref, other_ref, left, right, outs, *wins)


def add_kernel(slots, special, at_ref, *refs):
    shares, o_refs = refs[: -len(slots)], refs[-len(slots) :]
    width = shares[0].shape[1] - (LANES if special else 0)
    for slot, o_ref in zip(slots, o_refs):
        h = o_ref.shape[0]
        at = 0 if slot is None else pl.multiple_of(at_ref[slot] * h, h)
        parts = [ref[pl.ds(at, h), :].astype(F32) for ref in shares]
        o_ref[:, :width] = sum(part[:, :width] for part in parts).astype(BF16)
        if not special:
            continue
        last = [part[:, width:] for part in parts]
        x = sum(lane_sum3(part, GROUP) for part in last)
        lane = lax.broadcasted_iota(jnp.int32, x.shape, 1) - HALF
        h1, h2, h3 = [part.astype(F32) for part in split3(x)]
        packed = jnp.where(lane < 2 * GROUP, pltpu.roll(h2, GROUP, 1), pltpu.roll(h3, 2 * GROUP, 1))
        packed = jnp.where(lane < GROUP, h1, packed)
        packed = jnp.where(lane < 3 * GROUP, packed, 0.0)
        o_ref[:, width:] = jnp.where(lane < 0, sum(last), packed).astype(BF16)


def add_shares(index, special, shares, slots=()):
    rows, lanes = shares[0].shape
    shape = jax.ShapeDtypeStruct((rows // max(len(slots), 1), lanes), BF16)
    slots = slots or (None,)
    return kernel_call(
        functools.partial(add_kernel, slots, special),
        (shape,) * len(slots),
        in_specs=[smem()] + vmem(len(shares)),
        out_specs=tuple(vmem(len(slots))),
    )(index, *shares)


def unpack(offset, index_ref, share_refs, q_ref, full, u, v, diag):
    n = q_ref.shape[1]
    width = n // 2
    cut = share_refs[0].shape[1]
    bs = cut + share_refs[1].shape[1] - width
    nb = n // bs
    lane = lax.broadcasted_iota(jnp.int32, (bs, bs), 1)

    def one(r, _):
        i = index_ref[r + offset]
        frm = pl.multiple_of(r * bs, bs)
        to = pl.multiple_of(i * bs, bs)
        for d in range(nb // 2):
            ref, col = (share_refs[0], d * bs) if d * bs < cut else (share_refs[1], d * bs - cut)
            part = ref[pl.ds(frm, bs), col : col + bs]
            at = pl.multiple_of(lax.rem(i + d, nb) * bs, bs)
            full[pl.ds(to, bs), pl.ds(at, bs)] = part
            if d:
                full[pl.ds(at, bs), pl.ds(to, bs)] = part.T
        at = pl.multiple_of(lax.rem(i + nb // 2, nb) * bs, bs)
        last = share_refs[1][pl.ds(frm, bs), width - cut :].astype(F32)

        @pl.when(i < nb // 2)
        def _():
            old = full[pl.ds(to, bs), pl.ds(at, bs)].astype(F32)
            full[pl.ds(to, bs), pl.ds(at, bs)] = jnp.where(lane < HALF, last, old).astype(BF16)
            full[pl.ds(at, HALF), pl.ds(to, bs)] = last.T[:HALF].astype(BF16)

        @pl.when(i >= nb // 2)
        def _():
            low = jnp.where(lane[:HALF] < HALF, last[:HALF], pltpu.roll(last[HALF:], HALF, 1))
            full[pl.ds(pl.multiple_of(to + HALF, HALF), HALF), pl.ds(at, bs)] = low.astype(BF16)
            old = full[pl.ds(at, bs), pl.ds(to, bs)].astype(F32)
            new = jnp.concatenate([low, low], axis=0).T
            full[pl.ds(at, bs), pl.ds(to, bs)] = jnp.where(lane < HALF, old, new).astype(BF16)

        side = last.T[HALF:]
        w, d = side[:RANK], side[RANK : RANK + 1]
        for g in (1, 2):
            w = w + pltpu.roll(side, HALF - g * GROUP, 0)[:RANK]
            d = d + side[g * GROUP + RANK : g * GROUP + RANK + 1]
        diag[:, pl.ds(to, bs)] = jnp.broadcast_to(d, (diag.shape[0], bs))
        q = q_ref[:RANK, pl.ds(to, bs)]
        us = [part.astype(F32) for part in split3(jnp.concatenate([w, q], axis=0))]
        us.append(jnp.zeros((bs - 6 * RANK, bs), F32))
        u[pl.ds(to, bs), :] = jnp.concatenate(us, axis=0).T.astype(BF16)
        v1, v2, v3 = split3(jnp.concatenate([q, w], axis=0))
        v[:, pl.ds(to, bs)] = jnp.concatenate([v1, v2, v3, v1, v2, v1], axis=0)
        return 0

    lax.fori_loop(0, share_refs[0].shape[0] // bs, one, 0)


def unpack_kernel(offsets, index_ref, *refs):
    q_ref = refs[2 * len(offsets)]
    for i, offset in enumerate(offsets):
        unpack(offset, index_ref, refs[2 * i : 2 * i + 2], q_ref, *refs[-4:])


def iterate_kernel(offset, index_ref, far_0, far_1, q_ref, p0_ref, *refs):
    p_ref, inv_ref, full, u, v, diag = refs[4:]
    k, _ = q_ref.shape
    unpack(offset, index_ref, (far_0, far_1), q_ref, full, u, v, diag)
    lane = lax.broadcasted_iota(jnp.int32, (k, LANES), 1)

    def product(p):
        t = dot(p, u[...], NN)
        t = t + pltpu.roll(t, 4 * RANK, 1)
        t = t + pltpu.roll(t, 2 * RANK, 1)
        h1, h2, h3 = [h.astype(F32) for h in split3(t)]
        ts = jnp.concatenate(
            [jnp.where(lane < 6 * RANK, h1, h2), jnp.where(lane < 2 * RANK, h2, h3)[:, :HALF]], axis=1
        ).astype(BF16)
        y = dot(p, full[...], NN) + dot(ts, v[...], NN) + p.astype(F32) * diag[0:1, :]
        return split3(y)

    def sweep(step, p):
        parts = product(p)
        return apply_lower(inverse_lower(gram_of(parts, p)), parts).astype(BF16)

    p = lax.fori_loop(0, ITERS - 1, sweep, p0_ref[...])
    p_ref[...] = p
    inv_ref[...] = inverse_lower(gram_of(product(p), p))


def finish_kernel(scale, p_ref, inv_ref, block_ref, o_ref):
    back = dot(p_ref[...], block_ref[...], NN)
    o_ref[...] = (apply_lower(inv_ref[...], split3(back)) * scale).astype(BF16)


def flip(x, axes, perm):
    return lax.ppermute(x, axes, perm)


def ordered(own, recv, bit, axis=0):
    return jnp.where(
        bit == 0,
        jnp.concatenate([own, recv], axis=axis),
        jnp.concatenate([recv, own], axis=axis),
    )


def sample_space(stamps, start_panel):
    pix = lax.axis_size("pix")
    samp = lax.axis_size("samp")
    n = stamps.shape[0] * pix * samp
    k = start_panel.shape[1]
    scale = math.sqrt(start_panel.shape[0] * pix)
    p = lax.axis_index("pix")
    s = lax.axis_index("samp")
    xor_pix = lambda b: [(i, i ^ b) for i in range(pix)]
    xor_samp = lambda b: [(i, i ^ b) for i in range(samp)]

    core = p & 1
    x, y = (p >> 1) & 1, (p >> 2) & 1
    z0, z1 = s & 1, (s >> 1) & 1

    low = start_panel.astype(BF16).T
    for b in (2, 4):
        low = jnp.concatenate([low, flip(low, "pix", xor_pix(b))], axis=1)
    far = flip(low, "pix", xor_pix(1))
    bit_a = jnp.where(core == 0, x, y)
    bit_b = jnp.where(core == 0, y, x)
    bs = 2 * stamps.shape[0]
    nb = n // bs
    at = jnp.arange(pix, dtype=jnp.int32)
    place = p ^ (((at & 1) << 1) | ((at & 2) << 1) | (at >> 2))
    at = jnp.arange(nb, dtype=jnp.int32)
    c_of = core ^ ((at >> 3) & 1)
    a_of = jnp.where(c_of == 0, x, y) ^ ((at >> 2) & 1)
    b_of = jnp.where(c_of == 0, y, x) ^ ((at >> 1) & 1)
    order = c_of * 8 + a_of * 4 + b_of * 2 + (z0 ^ (at & 1))
    pairs = [
        (core * 4 + half * 2 + quarter) * (nb // 8)
        for half in (1 - bit_a, bit_a)
        for quarter in (1 - bit_b, bit_b)
    ]
    pairs += [1 - z0, z0, core, 0]
    index = jnp.concatenate([jnp.stack([jnp.int32(i) for i in pairs]), place, order]).astype(jnp.int32)

    block = lax.all_to_all(stamps, ("pix", "samp"), split_axis=1, concat_axis=0, tiled=True)

    proj = kernel_call(
        rows_kernel,
        jax.ShapeDtypeStruct((k, stamps.shape[0]), BF16),
        in_specs=[smem()] + vmem(3),
        out_specs=vmem()[0],
    )(index, low, far, stamps)
    for b in (1, 2, 4):
        proj = ordered(proj, flip(proj, "pix", xor_pix(b)), p & b, axis=1)
    for b in (1, 2):
        proj = ordered(proj, flip(proj, "samp", xor_samp(b)), s & b, axis=1)
    proj, q = kernel_call(
        functools.partial(basis_kernel, pix, samp),
        (jax.ShapeDtypeStruct((k, n), BF16), jax.ShapeDtypeStruct((k, n), F32)),
        in_specs=vmem(),
        out_specs=tuple(vmem(2)),
    )(proj)

    first = [(i, i ^ (2 if i % 2 == 0 else 4)) for i in range(pix)]
    second = [(i, i ^ (4 if i % 2 == 0 else 2)) for i in range(pix)]
    other = flip(block, "pix", xor_pix(1))
    px = block.shape[1]
    width = n // 2 + bs
    rows = n // 8
    window = rows - bs + width
    cut = (nb // 4 + 1) * bs
    pieces = tuple(jax.ShapeDtypeStruct((rows, c), BF16) for c in (cut, width - cut))
    stack = jax.ShapeDtypeStruct((12 * RANK, n), BF16)
    left, right = kernel_call(
        factors_kernel,
        (stack, stack),
        in_specs=vmem(3),
        out_specs=tuple(vmem(2)),
        scratch_mib=12,
    )(block, other, q)

    def form(quarter):
        return kernel_call(
            functools.partial(form_kernel, QUARTERS + quarter),
            pieces,
            in_specs=[smem()] + vmem(4),
            out_specs=tuple(vmem(2)),
            scratch_mib=12,
            scratch_shapes=[pltpu.VMEM((window, 2 * px), BF16), pltpu.VMEM((12 * RANK, window), BF16)],
        )(index, block, other, left, right)

    sent = [form(0), form(1)]
    held = [form(2), form(3)]
    swap = xor_pix(1)
    near, far, over_a, far_a, over_ab, far_ab = ([None, None] for _ in range(6))
    for e in (0, 1):
        add = functools.partial(add_shares, index, e == 1)
        passed, kept = [flip(sent[i][e], "pix", first) for i in (0, 1)]
        (send,) = add((held[0][e], passed))
        recv = flip(send, "pix", second)
        send, keep = add((held[1][e], kept, recv), (HALVES, HALVES + 1))
        (share,) = add((keep, flip(send, "samp", xor_samp(1))))
        (share,) = add((share, flip(share, "samp", xor_samp(2))))

        share = jnp.concatenate([share, flip(share, "samp", xor_samp(1))], axis=0)
        over_a[e] = flip(share, "pix", first)
        over_b = flip(share, "pix", second)
        over_ab[e] = flip(over_b, "pix", first)
        near[e] = jnp.concatenate([share, over_b], axis=0)
        far[e], far_a[e], far_ab[e] = [flip(t[e], "pix", swap) for t in (near, over_a, over_ab)]
    parts = (
        jax.ShapeDtypeStruct((n, n), BF16),
        jax.ShapeDtypeStruct((n, bs), BF16),
        jax.ShapeDtypeStruct((12 * RANK, n), BF16),
        jax.ShapeDtypeStruct((8, n), F32),
    )
    eighth = nb // 8
    now = kernel_call(
        functools.partial(unpack_kernel, (BLOCKS, BLOCKS + 4 * eighth)),
        parts,
        in_specs=[smem()] + vmem(5),
        out_specs=tuple(vmem(4)),
        scratch_mib=4,
    )(index, *near, *far, q)
    offsets = [BLOCKS + i * eighth for i in (2, 6, 3)]
    now = kernel_call(
        functools.partial(unpack_kernel, offsets),
        parts,
        in_specs=[smem()] + vmem(11),
        out_specs=tuple(vmem(4)),
        input_output_aliases={8 + i: i for i in range(4)},
        scratch_mib=4,
    )(index, *over_a, *far_a, *over_ab, q, *now)
    proj, inv = kernel_call(
        functools.partial(iterate_kernel, BLOCKS + 7 * eighth),
        (jax.ShapeDtypeStruct((k, n), BF16), jax.ShapeDtypeStruct((k, LANES), F32)) + parts,
        in_specs=[smem()] + vmem(8),
        out_specs=tuple(vmem(6)),
        input_output_aliases={5 + i: 2 + i for i in range(4)},
        scratch_mib=12,
    )(index, *far_ab, q, proj, *now)[:2]

    mine = kernel_call(
        functools.partial(finish_kernel, scale),
        jax.ShapeDtypeStruct((k, px), BF16),
        in_specs=vmem(3),
        out_specs=vmem()[0],
    )(proj, inv, block)
    for b in (2, 1):
        mine = jnp.concatenate([mine, flip(mine, "samp", xor_samp(b))], axis=1)
    parts = [mine[:, i * px : (i + 1) * px] for i in range(samp)]
    by_distance = {0: parts[0], 2: parts[1], 1: parts[2], 3: parts[3]}
    swap0 = [jnp.where(z0 == 0, by_distance[i], by_distance[i ^ 1]) for i in range(samp)]
    swap1 = [jnp.where(z1 == 0, swap0[i], swap0[i ^ 2]) for i in range(samp)]
    return jnp.concatenate(swap1, axis=1).astype(F32).T


def solution(mesh):
    pix, samp = mesh.shape["pix"], mesh.shape["samp"]

    def local(stamps, start_panel):
        n = stamps.shape[0] * pix * samp
        k = start_panel.shape[1]
        if n <= SAMPLE_SPACE_LIMIT and (pix, samp) == (8, 4) and 4 * k == LANES:
            return sample_space(stamps, start_panel)
        return pixel_space(stamps, start_panel)

    return jax.shard_map(
        local,
        mesh=mesh,
        in_specs=(P(("samp", "pix"), None), P("pix", None)),
        out_specs=P("pix", None),
        check_vma=False,
    )
```

```python
import functools
import math

import jax
import jax.numpy as jnp
from jax import lax
from jax.experimental import pallas as pl
from jax.experimental.pallas import tpu as pltpu
from jax.sharding import PartitionSpec as P


ITERS = 10
LANES = 128
PANEL = 16
RANK = 16
GROUP = 20
HALF = 64
STEP = 2
QUARTERS, HALVES, CORE, PLACE, BLOCKS = 0, 4, 6, 8, 16
SAMPLE_SPACE_LIMIT = 4096
F32 = jnp.float32
BF16 = jnp.bfloat16

NN = (((1,), (0,)), ((), ()))
NT = (((1,), (1,)), ((), ()))
TN = (((0,), (0,)), ((), ()))


def orthonormal(back, gram):
    lower = jnp.linalg.cholesky(gram)
    return lax.linalg.triangular_solve(lower, back, left_side=False, lower=True, transpose_a=True)


def pixel_space(stamps, start_panel):
    block = lax.all_to_all(stamps, "pix", split_axis=1, concat_axis=0, tiled=True)

    def sweep(step, panel):
        partial_value = jnp.dot(block, panel.astype(BF16), preferred_element_type=F32)
        proj = lax.psum(partial_value.astype(BF16), "pix")
        back = lax.dot_general(block, proj, TN, preferred_element_type=F32)
        summed = lax.psum(back.astype(BF16), "samp").astype(F32)
        gram = lax.psum(jnp.dot(summed.T, summed, precision=lax.Precision.HIGHEST), "pix")
        return orthonormal(summed, gram)

    panel = lax.fori_loop(0, ITERS, sweep, start_panel)
    return panel * math.sqrt(start_panel.shape[0] * lax.axis_size("pix"))


def dot(a, b, dims):
    return lax.dot_general(a, b, dims, preferred_element_type=F32)


def split3(x):
    hi = x.astype(BF16)
    rest = x - hi.astype(F32)
    mid = rest.astype(BF16)
    lo = (rest - mid.astype(F32)).astype(BF16)
    return hi, mid, lo


def kernel_call(body, out_shape, in_specs=(), scratch_mib=8, **kw):
    single = not isinstance(out_shape, tuple)
    outs = tuple(pltpu.VMEM(o.shape, o.dtype) for o in ((out_shape,) if single else out_shape))
    call = pl.pallas_call(
        body,
        out_shape=outs[0] if single else outs,
        in_specs=in_specs,
        compiler_params=pltpu.CompilerParams(vmem_limit_bytes=scratch_mib << 20),
        **kw,
    )

    def place(x, spec):
        if spec.memory_space != pltpu.VMEM:
            return x
        return pltpu.with_memory_space_constraint(x, pltpu.VMEM)

    return lambda *args: call(*map(place, args, in_specs))


def vmem(n=1):
    return [pl.BlockSpec(memory_space=pltpu.VMEM)] * n


def smem():
    return pl.BlockSpec(memory_space=pltpu.SMEM)


def inverse_lower(gram):
    k = gram.shape[0]
    lane = lax.broadcasted_iota(jnp.int32, gram.shape, 1)
    row = lax.broadcasted_iota(jnp.int32, gram.shape, 0)
    m = jnp.where(lane < k, gram, jnp.where(lane % k == row, 1.0, 0.0))
    pivots = jnp.ones(gram.shape, F32)
    for start in range(0, k, PANEL):
        cols = [jnp.broadcast_to(m[:, j : j + 1], m.shape) for j in range(start, start + PANEL)]
        for t in range(PANEL):
            j = start + t
            pivot = cols[t][j : j + 1, :]
            factor = jnp.where(row > j, cols[t] * (1.0 / pivot), 0.0)
            pivots = jnp.where(row == j, pivot, pivots)
            for later in range(t + 1, PANEL):
                cols[later] = cols[later] - factor * cols[later][j : j + 1, :]
            m = m - factor * m[j : j + 1, :]
    return m * lax.rsqrt(pivots)


def lane_sum3(x, k):
    return x + pltpu.roll(x, LANES - k, 1) + pltpu.roll(x, LANES - 2 * k, 1)


def gram_of(parts, right):
    k = right.shape[0]
    wide = jnp.concatenate([right, jnp.zeros((3 * k, right.shape[1]), right.dtype)], axis=0)
    g = dot(jnp.concatenate(parts, axis=0), wide, NT)
    return g[:k] + g[k : 2 * k] + g[2 * k :]


def apply_lower(inv, parts):
    k = inv.shape[0]
    lane = lax.broadcasted_iota(jnp.int32, inv.shape, 1)
    h1, h2, h3 = [h.astype(F32) for h in split3(inv)]
    first = jnp.where(lane < k, 0.0, h1)
    second = jnp.where(lane < k, 0.0, jnp.where(lane < 3 * k, h2, h3))
    left = jnp.concatenate([first, second], axis=1).astype(BF16)
    y1, y2, y3 = parts
    zeros = jnp.zeros_like(y1)
    return dot(left, jnp.concatenate([zeros, y1, y2, y3, zeros, y1, y2, y1], axis=0), NN)


def rows_kernel(index_ref, near_ref, far_ref, stamps_ref, o_ref):
    total = jnp.zeros(o_ref.shape, F32)
    pix = BLOCKS - PLACE
    m = near_ref.shape[1] * 2 // pix
    for j in range(pix):
        ref = near_ref if j * m < near_ref.shape[1] else far_ref
        at = j * m % near_ref.shape[1]
        stamps = stamps_ref[:, pl.ds(pl.multiple_of(index_ref[PLACE + j] * m, LANES), m)]
        total += dot(ref[:, at : at + m], stamps, NT)
    o_ref[...] = total.astype(BF16)


def basis_kernel(pix, samp, p0_ref, p_ref, q_ref):
    k, n = p0_ref.shape
    m = n // (pix * samp)
    per = LANES // m
    lane = lax.broadcasted_iota(jnp.int32, (k, LANES), 1)
    for to in range(n // LANES):
        block = jnp.zeros((k, LANES), F32)
        for j in range(per):
            p, s = divmod(to * per + j, samp)
            group, slot = divmod(s * pix + p, per)
            part = p0_ref[:, group * LANES : (group + 1) * LANES].astype(F32)
            part = pltpu.roll(part, (j - slot) * m % LANES, 1) if j != slot else part
            block = jnp.where(lane // m == j, part, block)
        p_ref[:, to * LANES : (to + 1) * LANES] = block.astype(BF16)
    p0 = p_ref[...]
    parts = (p0, jnp.zeros_like(p0), jnp.zeros_like(p0))
    q = apply_lower(inverse_lower(gram_of(parts, p0)), parts)
    q_ref[...] = jnp.where(lax.broadcasted_iota(jnp.int32, q.shape, 0) < RANK, q, 0.0)


def factors_kernel(own_ref, other_ref, q_ref, left, right):
    k = q_ref.shape[0]
    q = q_ref[...]
    zeros = jnp.zeros(q.shape, BF16)
    q1, q2, q3 = split3(q)
    qs = jnp.concatenate([q1, q2, q3], axis=0)
    w = jnp.zeros(q.shape, F32)
    for ref in (own_ref, other_ref):
        t3 = dot(qs, ref[...], NN)
        ts = split3(t3[:k] + t3[k : 2 * k] + t3[2 * k :])
        w3 = dot(jnp.concatenate(ts, axis=0), ref[...], NT)
        w += w3[:k] + w3[k : 2 * k] + w3[2 * k :]
    ws = jnp.concatenate(list(split3(w)) + [zeros], axis=0)
    m = lane_sum3(dot(q1, ws, NT) + dot(q2, ws, NT) + dot(q3, ws, NT), k)
    m = jnp.where(lax.broadcasted_iota(jnp.int32, m.shape, 1) < k, m, 0.0)
    m = pltpu.roll(m, k, 1) + pltpu.roll(m, 2 * k, 1) + pltpu.roll(m, 3 * k, 1)
    w1, w2, w3 = split3(w - 0.5 * apply_lower(m, (q1, q2, q3)))
    q1, q2, q3, w1, w2, w3 = [part[:RANK] for part in (q1, q2, q3, w1, w2, w3)]
    left[...] = jnp.concatenate([q1, w1, q1, w1, q1, w1, q2, w2, q2, w2, q3, w3], axis=0)
    right[...] = jnp.concatenate([w1, q1, w2, q2, w3, q3, w1, q1, w2, q2, w1, q1], axis=0)


def form_rows(first, core, own_ref, other_ref, left, right, out_refs, window, right_win):
    n, px = own_ref.shape
    rows, cut = out_refs[0].shape
    width = n // 2
    bs = cut + out_refs[1].shape[1] - width
    nb = n // bs
    for b in range(window.shape[0] // bs):
        at = pl.multiple_of(lax.rem(first + b, nb) * bs, bs)
        window[b * bs : (b + 1) * bs, :px] = own_ref[pl.ds(at, bs), :]
        window[b * bs : (b + 1) * bs, px:] = other_ref[pl.ds(at, bs), :]
        right_win[:, b * bs : (b + 1) * bs] = right[:, pl.ds(at, bs)]
    lane = lax.broadcasted_iota(jnp.int32, (bs, bs), 1)
    eye = lax.broadcasted_iota(jnp.int32, (bs, bs), 0) == lane
    step = STEP * bs
    for i in range(rows // bs):
        if i % STEP == 0:
            at = pl.multiple_of((first + i) * bs, bs)
            lo, end = i * bs, i * bs + step + width
            wide = dot(window[lo : lo + step, :], window[lo:end, :], NT)
            wide -= dot(left[:, pl.ds(at, step)], right_win[:, lo:end], TN)
        off = i % STEP * bs
        to = i * bs
        s = wide[off : off + bs, off : off + width + bs]
        corner = s[:, :bs]
        diagonal = jnp.sum(jnp.where(eye, corner, 0.0), axis=0, keepdims=True)
        out_refs[0][to : to + bs, :bs] = jnp.where(eye, 0.0, corner).astype(BF16)
        out_refs[0][to : to + bs, bs:] = s[:, bs:cut].astype(BF16)
        out_refs[1][to : to + bs, : width - cut] = s[:, cut:width].astype(BF16)
        last = s[:, width:]
        low = last[HALF:]
        last = jnp.where(core == 0, last, jnp.concatenate([low, pltpu.roll(low, HALF, 1)], axis=0))
        side = [jnp.zeros((HALF, bs), F32)]
        for g, d in enumerate(split3(diagonal)):
            w = right_win[2 * g * RANK : (2 * g + 1) * RANK, to : to + bs]
            side.append(w.astype(F32))
            side.append(jnp.broadcast_to(d.astype(F32), (GROUP - RANK, bs)))
        side.append(jnp.zeros((bs - HALF - 3 * GROUP, bs), F32))
        side = jnp.concatenate(side, axis=0).T
        last = jnp.where(lane < HALF, last, side)
        out_refs[1][to : to + bs, width - cut :] = last.astype(BF16)


def form_kernel(slot, at_ref, own_ref, other_ref, left, right, out_0, out_1, *wins):
    outs = (out_0, out_1)
    form_rows(at_ref[slot], at_ref[CORE], own_ref, other_ref, left, right, outs, *wins)


def add_kernel(slots, special, at_ref, *refs):
    shares, o_refs = refs[: -len(slots)], refs[-len(slots) :]
    width = shares[0].shape[1] - (LANES if special else 0)
    for slot, o_ref in zip(slots, o_refs):
        h = o_ref.shape[0]
        at = 0 if slot is None else pl.multiple_of(at_ref[slot] * h, h)
        parts = [ref[pl.ds(at, h), :].astype(F32) for ref in shares]
        o_ref[:, :width] = sum(part[:, :width] for part in parts).astype(BF16)
        if not special:
            continue
        last = [part[:, width:] for part in parts]
        x = sum(lane_sum3(part, GROUP) for part in last)
        lane = lax.broadcasted_iota(jnp.int32, x.shape, 1) - HALF
        h1, h2, h3 = [part.astype(F32) for part in split3(x)]
        packed = jnp.where(lane < 2 * GROUP, pltpu.roll(h2, GROUP, 1), pltpu.roll(h3, 2 * GROUP, 1))
        packed = jnp.where(lane < GROUP, h1, packed)
        packed = jnp.where(lane < 3 * GROUP, packed, 0.0)
        o_ref[:, width:] = jnp.where(lane < 0, sum(last), packed).astype(BF16)


def add_shares(index, special, shares, slots=()):
    rows, lanes = shares[0].shape
    shape = jax.ShapeDtypeStruct((rows // max(len(slots), 1), lanes), BF16)
    slots = slots or (None,)
    return kernel_call(
        functools.partial(add_kernel, slots, special),
        (shape,) * len(slots),
        in_specs=[smem()] + vmem(len(shares)),
        out_specs=tuple(vmem(len(slots))),
    )(index, *shares)


def unpack(offset, index_ref, share_refs, q_ref, full, u, v, diag):
    n = q_ref.shape[1]
    width = n // 2
    cut = share_refs[0].shape[1]
    bs = cut + share_refs[1].shape[1] - width
    nb = n // bs
    lane = lax.broadcasted_iota(jnp.int32, (bs, bs), 1)

    def one(r, _):
        i = index_ref[r + offset]
        frm = pl.multiple_of(r * bs, bs)
        to = pl.multiple_of(i * bs, bs)
        for d in range(nb // 2):
            ref, col = (share_refs[0], d * bs) if d * bs < cut else (share_refs[1], d * bs - cut)
            part = ref[pl.ds(frm, bs), col : col + bs]
            at = pl.multiple_of(lax.rem(i + d, nb) * bs, bs)
            full[pl.ds(to, bs), pl.ds(at, bs)] = part
            if d:
                full[pl.ds(at, bs), pl.ds(to, bs)] = part.T
        at = pl.multiple_of(lax.rem(i + nb // 2, nb) * bs, bs)
        last = share_refs[1][pl.ds(frm, bs), width - cut :].astype(F32)

        @pl.when(i < nb // 2)
        def _():
            old = full[pl.ds(to, bs), pl.ds(at, bs)].astype(F32)
            full[pl.ds(to, bs), pl.ds(at, bs)] = jnp.where(lane < HALF, last, old).astype(BF16)
            full[pl.ds(at, HALF), pl.ds(to, bs)] = last.T[:HALF].astype(BF16)

        @pl.when(i >= nb // 2)
        def _():
            low = jnp.where(lane[:HALF] < HALF, last[:HALF], pltpu.roll(last[HALF:], HALF, 1))
            full[pl.ds(pl.multiple_of(to + HALF, HALF), HALF), pl.ds(at, bs)] = low.astype(BF16)
            old = full[pl.ds(at, bs), pl.ds(to, bs)].astype(F32)
            new = jnp.concatenate([low, low], axis=0).T
            full[pl.ds(at, bs), pl.ds(to, bs)] = jnp.where(lane < HALF, old, new).astype(BF16)

        side = last.T[HALF:]
        w, d = side[:RANK], side[RANK : RANK + 1]
        for g in (1, 2):
            w = w + pltpu.roll(side, HALF - g * GROUP, 0)[:RANK]
            d = d + side[g * GROUP + RANK : g * GROUP + RANK + 1]
        diag[:, pl.ds(to, bs)] = jnp.broadcast_to(d, (diag.shape[0], bs))
        q = q_ref[:RANK, pl.ds(to, bs)]
        us = [part.astype(F32) for part in split3(jnp.concatenate([w, q], axis=0))]
        us.append(jnp.zeros((bs - 6 * RANK, bs), F32))
        u[pl.ds(to, bs), :] = jnp.concatenate(us, axis=0).T.astype(BF16)
        v1, v2, v3 = split3(jnp.concatenate([q, w], axis=0))
        v[:, pl.ds(to, bs)] = jnp.concatenate([v1, v2, v3, v1, v2, v1], axis=0)
        return 0

    lax.fori_loop(0, share_refs[0].shape[0] // bs, one, 0)


def unpack_kernel(offsets, index_ref, *refs):
    q_ref = refs[2 * len(offsets)]
    for i, offset in enumerate(offsets):
        unpack(offset, index_ref, refs[2 * i : 2 * i + 2], q_ref, *refs[-4:])


def iterate_kernel(offset, index_ref, far_0, far_1, q_ref, p0_ref, *refs):
    p_ref, inv_ref, full, u, v, diag = refs[4:]
    k, _ = q_ref.shape
    unpack(offset, index_ref, (far_0, far_1), q_ref, full, u, v, diag)
    lane = lax.broadcasted_iota(jnp.int32, (k, LANES), 1)

    def product(p):
        t = dot(p, u[...], NN)
        t = t + pltpu.roll(t, 4 * RANK, 1)
        t = t + pltpu.roll(t, 2 * RANK, 1)
        h1, h2, h3 = [h.astype(F32) for h in split3(t)]
        ts = jnp.concatenate(
            [jnp.where(lane < 6 * RANK, h1, h2), jnp.where(lane < 2 * RANK, h2, h3)[:, :HALF]], axis=1
        ).astype(BF16)
        y = dot(p, full[...], NN) + dot(ts, v[...], NN) + p.astype(F32) * diag[0:1, :]
        return split3(y)

    def sweep(step, p):
        parts = product(p)
        return apply_lower(inverse_lower(gram_of(parts, p)), parts).astype(BF16)

    p = lax.fori_loop(0, ITERS - 1, sweep, p0_ref[...])
    p_ref[...] = p
    inv_ref[...] = inverse_lower(gram_of(product(p), p))


def finish_kernel(scale, p_ref, inv_ref, block_ref, o_ref):
    back = dot(p_ref[...], block_ref[...], NN)
    o_ref[...] = (apply_lower(inv_ref[...], split3(back)) * scale).astype(BF16)


def flip(x, axes, perm):
    return lax.ppermute(x, axes, perm)


def ordered(own, recv, bit, axis=0):
    return jnp.where(
        bit == 0,
        jnp.concatenate([own, recv], axis=axis),
        jnp.concatenate([recv, own], axis=axis),
    )


def sample_space(stamps, start_panel):
    pix = lax.axis_size("pix")
    samp = lax.axis_size("samp")
    n = stamps.shape[0] * pix * samp
    k = start_panel.shape[1]
    scale = math.sqrt(start_panel.shape[0] * pix)
    p = lax.axis_index("pix")
    s = lax.axis_index("samp")
    xor_pix = lambda b: [(i, i ^ b) for i in range(pix)]
    xor_samp = lambda b: [(i, i ^ b) for i in range(samp)]

    core = p & 1
    x, y = (p >> 1) & 1, (p >> 2) & 1
    z0, z1 = s & 1, (s >> 1) & 1

    low = start_panel.astype(BF16).T
    for b in (2, 4):
        low = jnp.concatenate([low, flip(low, "pix", xor_pix(b))], axis=1)
    far = flip(low, "pix", xor_pix(1))
    bit_a = jnp.where(core == 0, x, y)
    bit_b = jnp.where(core == 0, y, x)
    bs = 2 * stamps.shape[0]
    nb = n // bs
    at = jnp.arange(pix, dtype=jnp.int32)
    place = p ^ (((at & 1) << 1) | ((at & 2) << 1) | (at >> 2))
    at = jnp.arange(nb, dtype=jnp.int32)
    c_of = core ^ ((at >> 3) & 1)
    a_of = jnp.where(c_of == 0, x, y) ^ ((at >> 2) & 1)
    b_of = jnp.where(c_of == 0, y, x) ^ ((at >> 1) & 1)
    order = c_of * 8 + a_of * 4 + b_of * 2 + (z0 ^ (at & 1))
    pairs = [
        (core * 4 + half * 2 + quarter) * (nb // 8)
        for half in (1 - bit_a, bit_a)
        for quarter in (1 - bit_b, bit_b)
    ]
    pairs += [1 - z0, z0, core, 0]
    index = jnp.concatenate([jnp.stack([jnp.int32(i) for i in pairs]), place, order]).astype(jnp.int32)

    block = lax.all_to_all(stamps, ("pix", "samp"), split_axis=1, concat_axis=0, tiled=True)

    proj = kernel_call(
        rows_kernel,
        jax.ShapeDtypeStruct((k, stamps.shape[0]), BF16),
        in_specs=[smem()] + vmem(3),
        out_specs=vmem()[0],
    )(index, low, far, stamps)
    for b in (1, 2, 4):
        proj = ordered(proj, flip(proj, "pix", xor_pix(b)), p & b, axis=1)
    for b in (1, 2):
        proj = ordered(proj, flip(proj, "samp", xor_samp(b)), s & b, axis=1)
    proj, q = kernel_call(
        functools.partial(basis_kernel, pix, samp),
        (jax.ShapeDtypeStruct((k, n), BF16), jax.ShapeDtypeStruct((k, n), F32)),
        in_specs=vmem(),
        out_specs=tuple(vmem(2)),
    )(proj)

    first = [(i, i ^ (2 if i % 2 == 0 else 4)) for i in range(pix)]
    second = [(i, i ^ (4 if i % 2 == 0 else 2)) for i in range(pix)]
    other = flip(block, "pix", xor_pix(1))
    px = block.shape[1]
    width = n // 2 + bs
    rows = n // 8
    window = rows - bs + width
    cut = (nb // 4 + 1) * bs
    pieces = tuple(jax.ShapeDtypeStruct((rows, c), BF16) for c in (cut, width - cut))
    stack = jax.ShapeDtypeStruct((12 * RANK, n), BF16)
    left, right = kernel_call(
        factors_kernel,
        (stack, stack),
        in_specs=vmem(3),
        out_specs=tuple(vmem(2)),
        scratch_mib=12,
    )(block, other, q)

    def form(quarter):
        return kernel_call(
            functools.partial(form_kernel, QUARTERS + quarter),
            pieces,
            in_specs=[smem()] + vmem(4),
            out_specs=tuple(vmem(2)),
            scratch_mib=12,
            scratch_shapes=[pltpu.VMEM((window, 2 * px), BF16), pltpu.VMEM((12 * RANK, window), BF16)],
        )(index, block, other, left, right)

    sent = [form(0), form(1)]
    held = [form(2)]
    held.append(form(3))
    swap = xor_pix(1)
    near, far, over_a, far_a, over_ab, far_ab = ([None, None] for _ in range(6))
    for e in (0, 1):
        add = functools.partial(add_shares, index, e == 1)
        passed, kept = [flip(sent[i][e], "pix", first) for i in (0, 1)]
        (send,) = add((held[0][e], passed))
        recv = flip(send, "pix", second)
        send, keep = add((held[1][e], kept, recv), (HALVES, HALVES + 1))
        recv = flip(send, "samp", xor_samp(1))
        (share,) = add((keep, recv))
        recv = flip(share, "samp", xor_samp(2))
        (share,) = add((share, recv))

        recv = flip(share, "samp", xor_samp(1))
        share = jnp.concatenate([share, recv], axis=0)
        over_a[e] = flip(share, "pix", first)
        over_b = flip(share, "pix", second)
        over_ab[e] = flip(over_b, "pix", first)
        near[e] = jnp.concatenate([share, over_b], axis=0)
        far[e], far_a[e], far_ab[e] = [flip(t[e], "pix", swap) for t in (near, over_a, over_ab)]
    parts = (
        jax.ShapeDtypeStruct((n, n), BF16),
        jax.ShapeDtypeStruct((n, bs), BF16),
        jax.ShapeDtypeStruct((12 * RANK, n), BF16),
        jax.ShapeDtypeStruct((8, n), F32),
    )
    eighth = nb // 8
    now = kernel_call(
        functools.partial(unpack_kernel, (BLOCKS, BLOCKS + 4 * eighth)),
        parts,
        in_specs=[smem()] + vmem(5),
        out_specs=tuple(vmem(4)),
        scratch_mib=4,
    )(index, *near, *far, q)
    offsets = [BLOCKS + i * eighth for i in (2, 6, 3)]
    now = kernel_call(
        functools.partial(unpack_kernel, offsets),
        parts,
        in_specs=[smem()] + vmem(11),
        out_specs=tuple(vmem(4)),
        input_output_aliases={8 + i: i for i in range(4)},
        scratch_mib=4,
    )(index, *over_a, *far_a, *over_ab, q, *now)
    proj, inv = kernel_call(
        functools.partial(iterate_kernel, BLOCKS + 7 * eighth),
        (jax.ShapeDtypeStruct((k, n), BF16), jax.ShapeDtypeStruct((k, LANES), F32)) + parts,
        in_specs=[smem()] + vmem(8),
        out_specs=tuple(vmem(6)),
        input_output_aliases={5 + i: 2 + i for i in range(4)},
        scratch_mib=12,
    )(index, *far_ab, q, proj, *now)[:2]

    mine = kernel_call(
        functools.partial(finish_kernel, scale),
        jax.ShapeDtypeStruct((k, px), BF16),
        in_specs=vmem(3),
        out_specs=vmem()[0],
    )(proj, inv, block)
    for b in (2, 1):
        mine = jnp.concatenate([mine, flip(mine, "samp", xor_samp(b))], axis=1)
    parts = [mine[:, i * px : (i + 1) * px] for i in range(samp)]
    by_distance = {0: parts[0], 2: parts[1], 1: parts[2], 3: parts[3]}
    swap0 = [jnp.where(z0 == 0, by_distance[i], by_distance[i ^ 1]) for i in range(samp)]
    swap1 = [jnp.where(z1 == 0, swap0[i], swap0[i ^ 2]) for i in range(samp)]
    return jnp.concatenate(swap1, axis=1).astype(F32).T


def solution(mesh):
    pix, samp = mesh.shape["pix"], mesh.shape["samp"]

    def local(stamps, start_panel):
        n = stamps.shape[0] * pix * samp
        k = start_panel.shape[1]
        if n <= SAMPLE_SPACE_LIMIT and (pix, samp) == (8, 4) and 4 * k == LANES:
            return sample_space(stamps, start_panel)
        return pixel_space(stamps, start_panel)

    return jax.shard_map(
        local,
        mesh=mesh,
        in_specs=(P(("samp", "pix"), None), P("pix", None)),
        out_specs=P("pix", None),
        check_vma=False,
    )
```

```python
import functools
import math

import jax
import jax.numpy as jnp
from jax import lax
from jax.experimental import pallas as pl
from jax.experimental.pallas import tpu as pltpu
from jax.sharding import PartitionSpec as P


ITERS = 10
LANES = 128
PANEL = 16
RANK = 16
GROUP = 20
HALF = 64
STEP = 2
QUARTERS, HALVES, CORE, PLACE, BLOCKS = 0, 4, 6, 8, 16
SAMPLE_SPACE_LIMIT = 4096
F32 = jnp.float32
BF16 = jnp.bfloat16

NN = (((1,), (0,)), ((), ()))
NT = (((1,), (1,)), ((), ()))
TN = (((0,), (0,)), ((), ()))


def orthonormal(back, gram):
    lower = jnp.linalg.cholesky(gram)
    return lax.linalg.triangular_solve(lower, back, left_side=False, lower=True, transpose_a=True)


def pixel_space(stamps, start_panel):
    block = lax.all_to_all(stamps, "pix", split_axis=1, concat_axis=0, tiled=True)

    def sweep(step, panel):
        partial_value = jnp.dot(block, panel.astype(BF16), preferred_element_type=F32)
        proj = lax.psum(partial_value.astype(BF16), "pix")
        back = lax.dot_general(block, proj, TN, preferred_element_type=F32)
        summed = lax.psum(back.astype(BF16), "samp").astype(F32)
        gram = lax.psum(jnp.dot(summed.T, summed, precision=lax.Precision.HIGHEST), "pix")
        return orthonormal(summed, gram)

    panel = lax.fori_loop(0, ITERS, sweep, start_panel)
    return panel * math.sqrt(start_panel.shape[0] * lax.axis_size("pix"))


def dot(a, b, dims):
    return lax.dot_general(a, b, dims, preferred_element_type=F32)


def split3(x):
    hi = x.astype(BF16)
    rest = x - hi.astype(F32)
    mid = rest.astype(BF16)
    lo = (rest - mid.astype(F32)).astype(BF16)
    return hi, mid, lo


def kernel_call(body, out_shape, in_specs=(), scratch_mib=8, **kw):
    single = not isinstance(out_shape, tuple)
    outs = tuple(pltpu.VMEM(o.shape, o.dtype) for o in ((out_shape,) if single else out_shape))
    call = pl.pallas_call(
        body,
        out_shape=outs[0] if single else outs,
        in_specs=in_specs,
        compiler_params=pltpu.CompilerParams(vmem_limit_bytes=scratch_mib << 20),
        **kw,
    )

    def place(x, spec):
        if spec.memory_space != pltpu.VMEM:
            return x
        return pltpu.with_memory_space_constraint(x, pltpu.VMEM)

    return lambda *args: call(*map(place, args, in_specs))


def vmem(n=1):
    return [pl.BlockSpec(memory_space=pltpu.VMEM)] * n


def smem():
    return pl.BlockSpec(memory_space=pltpu.SMEM)


def inverse_lower(gram):
    k = gram.shape[0]
    lane = lax.broadcasted_iota(jnp.int32, gram.shape, 1)
    row = lax.broadcasted_iota(jnp.int32, gram.shape, 0)
    m = jnp.where(lane < k, gram, jnp.where(lane % k == row, 1.0, 0.0))
    pivots = jnp.ones(gram.shape, F32)
    for start in range(0, k, PANEL):
        cols = [jnp.broadcast_to(m[:, j : j + 1], m.shape) for j in range(start, start + PANEL)]
        for t in range(PANEL):
            j = start + t
            pivot = cols[t][j : j + 1, :]
            factor = jnp.where(row > j, cols[t] * (1.0 / pivot), 0.0)
            pivots = jnp.where(row == j, pivot, pivots)
            for later in range(t + 1, PANEL):
                cols[later] = cols[later] - factor * cols[later][j : j + 1, :]
            m = m - factor * m[j : j + 1, :]
    return m * lax.rsqrt(pivots)


def lane_sum3(x, k):
    return x + pltpu.roll(x, LANES - k, 1) + pltpu.roll(x, LANES - 2 * k, 1)


def gram_of(parts, right):
    k = right.shape[0]
    wide = jnp.concatenate([right, jnp.zeros((3 * k, right.shape[1]), right.dtype)], axis=0)
    g = dot(jnp.concatenate(parts, axis=0), wide, NT)
    return g[:k] + g[k : 2 * k] + g[2 * k :]


def apply_lower(inv, parts):
    k = inv.shape[0]
    lane = lax.broadcasted_iota(jnp.int32, inv.shape, 1)
    h1, h2, h3 = [h.astype(F32) for h in split3(inv)]
    first = jnp.where(lane < k, 0.0, h1)
    second = jnp.where(lane < k, 0.0, jnp.where(lane < 3 * k, h2, h3))
    left = jnp.concatenate([first, second], axis=1).astype(BF16)
    y1, y2, y3 = parts
    zeros = jnp.zeros_like(y1)
    return dot(left, jnp.concatenate([zeros, y1, y2, y3, zeros, y1, y2, y1], axis=0), NN)


def rows_kernel(index_ref, near_ref, far_ref, stamps_ref, o_ref):
    total = jnp.zeros(o_ref.shape, F32)
    pix = BLOCKS - PLACE
    m = near_ref.shape[1] * 2 // pix
    for j in range(pix):
        ref = near_ref if j * m < near_ref.shape[1] else far_ref
        at = j * m % near_ref.shape[1]
        stamps = stamps_ref[:, pl.ds(pl.multiple_of(index_ref[PLACE + j] * m, LANES), m)]
        total += dot(ref[:, at : at + m], stamps, NT)
    o_ref[...] = total.astype(BF16)


def basis_kernel(pix, samp, p0_ref, p_ref, q_ref):
    k, n = p0_ref.shape
    m = n // (pix * samp)
    per = LANES // m
    lane = lax.broadcasted_iota(jnp.int32, (k, LANES), 1)
    for to in range(n // LANES):
        block = jnp.zeros((k, LANES), F32)
        for j in range(per):
            p, s = divmod(to * per + j, samp)
            group, slot = divmod(s * pix + p, per)
            part = p0_ref[:, group * LANES : (group + 1) * LANES].astype(F32)
            part = pltpu.roll(part, (j - slot) * m % LANES, 1) if j != slot else part
            block = jnp.where(lane // m == j, part, block)
        p_ref[:, to * LANES : (to + 1) * LANES] = block.astype(BF16)
    p0 = p_ref[...]
    parts = (p0, jnp.zeros_like(p0), jnp.zeros_like(p0))
    q = apply_lower(inverse_lower(gram_of(parts, p0)), parts)
    q_ref[...] = jnp.where(lax.broadcasted_iota(jnp.int32, q.shape, 0) < RANK, q, 0.0)


def factors_kernel(own_ref, other_ref, q_ref, left, right):
    k = q_ref.shape[0]
    q = q_ref[...]
    zeros = jnp.zeros(q.shape, BF16)
    q1, q2, q3 = split3(q)
    qs = jnp.concatenate([q1, q2, q3], axis=0)
    w = jnp.zeros(q.shape, F32)
    for ref in (own_ref, other_ref):
        t3 = dot(qs, ref[...], NN)
        ts = split3(t3[:k] + t3[k : 2 * k] + t3[2 * k :])
        w3 = dot(jnp.concatenate(ts, axis=0), ref[...], NT)
        w += w3[:k] + w3[k : 2 * k] + w3[2 * k :]
    ws = jnp.concatenate(list(split3(w)) + [zeros], axis=0)
    m = lane_sum3(dot(q1, ws, NT) + dot(q2, ws, NT) + dot(q3, ws, NT), k)
    m = jnp.where(lax.broadcasted_iota(jnp.int32, m.shape, 1) < k, m, 0.0)
    m = pltpu.roll(m, k, 1) + pltpu.roll(m, 2 * k, 1) + pltpu.roll(m, 3 * k, 1)
    w1, w2, w3 = split3(w - 0.5 * apply_lower(m, (q1, q2, q3)))
    q1, q2, q3, w1, w2, w3 = [part[:RANK] for part in (q1, q2, q3, w1, w2, w3)]
    left[...] = jnp.concatenate([q1, w1, q1, w1, q1, w1, q2, w2, q2, w2, q3, w3], axis=0)
    right[...] = jnp.concatenate([w1, q1, w2, q2, w3, q3, w1, q1, w2, q2, w1, q1], axis=0)


def form_rows(first, core, own_ref, other_ref, left, right, out_refs, window, right_win):
    n, px = own_ref.shape
    rows, cut = out_refs[0].shape
    width = n // 2
    bs = cut + out_refs[1].shape[1] - width
    nb = n // bs
    for b in range(window.shape[0] // bs):
        at = pl.multiple_of(lax.rem(first + b, nb) * bs, bs)
        window[b * bs : (b + 1) * bs, :px] = own_ref[pl.ds(at, bs), :]
        window[b * bs : (b + 1) * bs, px:] = other_ref[pl.ds(at, bs), :]
        right_win[:, b * bs : (b + 1) * bs] = right[:, pl.ds(at, bs)]
    lane = lax.broadcasted_iota(jnp.int32, (bs, bs), 1)
    eye = lax.broadcasted_iota(jnp.int32, (bs, bs), 0) == lane
    step = STEP * bs
    for i in range(rows // bs):
        if i % STEP == 0:
            at = pl.multiple_of((first + i) * bs, bs)
            lo, end = i * bs, i * bs + step + width
            wide = dot(window[lo : lo + step, :], window[lo:end, :], NT)
            wide -= dot(left[:, pl.ds(at, step)], right_win[:, lo:end], TN)
        off = i % STEP * bs
        to = i * bs
        s = wide[off : off + bs, off : off + width + bs]
        corner = s[:, :bs]
        diagonal = jnp.sum(jnp.where(eye, corner, 0.0), axis=0, keepdims=True)
        out_refs[0][to : to + bs, :bs] = jnp.where(eye, 0.0, corner).astype(BF16)
        out_refs[0][to : to + bs, bs:] = s[:, bs:cut].astype(BF16)
        out_refs[1][to : to + bs, : width - cut] = s[:, cut:width].astype(BF16)
        last = s[:, width:]
        low = last[HALF:]
        last = jnp.where(core == 0, last, jnp.concatenate([low, pltpu.roll(low, HALF, 1)], axis=0))
        side = [jnp.zeros((HALF, bs), F32)]
        for g, d in enumerate(split3(diagonal)):
            w = right_win[2 * g * RANK : (2 * g + 1) * RANK, to : to + bs]
            side.append(w.astype(F32))
            side.append(jnp.broadcast_to(d.astype(F32), (GROUP - RANK, bs)))
        side.append(jnp.zeros((bs - HALF - 3 * GROUP, bs), F32))
        side = jnp.concatenate(side, axis=0).T
        last = jnp.where(lane < HALF, last, side)
        out_refs[1][to : to + bs, width - cut :] = last.astype(BF16)


def form_kernel(slot, at_ref, own_ref, other_ref, left, right, out_0, out_1, *wins):
    outs = (out_0, out_1)
    form_rows(at_ref[slot], at_ref[CORE], own_ref, other_ref, left, right, outs, *wins)


def add_kernel(slots, special, at_ref, *refs):
    shares, o_refs = refs[: -len(slots)], refs[-len(slots) :]
    width = shares[0].shape[1] - (LANES if special else 0)
    for slot, o_ref in zip(slots, o_refs):
        h = o_ref.shape[0]
        at = 0 if slot is None else pl.multiple_of(at_ref[slot] * h, h)
        parts = [ref[pl.ds(at, h), :].astype(F32) for ref in shares]
        o_ref[:, :width] = sum(part[:, :width] for part in parts).astype(BF16)
        if not special:
            continue
        last = [part[:, width:] for part in parts]
        x = sum(lane_sum3(part, GROUP) for part in last)
        lane = lax.broadcasted_iota(jnp.int32, x.shape, 1) - HALF
        h1, h2, h3 = [part.astype(F32) for part in split3(x)]
        packed = jnp.where(lane < 2 * GROUP, pltpu.roll(h2, GROUP, 1), pltpu.roll(h3, 2 * GROUP, 1))
        packed = jnp.where(lane < GROUP, h1, packed)
        packed = jnp.where(lane < 3 * GROUP, packed, 0.0)
        o_ref[:, width:] = jnp.where(lane < 0, sum(last), packed).astype(BF16)


def add_shares(index, special, shares, slots=()):
    rows, lanes = shares[0].shape
    shape = jax.ShapeDtypeStruct((rows // max(len(slots), 1), lanes), BF16)
    slots = slots or (None,)
    return kernel_call(
        functools.partial(add_kernel, slots, special),
        (shape,) * len(slots),
        in_specs=[smem()] + vmem(len(shares)),
        out_specs=tuple(vmem(len(slots))),
    )(index, *shares)


def unpack(offset, index_ref, share_refs, q_ref, full, u, v, diag):
    n = q_ref.shape[1]
    width = n // 2
    cut = share_refs[0].shape[1]
    bs = cut + share_refs[1].shape[1] - width
    nb = n // bs
    lane = lax.broadcasted_iota(jnp.int32, (bs, bs), 1)

    def one(r, _):
        i = index_ref[r + offset]
        frm = pl.multiple_of(r * bs, bs)
        to = pl.multiple_of(i * bs, bs)
        for d in range(nb // 2):
            ref, col = (share_refs[0], d * bs) if d * bs < cut else (share_refs[1], d * bs - cut)
            part = ref[pl.ds(frm, bs), col : col + bs]
            at = pl.multiple_of(lax.rem(i + d, nb) * bs, bs)
            full[pl.ds(to, bs), pl.ds(at, bs)] = part
            if d:
                full[pl.ds(at, bs), pl.ds(to, bs)] = part.T
        at = pl.multiple_of(lax.rem(i + nb // 2, nb) * bs, bs)
        last = share_refs[1][pl.ds(frm, bs), width - cut :].astype(F32)

        @pl.when(i < nb // 2)
        def _():
            old = full[pl.ds(to, bs), pl.ds(at, bs)].astype(F32)
            full[pl.ds(to, bs), pl.ds(at, bs)] = jnp.where(lane < HALF, last, old).astype(BF16)
            full[pl.ds(at, HALF), pl.ds(to, bs)] = last.T[:HALF].astype(BF16)

        @pl.when(i >= nb // 2)
        def _():
            low = jnp.where(lane[:HALF] < HALF, last[:HALF], pltpu.roll(last[HALF:], HALF, 1))
            full[pl.ds(pl.multiple_of(to + HALF, HALF), HALF), pl.ds(at, bs)] = low.astype(BF16)
            old = full[pl.ds(at, bs), pl.ds(to, bs)].astype(F32)
            new = jnp.concatenate([low, low], axis=0).T
            full[pl.ds(at, bs), pl.ds(to, bs)] = jnp.where(lane < HALF, old, new).astype(BF16)

        side = last.T[HALF:]
        w, d = side[:RANK], side[RANK : RANK + 1]
        for g in (1, 2):
            w = w + pltpu.roll(side, HALF - g * GROUP, 0)[:RANK]
            d = d + side[g * GROUP + RANK : g * GROUP + RANK + 1]
        diag[:, pl.ds(to, bs)] = jnp.broadcast_to(d, (diag.shape[0], bs))
        q = q_ref[:RANK, pl.ds(to, bs)]
        us = [part.astype(F32) for part in split3(jnp.concatenate([w, q], axis=0))]
        us.append(jnp.zeros((bs - 6 * RANK, bs), F32))
        u[pl.ds(to, bs), :] = jnp.concatenate(us, axis=0).T.astype(BF16)
        v1, v2, v3 = split3(jnp.concatenate([q, w], axis=0))
        v[:, pl.ds(to, bs)] = jnp.concatenate([v1, v2, v3, v1, v2, v1], axis=0)
        return 0

    lax.fori_loop(0, share_refs[0].shape[0] // bs, one, 0)


def unpack_kernel(offsets, index_ref, *refs):
    q_ref = refs[2 * len(offsets)]
    for i, offset in enumerate(offsets):
        unpack(offset, index_ref, refs[2 * i : 2 * i + 2], q_ref, *refs[-4:])


def iterate_kernel(offset, index_ref, far_0, far_1, q_ref, p0_ref, *refs):
    p_ref, inv_ref, full, u, v, diag = refs[4:]
    k, _ = q_ref.shape
    unpack(offset, index_ref, (far_0, far_1), q_ref, full, u, v, diag)
    lane = lax.broadcasted_iota(jnp.int32, (k, LANES), 1)

    def product(p):
        t = dot(p, u[...], NN)
        t = t + pltpu.roll(t, 4 * RANK, 1)
        t = t + pltpu.roll(t, 2 * RANK, 1)
        h1, h2, h3 = [h.astype(F32) for h in split3(t)]
        ts = jnp.concatenate(
            [jnp.where(lane < 6 * RANK, h1, h2), jnp.where(lane < 2 * RANK, h2, h3)[:, :HALF]], axis=1
        ).astype(BF16)
        y = dot(p, full[...], NN) + dot(ts, v[...], NN) + p.astype(F32) * diag[0:1, :]
        return split3(y)

    def sweep(step, p):
        parts = product(p)
        return apply_lower(inverse_lower(gram_of(parts, p)), parts).astype(BF16)

    p = lax.fori_loop(0, ITERS - 1, sweep, p0_ref[...])
    p_ref[...] = p
    inv_ref[...] = inverse_lower(gram_of(product(p), p))


def finish_kernel(scale, p_ref, inv_ref, block_ref, o_ref):
    back = dot(p_ref[...], block_ref[...], NN)
    o_ref[...] = (apply_lower(inv_ref[...], split3(back)) * scale).astype(BF16)


def flip(x, axes, perm):
    return lax.ppermute(x, axes, perm)


def ordered(own, recv, bit, axis=0):
    return jnp.where(
        bit == 0,
        jnp.concatenate([own, recv], axis=axis),
        jnp.concatenate([recv, own], axis=axis),
    )


def sample_space(stamps, start_panel):
    pix = lax.axis_size("pix")
    samp = lax.axis_size("samp")
    n = stamps.shape[0] * pix * samp
    k = start_panel.shape[1]
    scale = math.sqrt(start_panel.shape[0] * pix)
    p = lax.axis_index("pix")
    s = lax.axis_index("samp")
    xor_pix = lambda b: [(i, i ^ b) for i in range(pix)]
    xor_samp = lambda b: [(i, i ^ b) for i in range(samp)]

    core = p & 1
    x, y = (p >> 1) & 1, (p >> 2) & 1
    z0, z1 = s & 1, (s >> 1) & 1

    low = start_panel.astype(BF16).T
    for b in (2, 4):
        low = jnp.concatenate([low, flip(low, "pix", xor_pix(b))], axis=1)
    far = flip(low, "pix", xor_pix(1))
    bit_a = jnp.where(core == 0, x, y)
    bit_b = jnp.where(core == 0, y, x)
    bs = 2 * stamps.shape[0]
    nb = n // bs
    at = jnp.arange(pix, dtype=jnp.int32)
    place = p ^ (((at & 1) << 1) | ((at & 2) << 1) | (at >> 2))
    at = jnp.arange(nb, dtype=jnp.int32)
    c_of = core ^ ((at >> 3) & 1)
    a_of = jnp.where(c_of == 0, x, y) ^ ((at >> 2) & 1)
    b_of = jnp.where(c_of == 0, y, x) ^ ((at >> 1) & 1)
    order = c_of * 8 + a_of * 4 + b_of * 2 + (z0 ^ (at & 1))
    pairs = [
        (core * 4 + half * 2 + quarter) * (nb // 8)
        for half in (1 - bit_a, bit_a)
        for quarter in (1 - bit_b, bit_b)
    ]
    pairs += [1 - z0, z0, core, 0]
    index = jnp.concatenate([jnp.stack([jnp.int32(i) for i in pairs]), place, order]).astype(jnp.int32)

    block = lax.all_to_all(stamps, ("pix", "samp"), split_axis=1, concat_axis=0, tiled=True)

    proj = kernel_call(
        rows_kernel,
        jax.ShapeDtypeStruct((k, stamps.shape[0]), BF16),
        in_specs=[smem()] + vmem(3),
        out_specs=vmem()[0],
    )(index, low, far, stamps)
    for b in (1, 2, 4):
        proj = ordered(proj, flip(proj, "pix", xor_pix(b)), p & b, axis=1)
    for b in (1, 2):
        proj = ordered(proj, flip(proj, "samp", xor_samp(b)), s & b, axis=1)
    proj, q = kernel_call(
        functools.partial(basis_kernel, pix, samp),
        (jax.ShapeDtypeStruct((k, n), BF16), jax.ShapeDtypeStruct((k, n), F32)),
        in_specs=vmem(),
        out_specs=tuple(vmem(2)),
    )(proj)

    first = [(i, i ^ (2 if i % 2 == 0 else 4)) for i in range(pix)]
    second = [(i, i ^ (4 if i % 2 == 0 else 2)) for i in range(pix)]
    other = flip(block, "pix", xor_pix(1))
    px = block.shape[1]
    width = n // 2 + bs
    rows = n // 8
    window = rows - bs + width
    cut = (nb // 4 + 1) * bs
    pieces = tuple(jax.ShapeDtypeStruct((rows, c), BF16) for c in (cut, width - cut))
    stack = jax.ShapeDtypeStruct((12 * RANK, n), BF16)
    left, right = kernel_call(
        factors_kernel,
        (stack, stack),
        in_specs=vmem(3),
        out_specs=tuple(vmem(2)),
        scratch_mib=12,
    )(block, other, q)

    def form(quarter):
        return kernel_call(
            functools.partial(form_kernel, QUARTERS + quarter),
            pieces,
            in_specs=[smem()] + vmem(4),
            out_specs=tuple(vmem(2)),
            scratch_mib=12,
            scratch_shapes=[pltpu.VMEM((window, 2 * px), BF16), pltpu.VMEM((12 * RANK, window), BF16)],
        )(index, block, other, left, right)

    sent = [form(0), form(1)]
    held = [form(2)]
    held.append(form(3))
    swap = xor_pix(1)
    near, far, over_a, far_a, over_ab, far_ab = ([None, None] for _ in range(6))
    for e in (0, 1):
        add = functools.partial(add_shares, index, e == 1)
        passed, kept = [flip(sent[i][e], "pix", first) for i in (0, 1)]
        (send,) = add((held[0][e], passed))
        recv = flip(send, "pix", second)
        send, keep = add((held[1][e], kept, recv), (HALVES, HALVES + 1))
        recv = flip(send, "samp", xor_samp(1))
        (share,) = add((keep, recv))
        recv = flip(share, "samp", xor_samp(2))
        (share,) = add((share, recv))

        recv = flip(share, "samp", xor_samp(1))
        share = jnp.concatenate([share, recv], axis=0)
        over_a[e] = flip(share, "pix", first)
        over_b = flip(share, "pix", second)
        over_ab[e] = flip(over_b, "pix", first)
        near[e] = jnp.concatenate([share, over_b], axis=0)
        far[e] = flip(near[e], "pix", swap)
        far_a[e], far_ab[e] = [flip(t[e], "pix", swap) for t in (over_a, over_ab)]
    parts = (
        jax.ShapeDtypeStruct((n, n), BF16),
        jax.ShapeDtypeStruct((n, bs), BF16),
        jax.ShapeDtypeStruct((12 * RANK, n), BF16),
        jax.ShapeDtypeStruct((8, n), F32),
    )
    eighth = nb // 8
    now = kernel_call(
        functools.partial(unpack_kernel, (BLOCKS, BLOCKS + 4 * eighth)),
        parts,
        in_specs=[smem()] + vmem(5),
        out_specs=tuple(vmem(4)),
        scratch_mib=4,
    )(index, *near, *far, q)

    def unpack_more(now, slots, *shares):
        return kernel_call(
            functools.partial(unpack_kernel, [BLOCKS + i * eighth for i in slots]),
            parts,
            in_specs=[smem()] + vmem(len(shares) + 5),
            out_specs=tuple(vmem(4)),
            input_output_aliases={len(shares) + 2 + i: i for i in range(4)},
            scratch_mib=4,
        )(index, *shares, q, *now)

    now = unpack_more(now, (2, 6), *over_a, *far_a)
    now = unpack_more(now, (3,), *over_ab)
    proj, inv = kernel_call(
        functools.partial(iterate_kernel, BLOCKS + 7 * eighth),
        (jax.ShapeDtypeStruct((k, n), BF16), jax.ShapeDtypeStruct((k, LANES), F32)) + parts,
        in_specs=[smem()] + vmem(8),
        out_specs=tuple(vmem(6)),
        input_output_aliases={5 + i: 2 + i for i in range(4)},
        scratch_mib=12,
    )(index, *far_ab, q, proj, *now)[:2]

    mine = kernel_call(
        functools.partial(finish_kernel, scale),
        jax.ShapeDtypeStruct((k, px), BF16),
        in_specs=vmem(3),
        out_specs=vmem()[0],
    )(proj, inv, block)
    for b in (2, 1):
        mine = jnp.concatenate([mine, flip(mine, "samp", xor_samp(b))], axis=1)
    parts = [mine[:, i * px : (i + 1) * px] for i in range(samp)]
    by_distance = {0: parts[0], 2: parts[1], 1: parts[2], 3: parts[3]}
    swap0 = [jnp.where(z0 == 0, by_distance[i], by_distance[i ^ 1]) for i in range(samp)]
    swap1 = [jnp.where(z1 == 0, swap0[i], swap0[i ^ 2]) for i in range(samp)]
    return jnp.concatenate(swap1, axis=1).astype(F32).T


def solution(mesh):
    pix, samp = mesh.shape["pix"], mesh.shape["samp"]

    def local(stamps, start_panel):
        n = stamps.shape[0] * pix * samp
        k = start_panel.shape[1]
        if n <= SAMPLE_SPACE_LIMIT and (pix, samp) == (8, 4) and 4 * k == LANES:
            return sample_space(stamps, start_panel)
        return pixel_space(stamps, start_panel)

    return jax.shard_map(
        local,
        mesh=mesh,
        in_specs=(P(("samp", "pix"), None), P("pix", None)),
        out_specs=P("pix", None),
        check_vma=False,
    )
```

```python
import functools
import math

import jax
import jax.numpy as jnp
from jax import lax
from jax.experimental import pallas as pl
from jax.experimental.pallas import tpu as pltpu
from jax.sharding import PartitionSpec as P


ITERS = 10
LANES = 128
PANEL = 16
RANK = 16
GROUP = 20
HALF = 64
STEP = 2
QUARTERS, HALVES, CORE, PLACE, BLOCKS = 0, 4, 6, 8, 16
SAMPLE_SPACE_LIMIT = 4096
F32 = jnp.float32
BF16 = jnp.bfloat16

NN = (((1,), (0,)), ((), ()))
NT = (((1,), (1,)), ((), ()))
TN = (((0,), (0,)), ((), ()))


def orthonormal(back, gram):
    lower = jnp.linalg.cholesky(gram)
    return lax.linalg.triangular_solve(lower, back, left_side=False, lower=True, transpose_a=True)


def pixel_space(stamps, start_panel):
    block = lax.all_to_all(stamps, "pix", split_axis=1, concat_axis=0, tiled=True)

    def sweep(step, panel):
        partial_value = jnp.dot(block, panel.astype(BF16), preferred_element_type=F32)
        proj = lax.psum(partial_value.astype(BF16), "pix")
        back = lax.dot_general(block, proj, TN, preferred_element_type=F32)
        summed = lax.psum(back.astype(BF16), "samp").astype(F32)
        gram = lax.psum(jnp.dot(summed.T, summed, precision=lax.Precision.HIGHEST), "pix")
        return orthonormal(summed, gram)

    panel = lax.fori_loop(0, ITERS, sweep, start_panel)
    return panel * math.sqrt(start_panel.shape[0] * lax.axis_size("pix"))


def dot(a, b, dims):
    return lax.dot_general(a, b, dims, preferred_element_type=F32)


def split3(x):
    hi = x.astype(BF16)
    rest = x - hi.astype(F32)
    mid = rest.astype(BF16)
    lo = (rest - mid.astype(F32)).astype(BF16)
    return hi, mid, lo


def kernel_call(body, out_shape, in_specs=(), scratch_mib=8, **kw):
    single = not isinstance(out_shape, tuple)
    outs = tuple(pltpu.VMEM(o.shape, o.dtype) for o in ((out_shape,) if single else out_shape))
    call = pl.pallas_call(
        body,
        out_shape=outs[0] if single else outs,
        in_specs=in_specs,
        compiler_params=pltpu.CompilerParams(vmem_limit_bytes=scratch_mib << 20),
        **kw,
    )

    def place(x, spec):
        if spec.memory_space != pltpu.VMEM:
            return x
        return pltpu.with_memory_space_constraint(x, pltpu.VMEM)

    return lambda *args: call(*map(place, args, in_specs))


def vmem(n=1):
    return [pl.BlockSpec(memory_space=pltpu.VMEM)] * n


def smem():
    return pl.BlockSpec(memory_space=pltpu.SMEM)


def inverse_lower(gram):
    k = gram.shape[0]
    lane = lax.broadcasted_iota(jnp.int32, gram.shape, 1)
    row = lax.broadcasted_iota(jnp.int32, gram.shape, 0)
    m = jnp.where(lane < k, gram, jnp.where(lane % k == row, 1.0, 0.0))
    pivots = jnp.ones(gram.shape, F32)
    for start in range(0, k, PANEL):
        cols = [jnp.broadcast_to(m[:, j : j + 1], m.shape) for j in range(start, start + PANEL)]
        for t in range(PANEL):
            j = start + t
            pivot = cols[t][j : j + 1, :]
            factor = jnp.where(row > j, cols[t] * (1.0 / pivot), 0.0)
            pivots = jnp.where(row == j, pivot, pivots)
            for later in range(t + 1, PANEL):
                cols[later] = cols[later] - factor * cols[later][j : j + 1, :]
            m = m - factor * m[j : j + 1, :]
    return m * lax.rsqrt(pivots)


def lane_sum3(x, k):
    return x + pltpu.roll(x, LANES - k, 1) + pltpu.roll(x, LANES - 2 * k, 1)


def gram_of(parts, right):
    k = right.shape[0]
    wide = jnp.concatenate([right, jnp.zeros((3 * k, right.shape[1]), right.dtype)], axis=0)
    g = dot(jnp.concatenate(parts, axis=0), wide, NT)
    return g[:k] + g[k : 2 * k] + g[2 * k :]


def apply_lower(inv, parts):
    k = inv.shape[0]
    lane = lax.broadcasted_iota(jnp.int32, inv.shape, 1)
    h1, h2, h3 = [h.astype(F32) for h in split3(inv)]
    first = jnp.where(lane < k, 0.0, h1)
    second = jnp.where(lane < k, 0.0, jnp.where(lane < 3 * k, h2, h3))
    left = jnp.concatenate([first, second], axis=1).astype(BF16)
    y1, y2, y3 = parts
    zeros = jnp.zeros_like(y1)
    return dot(left, jnp.concatenate([zeros, y1, y2, y3, zeros, y1, y2, y1], axis=0), NN)


def rows_kernel(index_ref, near_ref, far_ref, stamps_ref, o_ref):
    total = jnp.zeros(o_ref.shape, F32)
    pix = BLOCKS - PLACE
    m = near_ref.shape[1] * 2 // pix
    for j in range(pix):
        ref = near_ref if j * m < near_ref.shape[1] else far_ref
        at = j * m % near_ref.shape[1]
        stamps = stamps_ref[:, pl.ds(pl.multiple_of(index_ref[PLACE + j] * m, LANES), m)]
        total += dot(ref[:, at : at + m], stamps, NT)
    o_ref[...] = total.astype(BF16)


def basis_kernel(pix, samp, p0_ref, p_ref, q_ref):
    k, n = p0_ref.shape
    m = n // (pix * samp)
    per = LANES // m
    lane = lax.broadcasted_iota(jnp.int32, (k, LANES), 1)
    for to in range(n // LANES):
        block = jnp.zeros((k, LANES), F32)
        for j in range(per):
            p, s = divmod(to * per + j, samp)
            group, slot = divmod(s * pix + p, per)
            part = p0_ref[:, group * LANES : (group + 1) * LANES].astype(F32)
            part = pltpu.roll(part, (j - slot) * m % LANES, 1) if j != slot else part
            block = jnp.where(lane // m == j, part, block)
        p_ref[:, to * LANES : (to + 1) * LANES] = block.astype(BF16)
    p0 = p_ref[...]
    parts = (p0, jnp.zeros_like(p0), jnp.zeros_like(p0))
    q = apply_lower(inverse_lower(gram_of(parts, p0)), parts)
    q_ref[...] = jnp.where(lax.broadcasted_iota(jnp.int32, q.shape, 0) < RANK, q, 0.0)


def factors_kernel(own_ref, other_ref, q_ref, left, right):
    k = q_ref.shape[0]
    q = q_ref[...]
    zeros = jnp.zeros(q.shape, BF16)
    q1, q2, q3 = split3(q)
    qs = jnp.concatenate([q1, q2, q3], axis=0)
    w = jnp.zeros(q.shape, F32)
    for ref in (own_ref, other_ref):
        t3 = dot(qs, ref[...], NN)
        ts = split3(t3[:k] + t3[k : 2 * k] + t3[2 * k :])
        w3 = dot(jnp.concatenate(ts, axis=0), ref[...], NT)
        w += w3[:k] + w3[k : 2 * k] + w3[2 * k :]
    ws = jnp.concatenate(list(split3(w)) + [zeros], axis=0)
    m = lane_sum3(dot(q1, ws, NT) + dot(q2, ws, NT) + dot(q3, ws, NT), k)
    m = jnp.where(lax.broadcasted_iota(jnp.int32, m.shape, 1) < k, m, 0.0)
    m = pltpu.roll(m, k, 1) + pltpu.roll(m, 2 * k, 1) + pltpu.roll(m, 3 * k, 1)
    w1, w2, w3 = split3(w - 0.5 * apply_lower(m, (q1, q2, q3)))
    q1, q2, q3, w1, w2, w3 = [part[:RANK] for part in (q1, q2, q3, w1, w2, w3)]
    left[...] = jnp.concatenate([q1, w1, q1, w1, q1, w1, q2, w2, q2, w2, q3, w3], axis=0)
    right[...] = jnp.concatenate([w1, q1, w2, q2, w3, q3, w1, q1, w2, q2, w1, q1], axis=0)


def form_rows(first, core, own_ref, other_ref, left, right, out_refs, window, right_win):
    n, px = own_ref.shape
    rows, cut = out_refs[0].shape
    width = n // 2
    bs = cut + out_refs[1].shape[1] - width
    nb = n // bs
    for b in range(window.shape[0] // bs):
        at = pl.multiple_of(lax.rem(first + b, nb) * bs, bs)
        window[b * bs : (b + 1) * bs, :px] = own_ref[pl.ds(at, bs), :]
        window[b * bs : (b + 1) * bs, px:] = other_ref[pl.ds(at, bs), :]
        right_win[:, b * bs : (b + 1) * bs] = right[:, pl.ds(at, bs)]
    lane = lax.broadcasted_iota(jnp.int32, (bs, bs), 1)
    eye = lax.broadcasted_iota(jnp.int32, (bs, bs), 0) == lane
    step = STEP * bs
    for i in range(rows // bs):
        if i % STEP == 0:
            at = pl.multiple_of((first + i) * bs, bs)
            lo, end = i * bs, i * bs + step + width
            wide = dot(window[lo : lo + step, :], window[lo:end, :], NT)
            wide -= dot(left[:, pl.ds(at, step)], right_win[:, lo:end], TN)
        off = i % STEP * bs
        to = i * bs
        s = wide[off : off + bs, off : off + width + bs]
        corner = s[:, :bs]
        diagonal = jnp.sum(jnp.where(eye, corner, 0.0), axis=0, keepdims=True)
        out_refs[0][to : to + bs, :bs] = jnp.where(eye, 0.0, corner).astype(BF16)
        out_refs[0][to : to + bs, bs:] = s[:, bs:cut].astype(BF16)
        out_refs[1][to : to + bs, : width - cut] = s[:, cut:width].astype(BF16)
        last = s[:, width:]
        low = last[HALF:]
        last = jnp.where(core == 0, last, jnp.concatenate([low, pltpu.roll(low, HALF, 1)], axis=0))
        side = [jnp.zeros((HALF, bs), F32)]
        for g, d in enumerate(split3(diagonal)):
            w = right_win[2 * g * RANK : (2 * g + 1) * RANK, to : to + bs]
            side.append(w.astype(F32))
            side.append(jnp.broadcast_to(d.astype(F32), (GROUP - RANK, bs)))
        side.append(jnp.zeros((bs - HALF - 3 * GROUP, bs), F32))
        side = jnp.concatenate(side, axis=0).T
        last = jnp.where(lane < HALF, last, side)
        out_refs[1][to : to + bs, width - cut :] = last.astype(BF16)


def form_kernel(slot, at_ref, own_ref, other_ref, left, right, out_0, out_1, *wins):
    outs = (out_0, out_1)
    form_rows(at_ref[slot], at_ref[CORE], own_ref, other_ref, left, right, outs, *wins)


def add_kernel(slots, special, at_ref, *refs):
    shares, o_refs = refs[: -len(slots)], refs[-len(slots) :]
    width = shares[0].shape[1] - (LANES if special else 0)
    for slot, o_ref in zip(slots, o_refs):
        h = o_ref.shape[0]
        at = 0 if slot is None else pl.multiple_of(at_ref[slot] * h, h)
        parts = [ref[pl.ds(at, h), :].astype(F32) for ref in shares]
        o_ref[:, :width] = sum(part[:, :width] for part in parts).astype(BF16)
        if not special:
            continue
        last = [part[:, width:] for part in parts]
        x = sum(lane_sum3(part, GROUP) for part in last)
        lane = lax.broadcasted_iota(jnp.int32, x.shape, 1) - HALF
        h1, h2, h3 = [part.astype(F32) for part in split3(x)]
        packed = jnp.where(lane < 2 * GROUP, pltpu.roll(h2, GROUP, 1), pltpu.roll(h3, 2 * GROUP, 1))
        packed = jnp.where(lane < GROUP, h1, packed)
        packed = jnp.where(lane < 3 * GROUP, packed, 0.0)
        o_ref[:, width:] = jnp.where(lane < 0, sum(last), packed).astype(BF16)


def add_shares(index, special, shares, slots=()):
    rows, lanes = shares[0].shape
    shape = jax.ShapeDtypeStruct((rows // max(len(slots), 1), lanes), BF16)
    slots = slots or (None,)
    return kernel_call(
        functools.partial(add_kernel, slots, special),
        (shape,) * len(slots),
        in_specs=[smem()] + vmem(len(shares)),
        out_specs=tuple(vmem(len(slots))),
    )(index, *shares)


def unpack(offset, index_ref, share_refs, q_ref, full, u, v, diag):
    n = q_ref.shape[1]
    width = n // 2
    bs = LANES
    nb = n // bs
    cut = (nb // 4 + 1) * bs
    rows = [ref.shape[0] for ref in share_refs if ref is not None][0]
    lane = lax.broadcasted_iota(jnp.int32, (bs, bs), 1)

    def one(r, _):
        i = index_ref[r + offset]
        frm = pl.multiple_of(r * bs, bs)
        to = pl.multiple_of(i * bs, bs)
        for d in range(nb // 2):
            ref, col = (share_refs[0], d * bs) if d * bs < cut else (share_refs[1], d * bs - cut)
            if ref is None:
                continue
            part = ref[pl.ds(frm, bs), col : col + bs]
            at = pl.multiple_of(lax.rem(i + d, nb) * bs, bs)
            full[pl.ds(to, bs), pl.ds(at, bs)] = part
            if d:
                full[pl.ds(at, bs), pl.ds(to, bs)] = part.T
        if share_refs[1] is None:
            return 0
        at = pl.multiple_of(lax.rem(i + nb // 2, nb) * bs, bs)
        last = share_refs[1][pl.ds(frm, bs), width - cut :].astype(F32)

        @pl.when(i < nb // 2)
        def _():
            old = full[pl.ds(to, bs), pl.ds(at, bs)].astype(F32)
            full[pl.ds(to, bs), pl.ds(at, bs)] = jnp.where(lane < HALF, last, old).astype(BF16)
            full[pl.ds(at, HALF), pl.ds(to, bs)] = last.T[:HALF].astype(BF16)

        @pl.when(i >= nb // 2)
        def _():
            low = jnp.where(lane[:HALF] < HALF, last[:HALF], pltpu.roll(last[HALF:], HALF, 1))
            full[pl.ds(pl.multiple_of(to + HALF, HALF), HALF), pl.ds(at, bs)] = low.astype(BF16)
            old = full[pl.ds(at, bs), pl.ds(to, bs)].astype(F32)
            new = jnp.concatenate([low, low], axis=0).T
            full[pl.ds(at, bs), pl.ds(to, bs)] = jnp.where(lane < HALF, old, new).astype(BF16)

        side = last.T[HALF:]
        w, d = side[:RANK], side[RANK : RANK + 1]
        for g in (1, 2):
            w = w + pltpu.roll(side, HALF - g * GROUP, 0)[:RANK]
            d = d + side[g * GROUP + RANK : g * GROUP + RANK + 1]
        diag[:, pl.ds(to, bs)] = jnp.broadcast_to(d, (diag.shape[0], bs))
        q = q_ref[:RANK, pl.ds(to, bs)]
        us = [part.astype(F32) for part in split3(jnp.concatenate([w, q], axis=0))]
        us.append(jnp.zeros((bs - 6 * RANK, bs), F32))
        u[pl.ds(to, bs), :] = jnp.concatenate(us, axis=0).T.astype(BF16)
        v1, v2, v3 = split3(jnp.concatenate([q, w], axis=0))
        v[:, pl.ds(to, bs)] = jnp.concatenate([v1, v2, v3, v1, v2, v1], axis=0)
        return 0

    lax.fori_loop(0, rows // bs, one, 0)


def unpack_kernel(items, count, index_ref, *refs):
    shares = iter(refs[:count])
    for offset, given in items:
        pair = [next(shares) if e in given else None for e in (0, 1)]
        unpack(offset, index_ref, pair, refs[count], *refs[-4:])


def iterate_kernel(offset, index_ref, far_0, far_1, q_ref, p0_ref, *refs):
    p_ref, inv_ref, full, u, v, diag = refs[4:]
    k, _ = q_ref.shape
    unpack(offset, index_ref, (far_0, far_1), q_ref, full, u, v, diag)
    lane = lax.broadcasted_iota(jnp.int32, (k, LANES), 1)

    def product(p):
        t = dot(p, u[...], NN)
        t = t + pltpu.roll(t, 4 * RANK, 1)
        t = t + pltpu.roll(t, 2 * RANK, 1)
        h1, h2, h3 = [h.astype(F32) for h in split3(t)]
        ts = jnp.concatenate(
            [jnp.where(lane < 6 * RANK, h1, h2), jnp.where(lane < 2 * RANK, h2, h3)[:, :HALF]], axis=1
        ).astype(BF16)
        y = dot(p, full[...], NN) + dot(ts, v[...], NN) + p.astype(F32) * diag[0:1, :]
        return split3(y)

    def sweep(step, p):
        parts = product(p)
        return apply_lower(inverse_lower(gram_of(parts, p)), parts).astype(BF16)

    p = lax.fori_loop(0, ITERS - 1, sweep, p0_ref[...])
    p_ref[...] = p
    inv_ref[...] = inverse_lower(gram_of(product(p), p))


def finish_kernel(scale, p_ref, inv_ref, block_ref, o_ref):
    back = dot(p_ref[...], block_ref[...], NN)
    o_ref[...] = (apply_lower(inv_ref[...], split3(back)) * scale).astype(BF16)


def flip(x, axes, perm):
    return lax.ppermute(x, axes, perm)


def ordered(own, recv, bit, axis=0):
    return jnp.where(
        bit == 0,
        jnp.concatenate([own, recv], axis=axis),
        jnp.concatenate([recv, own], axis=axis),
    )


def sample_space(stamps, start_panel):
    pix = lax.axis_size("pix")
    samp = lax.axis_size("samp")
    n = stamps.shape[0] * pix * samp
    k = start_panel.shape[1]
    scale = math.sqrt(start_panel.shape[0] * pix)
    p = lax.axis_index("pix")
    s = lax.axis_index("samp")
    xor_pix = lambda b: [(i, i ^ b) for i in range(pix)]
    xor_samp = lambda b: [(i, i ^ b) for i in range(samp)]

    core = p & 1
    x, y = (p >> 1) & 1, (p >> 2) & 1
    z0, z1 = s & 1, (s >> 1) & 1

    low = start_panel.astype(BF16).T
    for b in (2, 4):
        low = jnp.concatenate([low, flip(low, "pix", xor_pix(b))], axis=1)
    far = flip(low, "pix", xor_pix(1))
    bit_a = jnp.where(core == 0, x, y)
    bit_b = jnp.where(core == 0, y, x)
    bs = 2 * stamps.shape[0]
    nb = n // bs
    at = jnp.arange(pix, dtype=jnp.int32)
    place = p ^ (((at & 1) << 1) | ((at & 2) << 1) | (at >> 2))
    at = jnp.arange(nb, dtype=jnp.int32)
    c_of = core ^ ((at >> 3) & 1)
    a_of = jnp.where(c_of == 0, x, y) ^ ((at >> 2) & 1)
    b_of = jnp.where(c_of == 0, y, x) ^ ((at >> 1) & 1)
    order = c_of * 8 + a_of * 4 + b_of * 2 + (z0 ^ (at & 1))
    pairs = [
        (core * 4 + half * 2 + quarter) * (nb // 8)
        for half in (1 - bit_a, bit_a)
        for quarter in (1 - bit_b, bit_b)
    ]
    pairs += [1 - z0, z0, core, 0]
    index = jnp.concatenate([jnp.stack([jnp.int32(i) for i in pairs]), place, order]).astype(jnp.int32)

    block = lax.all_to_all(stamps, ("pix", "samp"), split_axis=1, concat_axis=0, tiled=True)

    proj = kernel_call(
        rows_kernel,
        jax.ShapeDtypeStruct((k, stamps.shape[0]), BF16),
        in_specs=[smem()] + vmem(3),
        out_specs=vmem()[0],
    )(index, low, far, stamps)
    for b in (1, 2, 4):
        proj = ordered(proj, flip(proj, "pix", xor_pix(b)), p & b, axis=1)
    other = flip(proj, "samp", xor_samp(1))
    proj = ordered(proj, other, z0, axis=1)
    proj = ordered(proj, flip(proj, "samp", xor_samp(2)), z1, axis=1)
    proj, q = kernel_call(
        functools.partial(basis_kernel, pix, samp),
        (jax.ShapeDtypeStruct((k, n), BF16), jax.ShapeDtypeStruct((k, n), F32)),
        in_specs=vmem(),
        out_specs=tuple(vmem(2)),
    )(proj)

    first = [(i, i ^ (2 if i % 2 == 0 else 4)) for i in range(pix)]
    second = [(i, i ^ (4 if i % 2 == 0 else 2)) for i in range(pix)]
    other = flip(block, "pix", xor_pix(1))
    px = block.shape[1]
    width = n // 2 + bs
    rows = n // 8
    window = rows - bs + width
    cut = (nb // 4 + 1) * bs
    pieces = tuple(jax.ShapeDtypeStruct((rows, c), BF16) for c in (cut, width - cut))
    stack = jax.ShapeDtypeStruct((12 * RANK, n), BF16)
    left, right = kernel_call(
        factors_kernel,
        (stack, stack),
        in_specs=vmem(3),
        out_specs=tuple(vmem(2)),
        scratch_mib=12,
    )(block, other, q)

    def form(quarter):
        return kernel_call(
            functools.partial(form_kernel, QUARTERS + quarter),
            pieces,
            in_specs=[smem()] + vmem(4),
            out_specs=tuple(vmem(2)),
            scratch_mib=12,
            scratch_shapes=[pltpu.VMEM((window, 2 * px), BF16), pltpu.VMEM((12 * RANK, window), BF16)],
        )(index, block, other, left, right)

    sent = [form(0), form(1)]
    held = [form(2)]
    held.append(form(3))
    swap = xor_pix(1)
    near, far, over_a, far_a, over_ab, far_ab = ([None, None] for _ in range(6))
    for e in (0, 1):
        add = functools.partial(add_shares, index, e == 1)
        passed, kept = [flip(sent[i][e], "pix", first) for i in (0, 1)]
        (send,) = add((held[0][e], passed))
        recv = flip(send, "pix", second)
        send, keep = add((held[1][e], kept, recv), (HALVES, HALVES + 1))
        recv = flip(send, "samp", xor_samp(1))
        (share,) = add((keep, recv))
        recv = flip(share, "samp", xor_samp(2))
        (share,) = add((share, recv))

        recv = flip(share, "samp", xor_samp(1))
        share = jnp.concatenate([share, recv], axis=0)
        over_a[e] = flip(share, "pix", first)
        over_b = flip(share, "pix", second)
        over_ab[e] = flip(over_b, "pix", first)
        near[e] = jnp.concatenate([share, over_b], axis=0)
        far[e] = flip(near[e], "pix", swap)
        far_a[e], far_ab[e] = [flip(t[e], "pix", swap) for t in (over_a, over_ab)]
    parts = (
        jax.ShapeDtypeStruct((n, n), BF16),
        jax.ShapeDtypeStruct((n, bs), BF16),
        jax.ShapeDtypeStruct((12 * RANK, n), BF16),
        jax.ShapeDtypeStruct((8, n), F32),
    )
    eighth = nb // 8

    def unpack_into(now, slots, given, *shares):
        count = len(shares)
        items = [(BLOCKS + i * eighth, given) for i in slots]
        aliases = {count + 2 + i: i for i in range(len(now))}
        return kernel_call(
            functools.partial(unpack_kernel, items, count),
            parts,
            in_specs=[smem()] + vmem(count + 1 + len(now)),
            out_specs=tuple(vmem(4)),
            input_output_aliases=aliases,
            scratch_mib=4,
        )(index, *shares, q, *now)

    now = unpack_into((), (0, 4), (0,), near[0], far[0])
    now = unpack_into(now, (0, 4), (1,), near[1], far[1])
    now = unpack_into(now, (2, 6), (0, 1), *over_a, *far_a)
    now = unpack_into(now, (3,), (0, 1), *over_ab)
    proj, inv = kernel_call(
        functools.partial(iterate_kernel, BLOCKS + 7 * eighth),
        (jax.ShapeDtypeStruct((k, n), BF16), jax.ShapeDtypeStruct((k, LANES), F32)) + parts,
        in_specs=[smem()] + vmem(8),
        out_specs=tuple(vmem(6)),
        input_output_aliases={5 + i: 2 + i for i in range(4)},
        scratch_mib=12,
    )(index, *far_ab, q, proj, *now)[:2]

    mine = kernel_call(
        functools.partial(finish_kernel, scale),
        jax.ShapeDtypeStruct((k, px), BF16),
        in_specs=vmem(3),
        out_specs=vmem()[0],
    )(proj, inv, block)
    for b in (2, 1):
        mine = jnp.concatenate([mine, flip(mine, "samp", xor_samp(b))], axis=1)
    parts = [mine[:, i * px : (i + 1) * px] for i in range(samp)]
    by_distance = {0: parts[0], 2: parts[1], 1: parts[2], 3: parts[3]}
    swap0 = [jnp.where(z0 == 0, by_distance[i], by_distance[i ^ 1]) for i in range(samp)]
    swap1 = [jnp.where(z1 == 0, swap0[i], swap0[i ^ 2]) for i in range(samp)]
    return jnp.concatenate(swap1, axis=1).astype(F32).T


def solution(mesh):
    pix, samp = mesh.shape["pix"], mesh.shape["samp"]

    def local(stamps, start_panel):
        n = stamps.shape[0] * pix * samp
        k = start_panel.shape[1]
        if n <= SAMPLE_SPACE_LIMIT and (pix, samp) == (8, 4) and 4 * k == 2 * stamps.shape[0] == LANES:
            return sample_space(stamps, start_panel)
        return pixel_space(stamps, start_panel)

    return jax.shard_map(
        local,
        mesh=mesh,
        in_specs=(P(("samp", "pix"), None), P("pix", None)),
        out_specs=P("pix", None),
        check_vma=False,
    )
```

```python
import functools
import math

import jax
import jax.numpy as jnp
from jax import lax
from jax.experimental import pallas as pl
from jax.experimental.pallas import tpu as pltpu
from jax.sharding import PartitionSpec as P


ITERS = 10
LANES = 128
PANEL = 16
RANK = 16
GROUP = 20
HALF = 64
STEP = 2
QUARTERS, HALVES, CORE, PLACE, BLOCKS = 0, 4, 6, 8, 16
SAMPLE_SPACE_LIMIT = 4096
F32 = jnp.float32
BF16 = jnp.bfloat16

NN = (((1,), (0,)), ((), ()))
NT = (((1,), (1,)), ((), ()))
TN = (((0,), (0,)), ((), ()))


def orthonormal(back, gram):
    lower = jnp.linalg.cholesky(gram)
    return lax.linalg.triangular_solve(lower, back, left_side=False, lower=True, transpose_a=True)


def pixel_space(stamps, start_panel):
    block = lax.all_to_all(stamps, "pix", split_axis=1, concat_axis=0, tiled=True)

    def sweep(step, panel):
        partial_value = jnp.dot(block, panel.astype(BF16), preferred_element_type=F32)
        proj = lax.psum(partial_value.astype(BF16), "pix")
        back = lax.dot_general(block, proj, TN, preferred_element_type=F32)
        summed = lax.psum(back.astype(BF16), "samp").astype(F32)
        gram = lax.psum(jnp.dot(summed.T, summed, precision=lax.Precision.HIGHEST), "pix")
        return orthonormal(summed, gram)

    panel = lax.fori_loop(0, ITERS, sweep, start_panel)
    return panel * math.sqrt(start_panel.shape[0] * lax.axis_size("pix"))


def dot(a, b, dims):
    return lax.dot_general(a, b, dims, preferred_element_type=F32)


def split3(x):
    hi = x.astype(BF16)
    rest = x - hi.astype(F32)
    mid = rest.astype(BF16)
    lo = (rest - mid.astype(F32)).astype(BF16)
    return hi, mid, lo


def kernel_call(body, out_shape, in_specs=(), scratch_mib=8, **kw):
    single = not isinstance(out_shape, tuple)
    outs = tuple(pltpu.VMEM(o.shape, o.dtype) for o in ((out_shape,) if single else out_shape))
    call = pl.pallas_call(
        body,
        out_shape=outs[0] if single else outs,
        in_specs=in_specs,
        compiler_params=pltpu.CompilerParams(vmem_limit_bytes=scratch_mib << 20),
        **kw,
    )

    def place(x, spec):
        if spec.memory_space != pltpu.VMEM:
            return x
        return pltpu.with_memory_space_constraint(x, pltpu.VMEM)

    return lambda *args: call(*map(place, args, in_specs))


def vmem(n=1):
    return [pl.BlockSpec(memory_space=pltpu.VMEM)] * n


def smem():
    return pl.BlockSpec(memory_space=pltpu.SMEM)


def inverse_lower(gram):
    k = gram.shape[0]
    lane = lax.broadcasted_iota(jnp.int32, gram.shape, 1)
    row = lax.broadcasted_iota(jnp.int32, gram.shape, 0)
    m = jnp.where(lane < k, gram, jnp.where(lane % k == row, 1.0, 0.0))
    pivots = jnp.ones(gram.shape, F32)
    for start in range(0, k, PANEL):
        cols = [jnp.broadcast_to(m[:, j : j + 1], m.shape) for j in range(start, start + PANEL)]
        for t in range(PANEL):
            j = start + t
            pivot = cols[t][j : j + 1, :]
            factor = jnp.where(row > j, cols[t] * (1.0 / pivot), 0.0)
            pivots = jnp.where(row == j, pivot, pivots)
            for later in range(t + 1, PANEL):
                cols[later] = cols[later] - factor * cols[later][j : j + 1, :]
            m = m - factor * m[j : j + 1, :]
    return m * lax.rsqrt(pivots)


def lane_sum3(x, k):
    return x + pltpu.roll(x, LANES - k, 1) + pltpu.roll(x, LANES - 2 * k, 1)


def gram_of(parts, right):
    k = right.shape[0]
    wide = jnp.concatenate([right, jnp.zeros((3 * k, right.shape[1]), right.dtype)], axis=0)
    g = dot(jnp.concatenate(parts, axis=0), wide, NT)
    return g[:k] + g[k : 2 * k] + g[2 * k :]


def apply_lower(inv, parts):
    k = inv.shape[0]
    lane = lax.broadcasted_iota(jnp.int32, inv.shape, 1)
    h1, h2, h3 = [h.astype(F32) for h in split3(inv)]
    first = jnp.where(lane < k, 0.0, h1)
    second = jnp.where(lane < k, 0.0, jnp.where(lane < 3 * k, h2, h3))
    left = jnp.concatenate([first, second], axis=1).astype(BF16)
    y1, y2, y3 = parts
    zeros = jnp.zeros_like(y1)
    return dot(left, jnp.concatenate([zeros, y1, y2, y3, zeros, y1, y2, y1], axis=0), NN)


def rows_kernel(index_ref, near_ref, far_ref, stamps_ref, o_ref):
    total = jnp.zeros(o_ref.shape, F32)
    pix = BLOCKS - PLACE
    m = near_ref.shape[1] * 2 // pix
    for j in range(pix):
        ref = near_ref if j * m < near_ref.shape[1] else far_ref
        at = j * m % near_ref.shape[1]
        stamps = stamps_ref[:, pl.ds(pl.multiple_of(index_ref[PLACE + j] * m, LANES), m)]
        total += dot(ref[:, at : at + m], stamps, NT)
    o_ref[...] = total.astype(BF16)


def basis_kernel(pix, samp, p0_ref, p_ref, q_ref):
    k, n = p0_ref.shape
    m = n // (pix * samp)
    per = LANES // m
    lane = lax.broadcasted_iota(jnp.int32, (k, LANES), 1)
    for to in range(n // LANES):
        block = jnp.zeros((k, LANES), F32)
        for j in range(per):
            p, s = divmod(to * per + j, samp)
            group, slot = divmod(s * pix + p, per)
            part = p0_ref[:, group * LANES : (group + 1) * LANES].astype(F32)
            part = pltpu.roll(part, (j - slot) * m % LANES, 1) if j != slot else part
            block = jnp.where(lane // m == j, part, block)
        p_ref[:, to * LANES : (to + 1) * LANES] = block.astype(BF16)
    p0 = p_ref[...]
    parts = (p0, jnp.zeros_like(p0), jnp.zeros_like(p0))
    q = apply_lower(inverse_lower(gram_of(parts, p0)), parts)
    q_ref[...] = jnp.where(lax.broadcasted_iota(jnp.int32, q.shape, 0) < RANK, q, 0.0)


def factors_kernel(own_ref, other_ref, q_ref, left, right):
    k = q_ref.shape[0]
    q = q_ref[...]
    zeros = jnp.zeros(q.shape, BF16)
    q1, q2, q3 = split3(q)
    qs = jnp.concatenate([q1, q2, q3], axis=0)
    w = jnp.zeros(q.shape, F32)
    for ref in (own_ref, other_ref):
        t3 = dot(qs, ref[...], NN)
        ts = split3(t3[:k] + t3[k : 2 * k] + t3[2 * k :])
        w3 = dot(jnp.concatenate(ts, axis=0), ref[...], NT)
        w += w3[:k] + w3[k : 2 * k] + w3[2 * k :]
    ws = jnp.concatenate(list(split3(w)) + [zeros], axis=0)
    m = lane_sum3(dot(q1, ws, NT) + dot(q2, ws, NT) + dot(q3, ws, NT), k)
    m = jnp.where(lax.broadcasted_iota(jnp.int32, m.shape, 1) < k, m, 0.0)
    m = pltpu.roll(m, k, 1) + pltpu.roll(m, 2 * k, 1) + pltpu.roll(m, 3 * k, 1)
    w1, w2, w3 = split3(w - 0.5 * apply_lower(m, (q1, q2, q3)))
    q1, q2, q3, w1, w2, w3 = [part[:RANK] for part in (q1, q2, q3, w1, w2, w3)]
    left[...] = jnp.concatenate([q1, w1, q1, w1, q1, w1, q2, w2, q2, w2, q3, w3], axis=0)
    right[...] = jnp.concatenate([w1, q1, w2, q2, w3, q3, w1, q1, w2, q2, w1, q1], axis=0)


def form_rows(first, core, own_ref, other_ref, left, right, out_refs, window, right_win):
    n, px = own_ref.shape
    rows, cut = out_refs[0].shape
    width = n // 2
    bs = cut + out_refs[1].shape[1] - width
    nb = n // bs
    for b in range(window.shape[0] // bs):
        at = pl.multiple_of(lax.rem(first + b, nb) * bs, bs)
        window[b * bs : (b + 1) * bs, :px] = own_ref[pl.ds(at, bs), :]
        window[b * bs : (b + 1) * bs, px:] = other_ref[pl.ds(at, bs), :]
        right_win[:, b * bs : (b + 1) * bs] = right[:, pl.ds(at, bs)]
    lane = lax.broadcasted_iota(jnp.int32, (bs, bs), 1)
    eye = lax.broadcasted_iota(jnp.int32, (bs, bs), 0) == lane
    step = STEP * bs
    for i in range(rows // bs):
        if i % STEP == 0:
            at = pl.multiple_of((first + i) * bs, bs)
            lo, end = i * bs, i * bs + step + width
            wide = dot(window[lo : lo + step, :], window[lo:end, :], NT)
            wide -= dot(left[:, pl.ds(at, step)], right_win[:, lo:end], TN)
        off = i % STEP * bs
        to = i * bs
        s = wide[off : off + bs, off : off + width + bs]
        corner = s[:, :bs]
        diagonal = jnp.sum(jnp.where(eye, corner, 0.0), axis=0, keepdims=True)
        out_refs[0][to : to + bs, :bs] = jnp.where(eye, 0.0, corner).astype(BF16)
        out_refs[0][to : to + bs, bs:] = s[:, bs:cut].astype(BF16)
        out_refs[1][to : to + bs, : width - cut] = s[:, cut:width].astype(BF16)
        last = s[:, width:]
        low = last[HALF:]
        last = jnp.where(core == 0, last, jnp.concatenate([low, pltpu.roll(low, HALF, 1)], axis=0))
        side = [jnp.zeros((HALF, bs), F32)]
        for g, d in enumerate(split3(diagonal)):
            w = right_win[2 * g * RANK : (2 * g + 1) * RANK, to : to + bs]
            side.append(w.astype(F32))
            side.append(jnp.broadcast_to(d.astype(F32), (GROUP - RANK, bs)))
        side.append(jnp.zeros((bs - HALF - 3 * GROUP, bs), F32))
        side = jnp.concatenate(side, axis=0).T
        last = jnp.where(lane < HALF, last, side)
        out_refs[1][to : to + bs, width - cut :] = last.astype(BF16)


def form_kernel(slot, at_ref, own_ref, other_ref, left, right, out_0, out_1, *wins):
    outs = (out_0, out_1)
    form_rows(at_ref[slot], at_ref[CORE], own_ref, other_ref, left, right, outs, *wins)


def add_kernel(slots, special, at_ref, *refs):
    shares, o_refs = refs[: -len(slots)], refs[-len(slots) :]
    width = shares[0].shape[1] - (LANES if special else 0)
    for slot, o_ref in zip(slots, o_refs):
        h = o_ref.shape[0]
        at = 0 if slot is None else pl.multiple_of(at_ref[slot] * h, h)
        parts = [ref[pl.ds(at, h), :].astype(F32) for ref in shares]
        o_ref[:, :width] = sum(part[:, :width] for part in parts).astype(BF16)
        if not special:
            continue
        last = [part[:, width:] for part in parts]
        x = sum(lane_sum3(part, GROUP) for part in last)
        lane = lax.broadcasted_iota(jnp.int32, x.shape, 1) - HALF
        h1, h2, h3 = [part.astype(F32) for part in split3(x)]
        packed = jnp.where(lane < 2 * GROUP, pltpu.roll(h2, GROUP, 1), pltpu.roll(h3, 2 * GROUP, 1))
        packed = jnp.where(lane < GROUP, h1, packed)
        packed = jnp.where(lane < 3 * GROUP, packed, 0.0)
        o_ref[:, width:] = jnp.where(lane < 0, sum(last), packed).astype(BF16)


def add_shares(index, special, shares, slots=()):
    rows, lanes = shares[0].shape
    shape = jax.ShapeDtypeStruct((rows // max(len(slots), 1), lanes), BF16)
    slots = slots or (None,)
    return kernel_call(
        functools.partial(add_kernel, slots, special),
        (shape,) * len(slots),
        in_specs=[smem()] + vmem(len(shares)),
        out_specs=tuple(vmem(len(slots))),
    )(index, *shares)


def unpack(offset, index_ref, share_refs, q_ref, full, u, v, diag):
    n = q_ref.shape[1]
    width = n // 2
    bs = LANES
    nb = n // bs
    cut = (nb // 4 + 1) * bs
    rows = [ref.shape[0] for ref in share_refs if ref is not None][0]
    lane = lax.broadcasted_iota(jnp.int32, (bs, bs), 1)

    def one(first_half, r, _):
        i = index_ref[r + offset]
        frm = pl.multiple_of(r * bs, bs)
        to = pl.multiple_of(i * bs, bs)
        for d in range(nb // 2):
            ref, col = (share_refs[0], d * bs) if d * bs < cut else (share_refs[1], d * bs - cut)
            if ref is None:
                continue
            part = ref[pl.ds(frm, bs), col : col + bs]
            at = pl.multiple_of(lax.rem(i + d, nb) * bs, bs)
            full[pl.ds(to, bs), pl.ds(at, bs)] = part
            if d:
                full[pl.ds(at, bs), pl.ds(to, bs)] = part.T
        if share_refs[1] is None:
            return 0
        at = pl.multiple_of(lax.rem(i + nb // 2, nb) * bs, bs)
        last = share_refs[1][pl.ds(frm, bs), width - cut :].astype(F32)

        if first_half:
            old = full[pl.ds(to, bs), pl.ds(at, bs)].astype(F32)
            full[pl.ds(to, bs), pl.ds(at, bs)] = jnp.where(lane < HALF, last, old).astype(BF16)
            full[pl.ds(at, HALF), pl.ds(to, bs)] = last.T[:HALF].astype(BF16)
        else:
            low = jnp.where(lane[:HALF] < HALF, last[:HALF], pltpu.roll(last[HALF:], HALF, 1))
            full[pl.ds(pl.multiple_of(to + HALF, HALF), HALF), pl.ds(at, bs)] = low.astype(BF16)
            old = full[pl.ds(at, bs), pl.ds(to, bs)].astype(F32)
            new = jnp.concatenate([low, low], axis=0).T
            full[pl.ds(at, bs), pl.ds(to, bs)] = jnp.where(lane < HALF, old, new).astype(BF16)

        side = last.T[HALF:]
        w, d = side[:RANK], side[RANK : RANK + 1]
        for g in (1, 2):
            w = w + pltpu.roll(side, HALF - g * GROUP, 0)[:RANK]
            d = d + side[g * GROUP + RANK : g * GROUP + RANK + 1]
        diag[:, pl.ds(to, bs)] = jnp.broadcast_to(d, (diag.shape[0], bs))
        q = q_ref[:RANK, pl.ds(to, bs)]
        us = [part.astype(F32) for part in split3(jnp.concatenate([w, q], axis=0))]
        us.append(jnp.zeros((bs - 6 * RANK, bs), F32))
        u[pl.ds(to, bs), :] = jnp.concatenate(us, axis=0).T.astype(BF16)
        v1, v2, v3 = split3(jnp.concatenate([q, w], axis=0))
        v[:, pl.ds(to, bs)] = jnp.concatenate([v1, v2, v3, v1, v2, v1], axis=0)
        return 0

    def every(first_half):
        lax.fori_loop(0, rows // bs, functools.partial(one, first_half), 0, unroll=True)

    if share_refs[1] is None:
        every(True)
        return
    first_half = index_ref[offset] < nb // 2
    pl.when(first_half)(lambda: every(True))
    pl.when(jnp.logical_not(first_half))(lambda: every(False))


def unpack_kernel(items, count, index_ref, *refs):
    shares = iter(refs[:count])
    for offset, given in items:
        pair = [next(shares) if e in given else None for e in (0, 1)]
        unpack(offset, index_ref, pair, refs[count], *refs[-4:])


def iterate_kernel(offset, index_ref, far_0, far_1, q_ref, p0_ref, *refs):
    p_ref, inv_ref, full, u, v, diag = refs[4:]
    k, _ = q_ref.shape
    unpack(offset, index_ref, (far_0, far_1), q_ref, full, u, v, diag)
    lane = lax.broadcasted_iota(jnp.int32, (k, LANES), 1)

    def product(p):
        t = dot(p, u[...], NN)
        t = t + pltpu.roll(t, 4 * RANK, 1)
        t = t + pltpu.roll(t, 2 * RANK, 1)
        h1, h2, h3 = [h.astype(F32) for h in split3(t)]
        ts = jnp.concatenate(
            [jnp.where(lane < 6 * RANK, h1, h2), jnp.where(lane < 2 * RANK, h2, h3)[:, :HALF]], axis=1
        ).astype(BF16)
        y = dot(p, full[...], NN) + dot(ts, v[...], NN) + p.astype(F32) * diag[0:1, :]
        return split3(y)

    def sweep(step, p):
        parts = product(p)
        return apply_lower(inverse_lower(gram_of(parts, p)), parts).astype(BF16)

    p = lax.fori_loop(0, ITERS - 1, sweep, p0_ref[...], unroll=3)
    p_ref[...] = p
    inv_ref[...] = inverse_lower(gram_of(product(p), p))


def finish_kernel(scale, p_ref, inv_ref, block_ref, o_ref):
    back = dot(p_ref[...], block_ref[...], NN)
    o_ref[...] = (apply_lower(inv_ref[...], split3(back)) * scale).astype(BF16)


def flip(x, axes, perm):
    return lax.ppermute(x, axes, perm)


def ordered(own, recv, bit, axis=0):
    return jnp.where(
        bit == 0,
        jnp.concatenate([own, recv], axis=axis),
        jnp.concatenate([recv, own], axis=axis),
    )


def sample_space(stamps, start_panel):
    pix = lax.axis_size("pix")
    samp = lax.axis_size("samp")
    n = stamps.shape[0] * pix * samp
    k = start_panel.shape[1]
    scale = math.sqrt(start_panel.shape[0] * pix)
    p = lax.axis_index("pix")
    s = lax.axis_index("samp")
    xor_pix = lambda b: [(i, i ^ b) for i in range(pix)]
    xor_samp = lambda b: [(i, i ^ b) for i in range(samp)]

    core = p & 1
    x, y = (p >> 1) & 1, (p >> 2) & 1
    z0, z1 = s & 1, (s >> 1) & 1

    low = start_panel.astype(BF16).T
    for b in (2, 4):
        low = jnp.concatenate([low, flip(low, "pix", xor_pix(b))], axis=1)
    far = flip(low, "pix", xor_pix(1))
    bit_a = jnp.where(core == 0, x, y)
    bit_b = jnp.where(core == 0, y, x)
    bs = 2 * stamps.shape[0]
    nb = n // bs
    at = jnp.arange(pix, dtype=jnp.int32)
    place = p ^ (((at & 1) << 1) | ((at & 2) << 1) | (at >> 2))
    at = jnp.arange(nb, dtype=jnp.int32)
    c_of = core ^ ((at >> 3) & 1)
    a_of = jnp.where(c_of == 0, x, y) ^ ((at >> 2) & 1)
    b_of = jnp.where(c_of == 0, y, x) ^ ((at >> 1) & 1)
    order = c_of * 8 + a_of * 4 + b_of * 2 + (z0 ^ (at & 1))
    pairs = [
        (core * 4 + half * 2 + quarter) * (nb // 8)
        for half in (1 - bit_a, bit_a)
        for quarter in (1 - bit_b, bit_b)
    ]
    pairs += [1 - z0, z0, core, 0]
    index = jnp.concatenate([jnp.stack([jnp.int32(i) for i in pairs]), place, order]).astype(jnp.int32)

    block = lax.all_to_all(stamps, ("pix", "samp"), split_axis=1, concat_axis=0, tiled=True)

    proj = kernel_call(
        rows_kernel,
        jax.ShapeDtypeStruct((k, stamps.shape[0]), BF16),
        in_specs=[smem()] + vmem(3),
        out_specs=vmem()[0],
    )(index, low, far, stamps)
    for b in (1, 2, 4):
        proj = ordered(proj, flip(proj, "pix", xor_pix(b)), p & b, axis=1)
    other = flip(proj, "samp", xor_samp(1))
    proj = ordered(proj, other, z0, axis=1)
    proj = ordered(proj, flip(proj, "samp", xor_samp(2)), z1, axis=1)
    proj, q = kernel_call(
        functools.partial(basis_kernel, pix, samp),
        (jax.ShapeDtypeStruct((k, n), BF16), jax.ShapeDtypeStruct((k, n), F32)),
        in_specs=vmem(),
        out_specs=tuple(vmem(2)),
    )(proj)

    first = [(i, i ^ (2 if i % 2 == 0 else 4)) for i in range(pix)]
    second = [(i, i ^ (4 if i % 2 == 0 else 2)) for i in range(pix)]
    other = flip(block, "pix", xor_pix(1))
    px = block.shape[1]
    width = n // 2 + bs
    rows = n // 8
    window = rows - bs + width
    cut = (nb // 4 + 1) * bs
    pieces = tuple(jax.ShapeDtypeStruct((rows, c), BF16) for c in (cut, width - cut))
    stack = jax.ShapeDtypeStruct((12 * RANK, n), BF16)
    left, right = kernel_call(
        factors_kernel,
        (stack, stack),
        in_specs=vmem(3),
        out_specs=tuple(vmem(2)),
        scratch_mib=12,
    )(block, other, q)

    def form(quarter):
        return kernel_call(
            functools.partial(form_kernel, QUARTERS + quarter),
            pieces,
            in_specs=[smem()] + vmem(4),
            out_specs=tuple(vmem(2)),
            scratch_mib=12,
            scratch_shapes=[pltpu.VMEM((window, 2 * px), BF16), pltpu.VMEM((12 * RANK, window), BF16)],
        )(index, block, other, left, right)

    sent = [form(0), form(1)]
    held = [form(2)]
    held.append(form(3))
    swap = xor_pix(1)
    near, far, over_a, far_a, over_ab, far_ab = ([None, None] for _ in range(6))
    for e in (0, 1):
        add = functools.partial(add_shares, index, e == 1)
        passed, kept = [flip(sent[i][e], "pix", first) for i in (0, 1)]
        (send,) = add((held[0][e], passed))
        recv = flip(send, "pix", second)
        send, keep = add((held[1][e], kept, recv), (HALVES, HALVES + 1))
        recv = flip(send, "samp", xor_samp(1))
        (share,) = add((keep, recv))
        recv = flip(share, "samp", xor_samp(2))
        (share,) = add((share, recv))

        recv = flip(share, "samp", xor_samp(1))
        share = jnp.concatenate([share, recv], axis=0)
        over_a[e] = flip(share, "pix", first)
        over_b = flip(share, "pix", second)
        over_ab[e] = flip(over_b, "pix", first)
        near[e] = jnp.concatenate([share, over_b], axis=0)
        far[e] = flip(near[e], "pix", swap)
        far_a[e], far_ab[e] = [flip(t[e], "pix", swap) for t in (over_a, over_ab)]
    parts = (
        jax.ShapeDtypeStruct((n, n), BF16),
        jax.ShapeDtypeStruct((n, bs), BF16),
        jax.ShapeDtypeStruct((12 * RANK, n), BF16),
        jax.ShapeDtypeStruct((8, n), F32),
    )
    eighth = nb // 8

    def unpack_into(now, slots, given, *shares):
        count = len(shares)
        items = [(BLOCKS + i * eighth, given) for i in slots]
        aliases = {count + 2 + i: i for i in range(len(now))}
        return kernel_call(
            functools.partial(unpack_kernel, items, count),
            parts,
            in_specs=[smem()] + vmem(count + 1 + len(now)),
            out_specs=tuple(vmem(4)),
            input_output_aliases=aliases,
            scratch_mib=4,
        )(index, *shares, q, *now)

    now = unpack_into((), (0, 4), (0,), near[0], far[0])
    now = unpack_into(now, (2, 6), (0,), over_a[0], far_a[0])
    now = unpack_into(now, (0, 4), (1,), near[1], far[1])
    now = unpack_into(now, (2, 6), (1,), over_a[1], far_a[1])
    now = unpack_into(now, (3,), (0, 1), *over_ab)
    proj, inv = kernel_call(
        functools.partial(iterate_kernel, BLOCKS + 7 * eighth),
        (jax.ShapeDtypeStruct((k, n), BF16), jax.ShapeDtypeStruct((k, LANES), F32)) + parts,
        in_specs=[smem()] + vmem(8),
        out_specs=tuple(vmem(6)),
        input_output_aliases={5 + i: 2 + i for i in range(4)},
        scratch_mib=12,
    )(index, *far_ab, q, proj, *now)[:2]

    mine = kernel_call(
        functools.partial(finish_kernel, scale),
        jax.ShapeDtypeStruct((k, px), BF16),
        in_specs=vmem(3),
        out_specs=vmem()[0],
    )(proj, inv, block)
    for b in (2, 1):
        mine = jnp.concatenate([mine, flip(mine, "samp", xor_samp(b))], axis=1)
    parts = [mine[:, i * px : (i + 1) * px] for i in range(samp)]
    by_distance = {0: parts[0], 2: parts[1], 1: parts[2], 3: parts[3]}
    swap0 = [jnp.where(z0 == 0, by_distance[i], by_distance[i ^ 1]) for i in range(samp)]
    swap1 = [jnp.where(z1 == 0, swap0[i], swap0[i ^ 2]) for i in range(samp)]
    return jnp.concatenate(swap1, axis=1).astype(F32).T


def solution(mesh):
    pix, samp = mesh.shape["pix"], mesh.shape["samp"]

    def local(stamps, start_panel):
        n = stamps.shape[0] * pix * samp
        k = start_panel.shape[1]
        if n <= SAMPLE_SPACE_LIMIT and (pix, samp) == (8, 4) and 4 * k == 2 * stamps.shape[0] == LANES:
            return sample_space(stamps, start_panel)
        return pixel_space(stamps, start_panel)

    return jax.shard_map(
        local,
        mesh=mesh,
        in_specs=(P(("samp", "pix"), None), P("pix", None)),
        out_specs=P("pix", None),
        check_vma=False,
    )
```

```python
import functools
import math

import jax
import jax.numpy as jnp
from jax import lax
from jax.experimental import pallas as pl
from jax.experimental.pallas import tpu as pltpu
from jax.sharding import PartitionSpec as P


ITERS = 10
LANES = 128
PANEL = 16
RANK = 16
GROUP = 20
HALF = 64
STEP = 2
QUARTERS, HALVES, CORE, PLACE, BLOCKS = 0, 4, 6, 8, 16
SAMPLE_SPACE_LIMIT = 4096
F32 = jnp.float32
BF16 = jnp.bfloat16

NN = (((1,), (0,)), ((), ()))
NT = (((1,), (1,)), ((), ()))
TN = (((0,), (0,)), ((), ()))


def orthonormal(back, gram):
    lower = jnp.linalg.cholesky(gram)
    return lax.linalg.triangular_solve(lower, back, left_side=False, lower=True, transpose_a=True)


def pixel_space(stamps, start_panel):
    block = lax.all_to_all(stamps, "pix", split_axis=1, concat_axis=0, tiled=True)

    def sweep(step, panel):
        partial_value = jnp.dot(block, panel.astype(BF16), preferred_element_type=F32)
        proj = lax.psum(partial_value.astype(BF16), "pix")
        back = lax.dot_general(block, proj, TN, preferred_element_type=F32)
        summed = lax.psum(back.astype(BF16), "samp").astype(F32)
        gram = lax.psum(jnp.dot(summed.T, summed, precision=lax.Precision.HIGHEST), "pix")
        return orthonormal(summed, gram)

    panel = lax.fori_loop(0, ITERS, sweep, start_panel)
    return panel * math.sqrt(start_panel.shape[0] * lax.axis_size("pix"))


def dot(a, b, dims):
    return lax.dot_general(a, b, dims, preferred_element_type=F32)


def split3(x):
    hi = x.astype(BF16)
    rest = x - hi.astype(F32)
    mid = rest.astype(BF16)
    lo = (rest - mid.astype(F32)).astype(BF16)
    return hi, mid, lo


def kernel_call(body, out_shape, in_specs=(), scratch_mib=8, **kw):
    single = not isinstance(out_shape, tuple)
    outs = tuple(pltpu.VMEM(o.shape, o.dtype) for o in ((out_shape,) if single else out_shape))
    call = pl.pallas_call(
        body,
        out_shape=outs[0] if single else outs,
        in_specs=in_specs,
        compiler_params=pltpu.CompilerParams(vmem_limit_bytes=scratch_mib << 20),
        **kw,
    )

    def place(x, spec):
        if spec.memory_space != pltpu.VMEM:
            return x
        return pltpu.with_memory_space_constraint(x, pltpu.VMEM)

    return lambda *args: call(*map(place, args, in_specs))


def vmem(n=1):
    return [pl.BlockSpec(memory_space=pltpu.VMEM)] * n


def smem():
    return pl.BlockSpec(memory_space=pltpu.SMEM)


def inverse_lower(gram):
    k = gram.shape[0]
    lane = lax.broadcasted_iota(jnp.int32, gram.shape, 1)
    row = lax.broadcasted_iota(jnp.int32, gram.shape, 0)
    m = jnp.where(lane < k, gram, jnp.where(lane % k == row, 1.0, 0.0))
    pivots = jnp.ones(gram.shape, F32)
    for start in range(0, k, PANEL):
        cols = [jnp.broadcast_to(m[:, j : j + 1], m.shape) for j in range(start, start + PANEL)]
        for t in range(PANEL):
            j = start + t
            pivot = cols[t][j : j + 1, :]
            factor = jnp.where(row > j, cols[t] * (1.0 / pivot), 0.0)
            pivots = jnp.where(row == j, pivot, pivots)
            for later in range(t + 1, PANEL):
                cols[later] = cols[later] - factor * cols[later][j : j + 1, :]
            m = m - factor * m[j : j + 1, :]
    return m * lax.rsqrt(pivots)


def lane_sum3(x, k):
    return x + pltpu.roll(x, LANES - k, 1) + pltpu.roll(x, LANES - 2 * k, 1)


def gram_of(parts, right):
    k = right.shape[0]
    g = dot(jnp.concatenate(parts, axis=0), right, NT)
    g = g[:k] + g[k : 2 * k] + g[2 * k :]
    return jnp.concatenate([g, jnp.zeros((k, 3 * k), F32)], axis=1)


def apply_lower(inv, parts):
    k = inv.shape[0]
    lane = lax.broadcasted_iota(jnp.int32, inv.shape, 1)
    h1, h2, h3 = [h.astype(F32) for h in split3(inv)]
    first = jnp.where(lane < k, 0.0, h1)
    second = jnp.where(lane < k, 0.0, jnp.where(lane < 3 * k, h2, h3))
    left = jnp.concatenate([first, second], axis=1).astype(BF16)
    y1, y2, y3 = parts
    zeros = jnp.zeros_like(y1)
    return dot(left, jnp.concatenate([zeros, y1, y2, y3, zeros, y1, y2, y1], axis=0), NN)


def rows_kernel(index_ref, near_ref, far_ref, stamps_ref, o_ref):
    total = jnp.zeros(o_ref.shape, F32)
    pix = BLOCKS - PLACE
    m = near_ref.shape[1] * 2 // pix
    for j in range(pix):
        ref = near_ref if j * m < near_ref.shape[1] else far_ref
        at = j * m % near_ref.shape[1]
        stamps = stamps_ref[:, pl.ds(pl.multiple_of(index_ref[PLACE + j] * m, LANES), m)]
        total += dot(ref[:, at : at + m], stamps, NT)
    o_ref[...] = total.astype(BF16)


def basis_kernel(pix, samp, p0_ref, p_ref, q_ref):
    k, n = p0_ref.shape
    m = n // (pix * samp)
    per = LANES // m
    lane = lax.broadcasted_iota(jnp.int32, (k, LANES), 1)
    for to in range(n // LANES):
        block = jnp.zeros((k, LANES), F32)
        for j in range(per):
            p, s = divmod(to * per + j, samp)
            group, slot = divmod(s * pix + p, per)
            part = p0_ref[:, group * LANES : (group + 1) * LANES].astype(F32)
            part = pltpu.roll(part, (j - slot) * m % LANES, 1) if j != slot else part
            block = jnp.where(lane // m == j, part, block)
        p_ref[:, to * LANES : (to + 1) * LANES] = block.astype(BF16)
    p0 = p_ref[...]
    parts = (p0, jnp.zeros_like(p0), jnp.zeros_like(p0))
    q = apply_lower(inverse_lower(gram_of(parts, p0)), parts)
    q_ref[...] = jnp.where(lax.broadcasted_iota(jnp.int32, q.shape, 0) < RANK, q, 0.0)


def factors_kernel(own_ref, other_ref, q_ref, left, right):
    k = q_ref.shape[0]
    q = q_ref[...]
    zeros = jnp.zeros(q.shape, BF16)
    q1, q2, q3 = split3(q)
    qs = jnp.concatenate([q1, q2, q3], axis=0)
    w = jnp.zeros(q.shape, F32)
    for ref in (own_ref, other_ref):
        t3 = dot(qs, ref[...], NN)
        ts = split3(t3[:k] + t3[k : 2 * k] + t3[2 * k :])
        w3 = dot(jnp.concatenate(ts, axis=0), ref[...], NT)
        w += w3[:k] + w3[k : 2 * k] + w3[2 * k :]
    ws = jnp.concatenate(list(split3(w)) + [zeros], axis=0)
    m = lane_sum3(dot(q1, ws, NT) + dot(q2, ws, NT) + dot(q3, ws, NT), k)
    m = jnp.where(lax.broadcasted_iota(jnp.int32, m.shape, 1) < k, m, 0.0)
    m = pltpu.roll(m, k, 1) + pltpu.roll(m, 2 * k, 1) + pltpu.roll(m, 3 * k, 1)
    w1, w2, w3 = split3(w - 0.5 * apply_lower(m, (q1, q2, q3)))
    q1, q2, q3, w1, w2, w3 = [part[:RANK] for part in (q1, q2, q3, w1, w2, w3)]
    left[...] = jnp.concatenate([q1, w1, q1, w1, q1, w1, q2, w2, q2, w2, q3, w3], axis=0)
    right[...] = jnp.concatenate([w1, q1, w2, q2, w3, q3, w1, q1, w2, q2, w1, q1], axis=0)


def form_rows(first, core, own_ref, other_ref, left, right, out_refs, window, right_win):
    n, px = own_ref.shape
    rows, cut = out_refs[0].shape
    width = n // 2
    bs = cut + out_refs[1].shape[1] - width
    nb = n // bs
    for b in range(window.shape[0] // bs):
        at = pl.multiple_of(lax.rem(first + b, nb) * bs, bs)
        window[b * bs : (b + 1) * bs, :px] = own_ref[pl.ds(at, bs), :]
        window[b * bs : (b + 1) * bs, px:] = other_ref[pl.ds(at, bs), :]
        right_win[:, b * bs : (b + 1) * bs] = right[:, pl.ds(at, bs)]
    lane = lax.broadcasted_iota(jnp.int32, (bs, bs), 1)
    eye = lax.broadcasted_iota(jnp.int32, (bs, bs), 0) == lane
    step = STEP * bs
    for i in range(rows // bs):
        if i % STEP == 0:
            at = pl.multiple_of((first + i) * bs, bs)
            lo, end = i * bs, i * bs + step + width
            wide = dot(window[lo : lo + step, :], window[lo:end, :], NT)
            wide -= dot(left[:, pl.ds(at, step)], right_win[:, lo:end], TN)
        off = i % STEP * bs
        to = i * bs
        s = wide[off : off + bs, off : off + width + bs]
        corner = s[:, :bs]
        diagonal = jnp.sum(jnp.where(eye, corner, 0.0), axis=0, keepdims=True)
        out_refs[0][to : to + bs, :bs] = jnp.where(eye, 0.0, corner).astype(BF16)
        out_refs[0][to : to + bs, bs:] = s[:, bs:cut].astype(BF16)
        out_refs[1][to : to + bs, : width - cut] = s[:, cut:width].astype(BF16)
        last = s[:, width:]
        low = last[HALF:]
        last = jnp.where(core == 0, last, jnp.concatenate([low, pltpu.roll(low, HALF, 1)], axis=0))
        side = [jnp.zeros((HALF, bs), F32)]
        for g, d in enumerate(split3(diagonal)):
            w = right_win[2 * g * RANK : (2 * g + 1) * RANK, to : to + bs]
            side.append(w.astype(F32))
            side.append(jnp.broadcast_to(d.astype(F32), (GROUP - RANK, bs)))
        side.append(jnp.zeros((bs - HALF - 3 * GROUP, bs), F32))
        side = jnp.concatenate(side, axis=0).T
        last = jnp.where(lane < HALF, last, side)
        out_refs[1][to : to + bs, width - cut :] = last.astype(BF16)


def form_kernel(slot, at_ref, own_ref, other_ref, left, right, out_0, out_1, *wins):
    outs = (out_0, out_1)
    form_rows(at_ref[slot], at_ref[CORE], own_ref, other_ref, left, right, outs, *wins)


def add_kernel(slots, special, at_ref, *refs):
    shares, o_refs = refs[: -len(slots)], refs[-len(slots) :]
    width = shares[0].shape[1] - (LANES if special else 0)
    for slot, o_ref in zip(slots, o_refs):
        h = o_ref.shape[0]
        at = 0 if slot is None else pl.multiple_of(at_ref[slot] * h, h)
        parts = [ref[pl.ds(at, h), :].astype(F32) for ref in shares]
        o_ref[:, :width] = sum(part[:, :width] for part in parts).astype(BF16)
        if not special:
            continue
        last = [part[:, width:] for part in parts]
        x = sum(lane_sum3(part, GROUP) for part in last)
        lane = lax.broadcasted_iota(jnp.int32, x.shape, 1) - HALF
        h1, h2, h3 = [part.astype(F32) for part in split3(x)]
        packed = jnp.where(lane < 2 * GROUP, pltpu.roll(h2, GROUP, 1), pltpu.roll(h3, 2 * GROUP, 1))
        packed = jnp.where(lane < GROUP, h1, packed)
        packed = jnp.where(lane < 3 * GROUP, packed, 0.0)
        o_ref[:, width:] = jnp.where(lane < 0, sum(last), packed).astype(BF16)


def add_shares(index, special, shares, slots=()):
    rows, lanes = shares[0].shape
    shape = jax.ShapeDtypeStruct((rows // max(len(slots), 1), lanes), BF16)
    slots = slots or (None,)
    return kernel_call(
        functools.partial(add_kernel, slots, special),
        (shape,) * len(slots),
        in_specs=[smem()] + vmem(len(shares)),
        out_specs=tuple(vmem(len(slots))),
    )(index, *shares)


def unpack(offset, index_ref, share_refs, q_ref, full, u, v, diag):
    n = q_ref.shape[1]
    width = n // 2
    bs = LANES
    nb = n // bs
    cut = (nb // 4 + 1) * bs
    rows = [ref.shape[0] for ref in share_refs if ref is not None][0]
    lane = lax.broadcasted_iota(jnp.int32, (bs, bs), 1)

    def one(first_half, r, _):
        i = index_ref[r + offset]
        frm = pl.multiple_of(r * bs, bs)
        to = pl.multiple_of(i * bs, bs)
        for d in range(nb // 2):
            ref, col = (share_refs[0], d * bs) if d * bs < cut else (share_refs[1], d * bs - cut)
            if ref is None:
                continue
            part = ref[pl.ds(frm, bs), col : col + bs]
            at = pl.multiple_of(lax.rem(i + d, nb) * bs, bs)
            full[pl.ds(to, bs), pl.ds(at, bs)] = part
            if d:
                full[pl.ds(at, bs), pl.ds(to, bs)] = part.T
        if share_refs[1] is None:
            return 0
        at = pl.multiple_of(lax.rem(i + nb // 2, nb) * bs, bs)
        last = share_refs[1][pl.ds(frm, bs), width - cut :].astype(F32)

        if first_half:
            old = full[pl.ds(to, bs), pl.ds(at, bs)].astype(F32)
            full[pl.ds(to, bs), pl.ds(at, bs)] = jnp.where(lane < HALF, last, old).astype(BF16)
            full[pl.ds(at, HALF), pl.ds(to, bs)] = last.T[:HALF].astype(BF16)
        else:
            low = jnp.where(lane[:HALF] < HALF, last[:HALF], pltpu.roll(last[HALF:], HALF, 1))
            full[pl.ds(pl.multiple_of(to + HALF, HALF), HALF), pl.ds(at, bs)] = low.astype(BF16)
            old = full[pl.ds(at, bs), pl.ds(to, bs)].astype(F32)
            new = jnp.concatenate([low, low], axis=0).T
            full[pl.ds(at, bs), pl.ds(to, bs)] = jnp.where(lane < HALF, old, new).astype(BF16)

        side = last.T[HALF:]
        w, d = side[:RANK], side[RANK : RANK + 1]
        for g in (1, 2):
            w = w + pltpu.roll(side, HALF - g * GROUP, 0)[:RANK]
            d = d + side[g * GROUP + RANK : g * GROUP + RANK + 1]
        diag[:, pl.ds(to, bs)] = jnp.broadcast_to(d, (diag.shape[0], bs))
        q = q_ref[:RANK, pl.ds(to, bs)]
        us = [part.astype(F32) for part in split3(jnp.concatenate([w, q], axis=0))]
        us.append(jnp.zeros((bs - 6 * RANK, bs), F32))
        u[pl.ds(to, bs), :] = jnp.concatenate(us, axis=0).T.astype(BF16)
        v1, v2, v3 = split3(jnp.concatenate([q, w], axis=0))
        v[:, pl.ds(to, bs)] = jnp.concatenate([v1, v2, v3, v1, v2, v1], axis=0)
        return 0

    def every(first_half):
        lax.fori_loop(0, rows // bs, functools.partial(one, first_half), 0, unroll=True)

    if share_refs[1] is None:
        every(True)
        return
    first_half = index_ref[offset] < nb // 2
    pl.when(first_half)(lambda: every(True))
    pl.when(jnp.logical_not(first_half))(lambda: every(False))


def unpack_kernel(items, count, index_ref, *refs):
    shares = iter(refs[:count])
    for offset, given in items:
        pair = [next(shares) if e in given else None for e in (0, 1)]
        unpack(offset, index_ref, pair, refs[count], *refs[-4:])


def iterate_kernel(offset, index_ref, far_0, far_1, q_ref, p0_ref, *refs):
    p_ref, inv_ref, full, u, v, diag = refs[4:]
    k, _ = q_ref.shape
    unpack(offset, index_ref, (far_0, far_1), q_ref, full, u, v, diag)
    lane = lax.broadcasted_iota(jnp.int32, (k, LANES), 1)

    def product(p):
        t = dot(p, u[...], NN)
        t = t + pltpu.roll(t, 4 * RANK, 1)
        t = t + pltpu.roll(t, 2 * RANK, 1)
        h1, h2, h3 = [h.astype(F32) for h in split3(t)]
        ts = jnp.concatenate(
            [jnp.where(lane < 6 * RANK, h1, h2), jnp.where(lane < 2 * RANK, h2, h3)[:, :HALF]], axis=1
        ).astype(BF16)
        y = dot(p, full[...], NN) + dot(ts, v[...], NN) + p.astype(F32) * diag[0:1, :]
        return split3(y)

    def sweep(step, p):
        parts = product(p)
        return apply_lower(inverse_lower(gram_of(parts, p)), parts).astype(BF16)

    p = lax.fori_loop(0, ITERS - 1, sweep, p0_ref[...], unroll=3)
    p_ref[...] = p
    inv_ref[...] = inverse_lower(gram_of(product(p), p))


def finish_kernel(scale, p_ref, inv_ref, block_ref, o_ref):
    back = dot(p_ref[...], block_ref[...], NN)
    o_ref[...] = (apply_lower(inv_ref[...], split3(back)) * scale).astype(BF16)


def flip(x, axes, perm):
    return lax.ppermute(x, axes, perm)


def ordered(own, recv, bit, axis=0):
    return jnp.where(
        bit == 0,
        jnp.concatenate([own, recv], axis=axis),
        jnp.concatenate([recv, own], axis=axis),
    )


def sample_space(stamps, start_panel):
    pix = lax.axis_size("pix")
    samp = lax.axis_size("samp")
    n = stamps.shape[0] * pix * samp
    k = start_panel.shape[1]
    scale = math.sqrt(start_panel.shape[0] * pix)
    p = lax.axis_index("pix")
    s = lax.axis_index("samp")
    xor_pix = lambda b: [(i, i ^ b) for i in range(pix)]
    xor_samp = lambda b: [(i, i ^ b) for i in range(samp)]

    core = p & 1
    x, y = (p >> 1) & 1, (p >> 2) & 1
    z0, z1 = s & 1, (s >> 1) & 1

    low = start_panel.astype(BF16).T
    for b in (2, 4):
        low = jnp.concatenate([low, flip(low, "pix", xor_pix(b))], axis=1)
    far = flip(low, "pix", xor_pix(1))
    bit_a = jnp.where(core == 0, x, y)
    bit_b = jnp.where(core == 0, y, x)
    bs = 2 * stamps.shape[0]
    nb = n // bs
    at = jnp.arange(pix, dtype=jnp.int32)
    place = p ^ (((at & 1) << 1) | ((at & 2) << 1) | (at >> 2))
    at = jnp.arange(nb, dtype=jnp.int32)
    c_of = core ^ ((at >> 3) & 1)
    a_of = jnp.where(c_of == 0, x, y) ^ ((at >> 2) & 1)
    b_of = jnp.where(c_of == 0, y, x) ^ ((at >> 1) & 1)
    order = c_of * 8 + a_of * 4 + b_of * 2 + (z0 ^ (at & 1))
    pairs = [
        (core * 4 + half * 2 + quarter) * (nb // 8)
        for half in (1 - bit_a, bit_a)
        for quarter in (1 - bit_b, bit_b)
    ]
    pairs += [1 - z0, z0, core, 0]
    index = jnp.concatenate([jnp.stack([jnp.int32(i) for i in pairs]), place, order]).astype(jnp.int32)

    block = lax.all_to_all(stamps, ("pix", "samp"), split_axis=1, concat_axis=0, tiled=True)

    proj = kernel_call(
        rows_kernel,
        jax.ShapeDtypeStruct((k, stamps.shape[0]), BF16),
        in_specs=[smem()] + vmem(3),
        out_specs=vmem()[0],
    )(index, low, far, stamps)
    for b in (1, 2, 4):
        proj = ordered(proj, flip(proj, "pix", xor_pix(b)), p & b, axis=1)
    other = flip(proj, "samp", xor_samp(1))
    proj = ordered(proj, other, z0, axis=1)
    proj = ordered(proj, flip(proj, "samp", xor_samp(2)), z1, axis=1)
    proj, q = kernel_call(
        functools.partial(basis_kernel, pix, samp),
        (jax.ShapeDtypeStruct((k, n), BF16), jax.ShapeDtypeStruct((k, n), F32)),
        in_specs=vmem(),
        out_specs=tuple(vmem(2)),
    )(proj)

    first = [(i, i ^ (2 if i % 2 == 0 else 4)) for i in range(pix)]
    second = [(i, i ^ (4 if i % 2 == 0 else 2)) for i in range(pix)]
    other = flip(block, "pix", xor_pix(1))
    px = block.shape[1]
    width = n // 2 + bs
    rows = n // 8
    window = rows - bs + width
    cut = (nb // 4 + 1) * bs
    pieces = tuple(jax.ShapeDtypeStruct((rows, c), BF16) for c in (cut, width - cut))
    stack = jax.ShapeDtypeStruct((12 * RANK, n), BF16)
    left, right = kernel_call(
        factors_kernel,
        (stack, stack),
        in_specs=vmem(3),
        out_specs=tuple(vmem(2)),
        scratch_mib=12,
    )(block, other, q)

    def form(quarter):
        return kernel_call(
            functools.partial(form_kernel, QUARTERS + quarter),
            pieces,
            in_specs=[smem()] + vmem(4),
            out_specs=tuple(vmem(2)),
            scratch_mib=12,
            scratch_shapes=[pltpu.VMEM((window, 2 * px), BF16), pltpu.VMEM((12 * RANK, window), BF16)],
        )(index, block, other, left, right)

    sent = [form(0), form(1)]
    held = [form(2)]
    held.append(form(3))
    swap = xor_pix(1)
    near, far, over_a, far_a, over_ab, far_ab = ([None, None] for _ in range(6))
    for e in (0, 1):
        add = functools.partial(add_shares, index, e == 1)
        passed, kept = [flip(sent[i][e], "pix", first) for i in (0, 1)]
        (send,) = add((held[0][e], passed))
        recv = flip(send, "pix", second)
        send, keep = add((held[1][e], kept, recv), (HALVES, HALVES + 1))
        recv = flip(send, "samp", xor_samp(1))
        (share,) = add((keep, recv))
        recv = flip(share, "samp", xor_samp(2))
        (share,) = add((share, recv))

        recv = flip(share, "samp", xor_samp(1))
        share = jnp.concatenate([share, recv], axis=0)
        over_a[e] = flip(share, "pix", first)
        over_b = flip(share, "pix", second)
        over_ab[e] = flip(over_b, "pix", first)
        near[e] = jnp.concatenate([share, over_b], axis=0)
        far[e] = flip(near[e], "pix", swap)
        far_a[e], far_ab[e] = [flip(t[e], "pix", swap) for t in (over_a, over_ab)]
    parts = (
        jax.ShapeDtypeStruct((n, n), BF16),
        jax.ShapeDtypeStruct((n, bs), BF16),
        jax.ShapeDtypeStruct((12 * RANK, n), BF16),
        jax.ShapeDtypeStruct((8, n), F32),
    )
    eighth = nb // 8

    def unpack_into(now, slots, given, *shares):
        count = len(shares)
        items = [(BLOCKS + i * eighth, given) for i in slots]
        aliases = {count + 2 + i: i for i in range(len(now))}
        return kernel_call(
            functools.partial(unpack_kernel, items, count),
            parts,
            in_specs=[smem()] + vmem(count + 1 + len(now)),
            out_specs=tuple(vmem(4)),
            input_output_aliases=aliases,
            scratch_mib=4,
        )(index, *shares, q, *now)

    now = unpack_into((), (0, 4), (0,), near[0], far[0])
    now = unpack_into(now, (2, 6), (0,), over_a[0], far_a[0])
    now = unpack_into(now, (0, 4), (1,), near[1], far[1])
    now = unpack_into(now, (2, 6), (1,), over_a[1], far_a[1])
    now = unpack_into(now, (3,), (0, 1), *over_ab)
    proj, inv = kernel_call(
        functools.partial(iterate_kernel, BLOCKS + 7 * eighth),
        (jax.ShapeDtypeStruct((k, n), BF16), jax.ShapeDtypeStruct((k, LANES), F32)) + parts,
        in_specs=[smem()] + vmem(8),
        out_specs=tuple(vmem(6)),
        input_output_aliases={5 + i: 2 + i for i in range(4)},
        scratch_mib=12,
    )(index, *far_ab, q, proj, *now)[:2]

    mine = kernel_call(
        functools.partial(finish_kernel, scale),
        jax.ShapeDtypeStruct((k, px), BF16),
        in_specs=vmem(3),
        out_specs=vmem()[0],
    )(proj, inv, block)
    for b in (2, 1):
        mine = jnp.concatenate([mine, flip(mine, "samp", xor_samp(b))], axis=1)
    parts = [mine[:, i * px : (i + 1) * px] for i in range(samp)]
    by_distance = {0: parts[0], 2: parts[1], 1: parts[2], 3: parts[3]}
    swap0 = [jnp.where(z0 == 0, by_distance[i], by_distance[i ^ 1]) for i in range(samp)]
    swap1 = [jnp.where(z1 == 0, swap0[i], swap0[i ^ 2]) for i in range(samp)]
    return jnp.concatenate(swap1, axis=1).astype(F32).T


def solution(mesh):
    pix, samp = mesh.shape["pix"], mesh.shape["samp"]

    def local(stamps, start_panel):
        n = stamps.shape[0] * pix * samp
        k = start_panel.shape[1]
        if n <= SAMPLE_SPACE_LIMIT and (pix, samp) == (8, 4) and 4 * k == 2 * stamps.shape[0] == LANES:
            return sample_space(stamps, start_panel)
        return pixel_space(stamps, start_panel)

    return jax.shard_map(
        local,
        mesh=mesh,
        in_specs=(P(("samp", "pix"), None), P("pix", None)),
        out_specs=P("pix", None),
        check_vma=False,
    )
```
